32 devices in a mesh: rep: 2 (over y), cell: 4 (over z), sub: 4 (over x, core).
Axes of the slice: x: 2, y: 2, z: 4, core: 2. Of those that a mesh axis runs over, the one named last changes fastest.
Arguments:
- descriptors: bfloat16 [8, 4, 128, 128], P(('rep', 'cell'), 'sub'), parts along dimension 0, may hold values from -6 to 6
- positions: float32 [3, 8, 4, 128], P(None, ('rep', 'cell'), 'sub'), parts along dimension 1, may hold values from 0 to 4, as said below
- species: int32 [8, 4, 128], P(('rep', 'cell'), 'sub'), parts along dimension 0, may hold values from 0 to 3
- counts: int32 [8, 4], P(('rep', 'cell'), 'sub'), parts along dimension 0, may hold values from 80 to 128, as said below
- w_in: bfloat16 [8, 128, 256], replicated, may hold values from -0.5 to 0.5
- b_in: float32 [8, 256], replicated, may hold values from -3 to 3
- w_hid: bfloat16 [8, 256, 256], replicated, may hold values from -0.375 to 0.375
- b_hid: float32 [8, 256], replicated, may hold values from -3 to 3
- w_out: bfloat16 [8, 2, 256], replicated, may hold values from -0.375 to 0.375
Outputs:
- charges: float32 [8, 8, 4, 128], P(None, ('rep', 'cell'), 'sub'), parts along dimension 1
The draws below stay inside these ranges and needn't reach their ends.
There are 2 independent parts, one for each index of `rep`. The reference program is written for one: setup_inputs(seed, part) draws one part's arguments, and reference() takes and returns one part's arrays. A program takes and returns all parts, laid end to end along the dimension named above; an argument that names none is the same for every part. Nothing has to cross between parts.
Inputs may be any that keep to these rules, and one draw needn't show every extreme that they name: `positions`: the first two coordinates of a slot lie between its cell's indices and one more, the height between 0 and 1. `counts`: a cell's slots from its count up are empty.
All inputs are finite; a program needn't handle non-finite values.
Results may differ from the reference program's by a relative error of at most 0.0003.
The reference program's roundings to bfloat16 on the way (of `first` and `second`) count: a program that leaves them out, or rounds other values in their place, can miss the bound.
Values sent between devices are 32-bit elements; how exact they have to be, the bound alone decides.
No kernel may reach another device: no remote copies, remote signals or barrier semaphores. Data moves between devices by JAX's collectives and lax.ppermute only.
A program may use at most 64 MiB of HBM per device.

```python
import jax
import jax.numpy as jnp
from jax import lax

G = 128
H = 256
MEMBERS = 8
SLOT = 128
ITERS = 2
GA = 4
GB = 4


def draw_positions(key, part):
    fraction = jax.random.uniform(key, (3, GA, GB, SLOT), jnp.float32)
    row_grid = lax.broadcasted_iota(jnp.float32, (GA, GB, SLOT), 0)
    col_grid = lax.broadcasted_iota(jnp.float32, (GA, GB, SLOT), 1)
    return jnp.stack([row_grid + fraction[0], col_grid + fraction[1], fraction[2]])


def draw_counts(key, part):
    drawn = jax.random.randint(key, (GA, GB), SLOT * 5 // 8, SLOT + 1, dtype=jnp.int32)
    drawn = drawn.at[0, 0].set(SLOT)
    return drawn.at[GA - 1, GB - 1].set(SLOT * 5 // 8)


def with_ends(values, key, low, high):
    longest = values.shape.index(max(values.shape))
    spots = []
    for shift in (0, 1):
        where = [jax.random.randint(jax.random.fold_in(key, axis), (), 0, length) for axis, length in enumerate(values.shape)]
        where[longest] = (where[longest] + shift) % values.shape[longest]
        spots.append(tuple(where))
    return values.at[spots[0]].set(low).at[spots[1]].set(high)


def steps_of(own_key, extent, split, smallest, top_value):
    loudness, own = 1.0, jax.random.fold_in(own_key, 6)
    for position, shards_of in split:
        heights = jnp.exp(jax.random.uniform(jax.random.fold_in(own, position), (shards_of,), jnp.float32, smallest / len(split), top_value / len(split)))
        loudness = loudness * jnp.repeat(heights, extent[position] // shards_of).reshape([-1 if axis == position else 1 for axis in range(len(extent))])
    return loudness


def gaussian(rng, dims, scale, bound, cuts=(), kind=jnp.bfloat16):
    values = jax.random.normal(rng, dims, jnp.float32) * scale
    if len(cuts) > 0:
        values = steps_of(rng, dims, cuts, -0.22, 0.18) * values
    return jnp.clip(values, min=-bound, max=bound).astype(kind)


def setup_inputs(seed: int = 0, part: int = 0) -> dict:
    key_list = jax.random.split(jax.random.key(seed), 10)
    part_splits = jax.random.split(jax.random.fold_in(key_list[9], part), 10)
    descriptors = gaussian(part_splits[0], (GA, GB, SLOT, G), 1.0, 6.0, ((0, 4), (1, 4)))
    positions = draw_positions(jax.random.fold_in(jax.random.fold_in(key_list[9], part), 71), part)
    species = with_ends(jax.random.randint(part_splits[2], (GA, GB, SLOT), 0, 4), jax.random.fold_in(part_splits[2], 1), 0, 3).astype(jnp.int32)
    counts = draw_counts(jax.random.fold_in(jax.random.fold_in(key_list[9], part), 71), part)
    w_in = gaussian(key_list[4], (MEMBERS, G, H), G ** -0.5, 0.5)
    b_in = gaussian(key_list[5], (MEMBERS, H), 0.5, 3.0, (), jnp.float32)
    w_hid = gaussian(key_list[6], (MEMBERS, H, H), H ** -0.5, 0.375)
    b_hid = gaussian(key_list[7], (MEMBERS, H), 0.5, 3.0, (), jnp.float32)
    w_out = gaussian(key_list[8], (MEMBERS, 2, H), H ** -0.5, 0.375)
    return dict(descriptors=descriptors, positions=positions, species=species, counts=counts, w_in=w_in, b_in=b_in, w_hid=w_hid, b_hid=b_hid, w_out=w_out)


def lookup(species, entries):
    choices_table = jnp.array(entries, jnp.float32)
    kinds = jnp.arange(4, dtype=jnp.int32)
    return lax.optimization_barrier(jnp.sum((species[..., None] == kinds).astype(jnp.float32) * choices_table, axis=-1))

def coupling(own_atoms, far_atoms, self_cell):
    delta_a = own_atoms[0][..., :, None] - far_atoms[0][..., None, :]
    delta_b = own_atoms[1][..., :, None] - far_atoms[1][..., None, :]
    delta_c = own_atoms[2][..., :, None] - far_atoms[2][..., None, :]
    distance_sq = delta_a * delta_a + delta_b * delta_b + delta_c * delta_c
    radius = jnp.sqrt(distance_sq + 1e-06)
    pair_width = jnp.sqrt(own_atoms[3][..., :, None] ** 2 + far_atoms[3][..., None, :] ** 2)
    smooth_cut = (1.0 - jnp.minimum(distance_sq, 1.0)) ** 3
    kernel = 0.005 * smooth_cut * jax.scipy.special.erf(radius / pair_width) / radius
    kernel = kernel * own_atoms[4][..., :, None] * far_atoms[4][..., None, :]
    if self_cell:
        kernel = kernel * (1.0 - jnp.eye(kernel.shape[-1], dtype=jnp.float32))
    return kernel

def committee(flat_rows, w_in, b_in, w_hid, b_hid, w_out):

    def member_fn(weights):
        first_w, first_b, second_w, second_b, last_w = weights
        first = jnp.tanh(jnp.dot(flat_rows, first_w, preferred_element_type=jnp.float32) + first_b).astype(jnp.bfloat16)
        second = jnp.tanh(jnp.dot(first, second_w, preferred_element_type=jnp.float32) + second_b).astype(jnp.bfloat16)
        return jnp.dot(second, last_w.T, preferred_element_type=jnp.float32).T
    return lax.map(member_fn, (w_in, b_in, w_hid, b_hid, w_out))

def reference(descriptors, positions, species, counts, w_in, b_in, w_hid, b_hid, w_out):
    slot_iota = lax.broadcasted_iota(jnp.int32, (GA, GB, SLOT), 2)
    occupancy = (slot_iota < counts[:, :, None]).astype(jnp.float32)
    widths = lookup(species, (0.3, 0.4, 0.5, 0.35))
    shifts = lookup(species, (-0.8, 0.4, 1.2, -0.3))
    atom_data = jnp.stack([positions[0], positions[1], positions[2], widths, occupancy])
    outputs = committee(descriptors.reshape(-1, G), w_in, b_in, w_hid, b_hid, w_out)
    electro = outputs[:, 0].reshape(MEMBERS, GA, GB, SLOT) + shifts
    hardness = 2.5 + jax.nn.softplus(outputs[:, 1]).reshape(MEMBERS, GA, GB, SLOT)
    right_side = jnp.concatenate([-electro * occupancy, jnp.broadcast_to(occupancy, electro.shape)])
    diagonal = jnp.concatenate([hardness, hardness])
    atom_padded = jnp.pad(atom_data, ((0, 0), (1, 1), (1, 1), (0, 0)))

    def operate(vectors):
        vec_padded = jnp.pad(vectors, ((0, 0), (1, 1), (1, 1), (0, 0)))

        def row_fn(row_index):
            own_atoms = lax.dynamic_slice_in_dim(atom_padded, row_index + 1, 1, 1)[:, 0, 1:-1]
            summed = jnp.zeros((vectors.shape[0], GB, SLOT), jnp.float32)
            for row_step in (-1, 0, 1):
                far_row = lax.dynamic_slice_in_dim(atom_padded, row_index + 1 + row_step, 1, 1)[:, 0]
                vec_row = lax.dynamic_slice_in_dim(vec_padded, row_index + 1 + row_step, 1, 1)[:, 0]
                for col_step in (-1, 0, 1):
                    far_atoms = far_row[:, 1 + col_step:1 + col_step + GB]
                    tile_block = coupling(own_atoms, far_atoms, row_step == 0 and col_step == 0)
                    summed = summed + jnp.einsum('bij,rbj->rbi', tile_block, vec_row[:, 1 + col_step:1 + col_step + GB], precision=lax.Precision.HIGHEST)
            return summed
        rows_out = lax.map(row_fn, jnp.arange(GA, dtype=jnp.int32))
        return jnp.transpose(rows_out, (1, 0, 2, 3)) + diagonal * vectors

    def expand(values):
        return values[:, None, None, None]
    solution = jnp.zeros_like(right_side)
    residual = right_side
    direction = right_side
    norm_now = lax.optimization_barrier(jnp.sum(residual * residual, axis=(1, 2, 3)))
    for iteration in range(ITERS):
        image_vec = operate(direction)
        step_size = norm_now / lax.optimization_barrier(jnp.sum(direction * image_vec, axis=(1, 2, 3)))
        solution = solution + expand(step_size) * direction
        residual = residual - expand(step_size) * image_vec
        norm_next = lax.optimization_barrier(jnp.sum(residual * residual, axis=(1, 2, 3)))
        direction = residual + expand(norm_next / norm_now) * direction
        norm_now = norm_next
    source_part = solution[:MEMBERS]
    unit_part = solution[MEMBERS:]
    multiplier = lax.optimization_barrier(jnp.sum(source_part, axis=(1, 2, 3))) / lax.optimization_barrier(jnp.sum(unit_part, axis=(1, 2, 3)))
    return source_part - expand(multiplier) * unit_part
```

```python
import jax
import jax.numpy as jnp
from jax import lax
from jax.experimental import pallas as pl
from jax.experimental.pallas import tpu as pltpu
from jax.sharding import PartitionSpec as P

ITERS = 2

ERF_CENTRE = 1.000001 / 0.36
ERF_SERIES = (
    0.5889464636197189,
    -0.09338177281045029,
    0.018898799573350084,
    -0.003564793815999453,
    0.0005967292996019212,
    -8.816834134949323e-05,
    1.1544704937919275e-05,
    -1.3330679803919568e-06,
    1.4072010724176845e-07,
    -1.592848428884591e-08,
    1.4031096882113396e-09,
)

HARD, PLACE, SPREAD, FULL, ROWS = 8, 16, 19, 20, 24
OFFSETS = ((0, 0), (0, 1), (1, -1), (1, 0), (1, 1))
MOST_BLOCKS = 128


def pair_counts(rows, cols):
    return [(rows - da) * (cols - abs(db)) for da, db in OFFSETS]


def choose(species, entries):
    value = jnp.full(species.shape, entries[3], jnp.float32)
    for kind in (2, 1, 0):
        value = jnp.where(species == kind, entries[kind], value)
    return value


def slab_kernel(
    desc_ref, pos_ref, species_ref, counts_ref, w_in, b_in, w_hid, b_hid, w_out, out_ref
):
    members = w_in.shape[0]
    slots = desc_ref.shape[0]
    species = species_ref[0]
    slot_iota = lax.broadcasted_iota(jnp.int32, (1, slots), 1)
    occupancy = (slot_iota < counts_ref[0, 0]).astype(jnp.float32)
    widths = choose(species, (0.3, 0.4, 0.5, 0.35))
    shifts = choose(species, (-0.8, 0.4, 1.2, -0.3))
    rows = desc_ref[...]
    electro, raw = [], []
    for m in range(members):
        first = jnp.tanh(
            jnp.dot(rows, w_in[m], preferred_element_type=jnp.float32) + b_in[m : m + 1, :]
        ).astype(jnp.bfloat16)
        second = jnp.tanh(
            jnp.dot(first, w_hid[m], preferred_element_type=jnp.float32) + b_hid[m : m + 1, :]
        ).astype(jnp.bfloat16)
        outputs = lax.dot_general(
            w_out[m], second, (((1,), (1,)), ((), ())), preferred_element_type=jnp.float32
        )
        electro.append(outputs[0:1])
        raw.append(outputs[1:2])
    raw = jnp.concatenate(raw, axis=0)
    hardness = 2.5 + (jnp.maximum(raw, 0.0) + jnp.log1p(jnp.exp(-jnp.abs(raw))))
    right = -(jnp.concatenate(electro, axis=0) + shifts) * occupancy
    atoms = jnp.concatenate(
        [pos_ref[0, 0], pos_ref[1, 0], pos_ref[2, 0], widths * widths, occupancy]
        + [jnp.zeros((1, slots), jnp.float32)] * (ROWS - FULL - 1),
        axis=0,
    )
    for peer in range(out_ref.shape[0]):
        out_ref[peer, 0:HARD, :] = right
        out_ref[peer, HARD:PLACE, :] = hardness
        out_ref[peer, PLACE:ROWS, :] = atoms


def pair_block(cols, slab_ref, c, d, first_row, height, own):
    span = pl.ds(first_row, height)

    def gap(k):
        return cols[c, span, k : k + 1] - slab_ref[d, PLACE + k : PLACE + k + 1, :]

    da, db, dc = gap(0), gap(1), gap(2)
    capped = jnp.minimum(da * da + db * db + dc * dc, 1.0)
    left = 1.0 - capped
    inv = lax.rsqrt(cols[c, span, 3:4] + slab_ref[d, SPREAD : SPREAD + 1, :])
    y = (capped + 1e-06) * (inv * inv) - ERF_CENTRE
    value = jnp.full_like(y, 0.005 * ERF_SERIES[-1])
    for term in ERF_SERIES[-2::-1]:
        value = value * y + 0.005 * term
    value = value * ((left * inv) * (left * left))
    if own:
        i = lax.broadcasted_iota(jnp.int32, value.shape, 0) + first_row
        j = lax.broadcasted_iota(jnp.int32, value.shape, 1)
        value = jnp.where(i == j, 0.0, value)
    return value


def times(vectors, block):
    return jnp.dot(vectors, block, preferred_element_type=jnp.float32)


def times_t(vectors, block):
    return lax.dot_general(
        vectors, block, (((1,), (1,)), ((), ())), preferred_element_type=jnp.float32
    )


def halves(values):
    high = values.astype(jnp.bfloat16)
    return high, (values - high.astype(jnp.float32)).astype(jnp.bfloat16)


def solve_kernel(grid, slab_ref, out_ref, cols, vecs, sums, resid, resid_half, k_high, k_low):
    rows, columns = grid
    cells, _, slots = slab_ref.shape
    members = HARD
    starts = [0]
    for count in pair_counts(rows, columns):
        starts.append(starts[-1] + count)

    for c in range(cells):
        cols[c] = slab_ref[c, PLACE:ROWS, :].T
        high, low = halves(slab_ref[c, 0:HARD, :])
        vecs[c, 0:16, :] = jnp.concatenate([high.astype(jnp.float32), low.astype(jnp.float32)], axis=0).astype(jnp.bfloat16)
        full = slab_ref[c, FULL : FULL + 1, :]
        row = lax.broadcasted_iota(jnp.int32, (16, slots), 0)
        vecs[c, 16:32, :] = jnp.where(row == 0, full, 0.0).astype(jnp.bfloat16)
        sums[c] = jnp.zeros_like(sums[c])

    def each_pair(handle):
        for number, (da, db) in enumerate(OFFSETS):
            low_col = max(0, -db)
            width = columns - abs(db)

            def line(a, carry, number=number, da=da, db=db, low_col=low_col, width=width):
                for step in range(width):
                    c = a * columns + (low_col + step)
                    d = (a + da) * columns + (low_col + step + db)
                    carry = handle(c, d, starts[number] + a * width + step, number == 0, carry)
                return carry

            yield line, rows - da

    def first_pass(c, d, place, own, carry):
        for first_row in range(0, slots, 32):
            high, low = halves(pair_block(cols, slab_ref, c, d, first_row, 32, own))
            k_high[place, first_row : first_row + 32, :] = high
            k_low[place, first_row : first_row + 32, :] = low
        high, low = k_high[place], k_low[place]
        far = vecs[d]
        sums[c] += times_t(far, high) + times_t(far, low)
        if not own:
            near = vecs[c]
            sums[d] += times(near, high) + times(near, low)
        return carry

    for line, length in each_pair(first_pass):
        lax.fori_loop(0, length, line, 0)

    def applied(c):
        hard = slab_ref[c, HARD:PLACE, :]
        full = slab_ref[c, FULL : FULL + 1, :]
        right = slab_ref[c, 0:HARD, :]
        coupled = sums[c]
        image_s = hard * right + full * (coupled[0:8] + coupled[8:16])
        image_u = full * (hard + coupled[16:17])
        return hard, full, right, image_s, image_u

    shape = (members, slots)
    norm_s, prod_s, prod_u, total_s = (jnp.zeros(shape, jnp.float32) for _ in range(4))
    norm_u = jnp.zeros((1, slots), jnp.float32)
    for c in range(cells):
        hard, full, right, image_s, image_u = applied(c)
        norm_s += right * right
        norm_u += full * full
        prod_s += right * image_s
        prod_u += full * image_u
        total_s += right

    def over(values):
        return jnp.sum(values, axis=1, keepdims=True)

    both = lambda s, u: jnp.concatenate([s, jnp.broadcast_to(u, s.shape)], axis=0)
    norm0 = both(over(norm_s), over(norm_u))
    total0 = both(over(total_s), over(norm_u))
    alpha0 = norm0 / both(over(prod_s), over(prod_u))

    norm1, prod1, total1 = (jnp.zeros((2 * members, slots), jnp.float32) for _ in range(3))
    for c in range(cells):
        hard, full, right, image_s, image_u = applied(c)
        left = both(right, full) - alpha0 * jnp.concatenate([image_s, image_u], axis=0)
        resid[c] = left
        high, low = halves(left)
        resid_half[c, 0:16, :] = high
        resid_half[c, 16:32, :] = low
        square = left * left
        norm1 += square
        prod1 += jnp.concatenate([hard, hard], axis=0) * square
        total1 += left

    def second_pass(c, d, place, own, carry):
        near = resid_half[c]
        image = times(near, k_high[place]) + times(near, k_low[place])
        part = (image[0:16] + image[16:32]) * resid[d]
        return carry + (part if own else 2.0 * part)

    for line, length in each_pair(second_pass):
        prod1 = lax.fori_loop(0, length, line, prod1)

    norm1, prod1, total1 = over(norm1), over(prod1), over(total1)
    momentum = norm1 / norm0
    alpha1 = norm1 / (prod1 - momentum * norm1 / alpha0)
    weight0 = alpha0 + alpha1 * momentum
    totals = weight0 * total0 + alpha1 * total1
    multiplier = totals[0:members] / totals[members:]
    mine = lax.axis_index("cell") * columns + lax.axis_index("sub")
    right = both(slab_ref[mine, 0:HARD, :], slab_ref[mine, FULL : FULL + 1, :])
    answer = weight0 * right + alpha1 * resid[mine]
    out_ref[...] = answer[0:members] - multiplier * answer[members:]


def gathered(descriptors, positions, species, counts, w_in, b_in, w_hid, b_hid, w_out):
    rows, columns = lax.axis_size("cell"), lax.axis_size("sub")
    cells, slots, members = rows * columns, descriptors.shape[2], w_in.shape[0]
    vmem = pl.BlockSpec(memory_space=pltpu.VMEM)
    slabs = pl.pallas_call(
        slab_kernel,
        out_shape=jax.ShapeDtypeStruct((cells, ROWS, slots), jnp.float32),
        in_specs=[vmem] * 3 + [pl.BlockSpec(memory_space=pltpu.SMEM)] + [vmem] * 5,
        out_specs=vmem,
        compiler_params=pltpu.CompilerParams(vmem_limit_bytes=32 << 20),
        name="slab",
    )(descriptors.reshape(slots, -1), positions, species, counts, w_in, b_in, w_hid, b_hid, w_out)
    slabs = lax.all_to_all(slabs, ("cell", "sub"), 0, 0, tiled=True)
    blocks = sum(pair_counts(rows, columns))
    charges = pl.pallas_call(
        lambda *refs: solve_kernel((rows, columns), *refs),
        out_shape=jax.ShapeDtypeStruct((members, slots), jnp.float32),
        in_specs=[vmem],
        out_specs=vmem,
        scratch_shapes=[
            pltpu.VMEM((cells, slots, ROWS - PLACE), jnp.float32),
            pltpu.VMEM((cells, 32, slots), jnp.bfloat16),
            pltpu.VMEM((cells, 32, slots), jnp.float32),
            pltpu.VMEM((cells, 16, slots), jnp.float32),
            pltpu.VMEM((cells, 32, slots), jnp.bfloat16),
            pltpu.VMEM((blocks, slots, slots), jnp.bfloat16),
            pltpu.VMEM((blocks, slots, slots), jnp.bfloat16),
        ],
        compiler_params=pltpu.CompilerParams(vmem_limit_bytes=32 << 20),
        name="solve",
    )(slabs)
    return charges.reshape(members, 1, 1, slots)


def extended_2(shard, sides, width):
    for axis, dim in sides:
        size, length = (lax.axis_size(axis), shard.shape[dim])
        up = [(i, (i + 1) % size) for i in range(size - 1)]
        down = [(j, i) for i, j in up]
        last = lax.slice_in_dim(shard, length - width, length, axis=dim)
        leading = lax.slice_in_dim(shard, 0, width, axis=dim)
        before = lax.ppermute(last, axis, up)
        after = lax.ppermute(leading, axis, down)
        shard = jnp.concatenate([before, shard, after], axis=dim)
    return shard


def lookup(species, entries):
    choices_table = jnp.array(entries, jnp.float32)
    kinds = jnp.arange(4, dtype=jnp.int32)
    return jnp.sum((species[..., None] == kinds).astype(jnp.float32) * choices_table, axis=-1)


def coupling(own_atoms, far_atoms, self_cell):
    delta_a = own_atoms[0][..., :, None] - far_atoms[0][..., None, :]
    delta_b = own_atoms[1][..., :, None] - far_atoms[1][..., None, :]
    delta_c = own_atoms[2][..., :, None] - far_atoms[2][..., None, :]
    distance_sq = delta_a * delta_a + delta_b * delta_b + delta_c * delta_c
    radius = jnp.sqrt(distance_sq + 1e-06)
    pair_width = jnp.sqrt(own_atoms[3][..., :, None] ** 2 + far_atoms[3][..., None, :] ** 2)
    smooth_cut = (1.0 - jnp.minimum(distance_sq, 1.0)) ** 3
    kernel = 0.005 * smooth_cut * jax.scipy.special.erf(radius / pair_width) / radius
    kernel = kernel * own_atoms[4][..., :, None] * far_atoms[4][..., None, :]
    if self_cell:
        kernel = kernel * (1.0 - jnp.eye(kernel.shape[-1], dtype=jnp.float32))
    return kernel


def committee(flat_rows, w_in, b_in, w_hid, b_hid, w_out):

    def member_fn(weights):
        first_w, first_b, second_w, second_b, last_w = weights
        first = jnp.tanh(
            jnp.dot(flat_rows, first_w, preferred_element_type=jnp.float32) + first_b
        ).astype(jnp.bfloat16)
        second = jnp.tanh(
            jnp.dot(first, second_w, preferred_element_type=jnp.float32) + second_b
        ).astype(jnp.bfloat16)
        return jnp.dot(second, last_w.T, preferred_element_type=jnp.float32).T

    return lax.map(member_fn, (w_in, b_in, w_hid, b_hid, w_out))


def expand(values):
    return values[:, None, None, None]


def extend(vectors):
    return extended_2(vectors, (("cell", 1), ("sub", 2)), 1)


def two_products(residual, image_vec):
    return lax.psum(
        (
            jnp.sum(residual * residual, axis=(1, 2, 3)),
            jnp.sum(residual * image_vec, axis=(1, 2, 3)),
        ),
        ("cell", "sub"),
    )


def body(descriptors, positions, species, counts, w_in, b_in, w_hid, b_hid, w_out):
    rows_a, rows_b, slot_count, features = descriptors.shape
    members = w_in.shape[0]
    slot_iota = lax.broadcasted_iota(jnp.int32, (rows_a, rows_b, slot_count), 2)
    occupancy = (slot_iota < counts[:, :, None]).astype(jnp.float32)
    widths = lookup(species, (0.3, 0.4, 0.5, 0.35))
    shifts = lookup(species, (-0.8, 0.4, 1.2, -0.3))
    atom_data = jnp.stack([positions[0], positions[1], positions[2], widths, occupancy])
    extended = extended_2(atom_data, (("cell", 1), ("sub", 2)), 1)
    outputs = committee(descriptors.reshape(-1, features), w_in, b_in, w_hid, b_hid, w_out)
    electro = outputs[:, 0].reshape(members, rows_a, rows_b, slot_count) + shifts
    hardness = 2.5 + jax.nn.softplus(outputs[:, 1]).reshape(members, rows_a, rows_b, slot_count)
    right_side = jnp.concatenate([-electro * occupancy, jnp.broadcast_to(occupancy, electro.shape)])
    diagonal = jnp.concatenate([hardness, hardness])
    offsets = [(row_step, col_step) for row_step in (-1, 0, 1) for col_step in (-1, 0, 1)]

    def neighbours(grown, row_step, col_step):
        return grown[:, 1 + row_step : 1 + row_step + rows_a, 1 + col_step : 1 + col_step + rows_b]

    def block_for(row_step, col_step):
        return coupling(
            atom_data, neighbours(extended, row_step, col_step), row_step == 0 and col_step == 0
        )

    def operate(vectors):
        grown = extend(vectors)
        summed = diagonal * vectors
        for offset_number in range(9):
            row_step, col_step = offsets[offset_number]
            tile_block = block_for(row_step, col_step)
            summed = summed + jnp.einsum(
                "abij,rabj->rabi",
                tile_block,
                neighbours(grown, row_step, col_step),
                precision=lax.Precision.HIGHEST,
            )
        return summed

    solution = jnp.zeros_like(right_side)
    residual = right_side
    image_vec = operate(residual)
    norm_now, product = two_products(residual, image_vec)
    step_size = norm_now / product
    direction = residual
    along = image_vec
    for iteration in range(ITERS):
        solution = solution + expand(step_size) * direction
        residual = residual - expand(step_size) * along
        if iteration + 1 < ITERS:
            image_vec = operate(residual)
            norm_next, product = two_products(residual, image_vec)
            momentum = norm_next / norm_now
            step_size = norm_next / (product - momentum * norm_next / step_size)
            direction = residual + expand(momentum) * direction
            along = image_vec + expand(momentum) * along
            norm_now = norm_next
    source_part = solution[:members]
    unit_part = solution[members:]
    source_total, unit_total = lax.psum(
        (jnp.sum(source_part, axis=(1, 2, 3)), jnp.sum(unit_part, axis=(1, 2, 3))), ("cell", "sub")
    )
    multiplier = source_total / unit_total
    return source_part - expand(multiplier) * unit_part


def solution(mesh):
    placed = (
        P(("rep", "cell"), "sub", None, None),
        P(None, ("rep", "cell"), "sub", None),
        P(("rep", "cell"), "sub", None),
        P(("rep", "cell"), "sub"),
        P(),
        P(),
        P(),
        P(),
        P(),
    )
    rows, columns = mesh.shape["cell"], mesh.shape["sub"]
    return jax.shard_map(
        gathered if sum(pair_counts(rows, columns)) <= MOST_BLOCKS else body,
        mesh=mesh,
        in_specs=placed,
        out_specs=P(None, ("rep", "cell"), "sub", None),
        check_vma=False,
    )
```

```python
import jax
import jax.numpy as jnp
from jax import lax
from jax.experimental import pallas as pl
from jax.experimental.pallas import tpu as pltpu
from jax.sharding import PartitionSpec as P

ITERS = 2

ERF_CENTRE = 1.000001 / 0.36
ERF_SERIES = (
    0.5889464636197189,
    -0.09338177281045029,
    0.018898799573350084,
    -0.003564793815999453,
    0.0005967292996019212,
    -8.816834134949323e-05,
    1.1544704937919275e-05,
    -1.3330679803919568e-06,
    1.4072010724176845e-07,
    -1.592848428884591e-08,
    1.4031096882113396e-09,
)

HARD, PLACE, SPREAD, FULL, ROWS = 8, 16, 19, 20, 24
OFFSETS = ((0, 0), (0, 1), (1, -1), (1, 0), (1, 1))
MOST_BLOCKS = 128


def pair_counts(rows, cols):
    return [(rows - da) * (cols - abs(db)) for da, db in OFFSETS]


def choose(species, entries):
    value = jnp.full(species.shape, entries[3], jnp.float32)
    for kind in (2, 1, 0):
        value = jnp.where(species == kind, entries[kind], value)
    return value


def slab_kernel(*refs):
    sources, out_ref, landed, done = refs[:9], refs[9], refs[10:19], refs[19]
    members = sources[4].shape[0]
    copies = []

    def fetch(source, target):
        copy = pltpu.make_async_copy(source, target, done.at[len(copies)])
        copy.start()
        copies.append(copy)
        return copy

    desc_ref, pos_ref, species_ref, counts_ref, w_in, b_in, w_hid, b_hid, w_out = landed
    early = [fetch(sources[k], landed[k]) for k in (0, 5)]
    first_in = [fetch(sources[4].at[m], w_in.at[m]) for m in range(1)]
    early.append(fetch(sources[7], b_hid))
    hidden = [fetch(sources[6].at[m], w_hid.at[m]) for m in range(1)]
    early.append(fetch(sources[8], w_out))
    for m in range(1, members):
        first_in.append(fetch(sources[4].at[m], w_in.at[m]))
        hidden.append(fetch(sources[6].at[m], w_hid.at[m]))
    late = [fetch(sources[k], landed[k]) for k in (1, 2, 3)]
    for copy in early:
        copy.wait()
    rows = desc_ref[...]
    slots = rows.shape[0]
    electro, raw = [], []
    for m in range(members):
        first_in[m].wait()
        hidden[m].wait()
        first = jnp.tanh(
            jnp.dot(rows, w_in[m], preferred_element_type=jnp.float32) + b_in[m : m + 1, :]
        ).astype(jnp.bfloat16)
        second = jnp.tanh(
            jnp.dot(first, w_hid[m], preferred_element_type=jnp.float32) + b_hid[m : m + 1, :]
        ).astype(jnp.bfloat16)
        outputs = lax.dot_general(
            w_out[m], second, (((1,), (1,)), ((), ())), preferred_element_type=jnp.float32
        )
        electro.append(outputs[0:1])
        raw.append(outputs[1:2])
    for copy in late:
        copy.wait()
    species = species_ref[0]
    slot_iota = lax.broadcasted_iota(jnp.int32, (1, slots), 1)
    occupancy = (slot_iota < counts_ref[0, 0]).astype(jnp.float32)
    widths = choose(species, (0.3, 0.4, 0.5, 0.35))
    shifts = choose(species, (-0.8, 0.4, 1.2, -0.3))
    raw = jnp.concatenate(raw, axis=0)
    hardness = 2.5 + (jnp.maximum(raw, 0.0) + jnp.log1p(jnp.exp(-jnp.abs(raw))))
    right = -(jnp.concatenate(electro, axis=0) + shifts) * occupancy
    atoms = jnp.concatenate(
        [pos_ref[0, 0], pos_ref[1, 0], pos_ref[2, 0], widths * widths, occupancy]
        + [jnp.zeros((1, slots), jnp.float32)] * (ROWS - FULL - 1),
        axis=0,
    )
    for peer in range(out_ref.shape[0]):
        out_ref[peer, 0:HARD, :] = right
        out_ref[peer, HARD:PLACE, :] = hardness
        out_ref[peer, PLACE:ROWS, :] = atoms


def pair_block(cols, slab_ref, c, d, first_row, height, own):
    span = pl.ds(first_row, height)

    def gap(k):
        return cols[c, span, k : k + 1] - slab_ref[d, PLACE + k : PLACE + k + 1, :]

    da, db, dc = gap(0), gap(1), gap(2)
    capped = jnp.minimum(da * da + db * db + dc * dc, 1.0)
    left = 1.0 - capped
    inv = lax.rsqrt(cols[c, span, 3:4] + slab_ref[d, SPREAD : SPREAD + 1, :])
    y = (capped + 1e-06) * (inv * inv) - ERF_CENTRE
    value = jnp.full_like(y, 0.005 * ERF_SERIES[-1])
    for term in ERF_SERIES[-2::-1]:
        value = value * y + 0.005 * term
    value = value * ((left * inv) * (left * left))
    if own:
        i = lax.broadcasted_iota(jnp.int32, value.shape, 0) + first_row
        j = lax.broadcasted_iota(jnp.int32, value.shape, 1)
        value = jnp.where(i == j, 0.0, value)
    return value


def times(vectors, block):
    return jnp.dot(vectors, block, preferred_element_type=jnp.float32)


def times_t(vectors, block):
    return lax.dot_general(
        vectors, block, (((1,), (1,)), ((), ())), preferred_element_type=jnp.float32
    )


def halves(values):
    high = values.astype(jnp.bfloat16)
    return high, (values - high.astype(jnp.float32)).astype(jnp.bfloat16)


def solve_kernel(grid, slab_ref, out_ref, cols, vecs, sums, resid, resid_half, k_high, k_low):
    rows, columns = grid
    cells, _, slots = slab_ref.shape
    members = HARD
    starts = [0]
    for count in pair_counts(rows, columns):
        starts.append(starts[-1] + count)

    for c in range(cells):
        cols[c] = slab_ref[c, PLACE:ROWS, :].T
        high, low = halves(slab_ref[c, 0:HARD, :])
        vecs[c, 0:16, :] = jnp.concatenate([high.astype(jnp.float32), low.astype(jnp.float32)], axis=0).astype(jnp.bfloat16)
        full = slab_ref[c, FULL : FULL + 1, :]
        row = lax.broadcasted_iota(jnp.int32, (16, slots), 0)
        vecs[c, 16:32, :] = jnp.where(row == 0, full, 0.0).astype(jnp.bfloat16)
        sums[c] = jnp.zeros_like(sums[c])

    def each_pair(handle):
        for number, (da, db) in enumerate(OFFSETS):
            low_col = max(0, -db)
            width = columns - abs(db)

            def line(a, carry, number=number, da=da, db=db, low_col=low_col, width=width):
                pairs = []
                for step in range(width):
                    c = a * columns + (low_col + step)
                    d = (a + da) * columns + (low_col + step + db)
                    pairs.append((c, d, starts[number] + a * width + step))
                return handle(pairs, number == 0, carry)

            yield line, rows - da

    def first_pass(pairs, own, carry):
        terms = []
        for c, d, place in pairs:
            parts = []
            for first_row in range(0, slots, 32):
                parts.append(halves(pair_block(cols, slab_ref, c, d, first_row, 32, own)))
            high, low = (jnp.concatenate(part, axis=0) for part in zip(*parts))
            k_high[place] = high
            k_low[place] = low
            far = vecs[d]
            terms.append((c, times_t(far, high) + times_t(far, low)))
            if not own:
                near = vecs[c]
                terms.append((d, times(near, high) + times(near, low)))
        for cell, term in terms:
            sums[cell] += term
        return carry

    for line, length in each_pair(first_pass):
        lax.fori_loop(0, length, line, 0)

    def applied(c):
        hard = slab_ref[c, HARD:PLACE, :]
        full = slab_ref[c, FULL : FULL + 1, :]
        right = slab_ref[c, 0:HARD, :]
        coupled = sums[c]
        image_s = hard * right + full * (coupled[0:8] + coupled[8:16])
        image_u = full * (hard + coupled[16:17])
        return hard, full, right, image_s, image_u

    shape = (members, slots)
    norm_s, prod_s, prod_u, total_s = (jnp.zeros(shape, jnp.float32) for _ in range(4))
    norm_u = jnp.zeros((1, slots), jnp.float32)
    for c in range(cells):
        hard, full, right, image_s, image_u = applied(c)
        norm_s += right * right
        norm_u += full * full
        prod_s += right * image_s
        prod_u += full * image_u
        total_s += right

    def over(values):
        return jnp.sum(values, axis=1, keepdims=True)

    both = lambda s, u: jnp.concatenate([s, jnp.broadcast_to(u, s.shape)], axis=0)
    norm0 = both(over(norm_s), over(norm_u))
    total0 = both(over(total_s), over(norm_u))
    alpha0 = norm0 / both(over(prod_s), over(prod_u))

    norm1, prod1, total1 = (jnp.zeros((2 * members, slots), jnp.float32) for _ in range(3))
    for c in range(cells):
        hard, full, right, image_s, image_u = applied(c)
        left = both(right, full) - alpha0 * jnp.concatenate([image_s, image_u], axis=0)
        resid[c] = left
        high, low = halves(left)
        resid_half[c, 0:16, :] = high
        resid_half[c, 16:32, :] = low
        square = left * left
        norm1 += square
        prod1 += jnp.concatenate([hard, hard], axis=0) * square
        total1 += left

    def second_pass(pairs, own, carry):
        parts = []
        for c, d, place in pairs:
            near = resid_half[c]
            image = times(near, k_high[place]) + times(near, k_low[place])
            parts.append((image[0:16] + image[16:32]) * resid[d])
        total = sum(parts[1:], parts[0])
        return carry + (total if own else 2.0 * total)

    for line, length in each_pair(second_pass):
        prod1 = lax.fori_loop(0, length, line, prod1)

    norm1, prod1, total1 = over(norm1), over(prod1), over(total1)
    momentum = norm1 / norm0
    alpha1 = norm1 / (prod1 - momentum * norm1 / alpha0)
    weight0 = alpha0 + alpha1 * momentum
    totals = weight0 * total0 + alpha1 * total1
    multiplier = totals[0:members] / totals[members:]
    mine = lax.axis_index("cell") * columns + lax.axis_index("sub")
    right = both(slab_ref[mine, 0:HARD, :], slab_ref[mine, FULL : FULL + 1, :])
    answer = weight0 * right + alpha1 * resid[mine]
    out_ref[...] = answer[0:members] - multiplier * answer[members:]


def solve_only(slabs):
    rows, columns = lax.axis_size("cell"), lax.axis_size("sub")
    cells, _, slots = slabs.shape
    vmem = pl.BlockSpec(memory_space=pltpu.VMEM)
    blocks = sum(pair_counts(rows, columns))
    return pl.pallas_call(
        lambda *refs: solve_kernel((rows, columns), *refs),
        out_shape=jax.ShapeDtypeStruct((HARD, slots), jnp.float32),
        in_specs=[vmem],
        out_specs=vmem,
        scratch_shapes=[
            pltpu.VMEM((cells, slots, ROWS - PLACE), jnp.float32),
            pltpu.VMEM((cells, 32, slots), jnp.bfloat16),
            pltpu.VMEM((cells, 32, slots), jnp.float32),
            pltpu.VMEM((cells, 16, slots), jnp.float32),
            pltpu.VMEM((cells, 32, slots), jnp.bfloat16),
            pltpu.VMEM((blocks, slots, slots), jnp.bfloat16),
            pltpu.VMEM((blocks, slots, slots), jnp.bfloat16),
        ],
        compiler_params=pltpu.CompilerParams(vmem_limit_bytes=32 << 20),
        name="solve",
    )(slabs)


def gathered(descriptors, positions, species, counts, w_in, b_in, w_hid, b_hid, w_out):
    rows, columns = lax.axis_size("cell"), lax.axis_size("sub")
    cells, slots, members = rows * columns, descriptors.shape[2], w_in.shape[0]
    vmem = pl.BlockSpec(memory_space=pltpu.VMEM)
    args = (
        descriptors.reshape(slots, -1), positions, species, counts, w_in, b_in, w_hid, b_hid, w_out
    )
    landed = [
        (pltpu.SMEM if arg is counts else pltpu.VMEM)(arg.shape, arg.dtype) for arg in args
    ]
    slabs = pl.pallas_call(
        slab_kernel,
        out_shape=jax.ShapeDtypeStruct((cells, ROWS, slots), jnp.float32),
        in_specs=[pl.BlockSpec(memory_space=pltpu.HBM)] * len(args),
        out_specs=vmem,
        scratch_shapes=landed + [pltpu.SemaphoreType.DMA((7 + 2 * members,))],
        compiler_params=pltpu.CompilerParams(vmem_limit_bytes=32 << 20),
        name="slab",
    )(*args)
    slabs = lax.all_to_all(slabs, ("cell", "sub"), 0, 0, tiled=True)
    charges = solve_only(slabs)
    return charges.reshape(members, 1, 1, slots)


def extended_2(shard, sides, width):
    for axis, dim in sides:
        size, length = (lax.axis_size(axis), shard.shape[dim])
        up = [(i, (i + 1) % size) for i in range(size - 1)]
        down = [(j, i) for i, j in up]
        last = lax.slice_in_dim(shard, length - width, length, axis=dim)
        leading = lax.slice_in_dim(shard, 0, width, axis=dim)
        before = lax.ppermute(last, axis, up)
        after = lax.ppermute(leading, axis, down)
        shard = jnp.concatenate([before, shard, after], axis=dim)
    return shard


def lookup(species, entries):
    choices_table = jnp.array(entries, jnp.float32)
    kinds = jnp.arange(4, dtype=jnp.int32)
    return jnp.sum((species[..., None] == kinds).astype(jnp.float32) * choices_table, axis=-1)


def coupling(own_atoms, far_atoms, self_cell):
    delta_a = own_atoms[0][..., :, None] - far_atoms[0][..., None, :]
    delta_b = own_atoms[1][..., :, None] - far_atoms[1][..., None, :]
    delta_c = own_atoms[2][..., :, None] - far_atoms[2][..., None, :]
    distance_sq = delta_a * delta_a + delta_b * delta_b + delta_c * delta_c
    radius = jnp.sqrt(distance_sq + 1e-06)
    pair_width = jnp.sqrt(own_atoms[3][..., :, None] ** 2 + far_atoms[3][..., None, :] ** 2)
    smooth_cut = (1.0 - jnp.minimum(distance_sq, 1.0)) ** 3
    kernel = 0.005 * smooth_cut * jax.scipy.special.erf(radius / pair_width) / radius
    kernel = kernel * own_atoms[4][..., :, None] * far_atoms[4][..., None, :]
    if self_cell:
        kernel = kernel * (1.0 - jnp.eye(kernel.shape[-1], dtype=jnp.float32))
    return kernel


def committee(flat_rows, w_in, b_in, w_hid, b_hid, w_out):

    def member_fn(weights):
        first_w, first_b, second_w, second_b, last_w = weights
        first = jnp.tanh(
            jnp.dot(flat_rows, first_w, preferred_element_type=jnp.float32) + first_b
        ).astype(jnp.bfloat16)
        second = jnp.tanh(
            jnp.dot(first, second_w, preferred_element_type=jnp.float32) + second_b
        ).astype(jnp.bfloat16)
        return jnp.dot(second, last_w.T, preferred_element_type=jnp.float32).T

    return lax.map(member_fn, (w_in, b_in, w_hid, b_hid, w_out))


def expand(values):
    return values[:, None, None, None]


def extend(vectors):
    return extended_2(vectors, (("cell", 1), ("sub", 2)), 1)


def two_products(residual, image_vec):
    return lax.psum(
        (
            jnp.sum(residual * residual, axis=(1, 2, 3)),
            jnp.sum(residual * image_vec, axis=(1, 2, 3)),
        ),
        ("cell", "sub"),
    )


def body(descriptors, positions, species, counts, w_in, b_in, w_hid, b_hid, w_out):
    rows_a, rows_b, slot_count, features = descriptors.shape
    members = w_in.shape[0]
    slot_iota = lax.broadcasted_iota(jnp.int32, (rows_a, rows_b, slot_count), 2)
    occupancy = (slot_iota < counts[:, :, None]).astype(jnp.float32)
    widths = lookup(species, (0.3, 0.4, 0.5, 0.35))
    shifts = lookup(species, (-0.8, 0.4, 1.2, -0.3))
    atom_data = jnp.stack([positions[0], positions[1], positions[2], widths, occupancy])
    extended = extended_2(atom_data, (("cell", 1), ("sub", 2)), 1)
    outputs = committee(descriptors.reshape(-1, features), w_in, b_in, w_hid, b_hid, w_out)
    electro = outputs[:, 0].reshape(members, rows_a, rows_b, slot_count) + shifts
    hardness = 2.5 + jax.nn.softplus(outputs[:, 1]).reshape(members, rows_a, rows_b, slot_count)
    right_side = jnp.concatenate([-electro * occupancy, jnp.broadcast_to(occupancy, electro.shape)])
    diagonal = jnp.concatenate([hardness, hardness])
    offsets = [(row_step, col_step) for row_step in (-1, 0, 1) for col_step in (-1, 0, 1)]

    def neighbours(grown, row_step, col_step):
        return grown[:, 1 + row_step : 1 + row_step + rows_a, 1 + col_step : 1 + col_step + rows_b]

    def block_for(row_step, col_step):
        return coupling(
            atom_data, neighbours(extended, row_step, col_step), row_step == 0 and col_step == 0
        )

    def operate(vectors):
        grown = extend(vectors)
        summed = diagonal * vectors
        for offset_number in range(9):
            row_step, col_step = offsets[offset_number]
            tile_block = block_for(row_step, col_step)
            summed = summed + jnp.einsum(
                "abij,rabj->rabi",
                tile_block,
                neighbours(grown, row_step, col_step),
                precision=lax.Precision.HIGHEST,
            )
        return summed

    solution = jnp.zeros_like(right_side)
    residual = right_side
    image_vec = operate(residual)
    norm_now, product = two_products(residual, image_vec)
    step_size = norm_now / product
    direction = residual
    along = image_vec
    for iteration in range(ITERS):
        solution = solution + expand(step_size) * direction
        residual = residual - expand(step_size) * along
        if iteration + 1 < ITERS:
            image_vec = operate(residual)
            norm_next, product = two_products(residual, image_vec)
            momentum = norm_next / norm_now
            step_size = norm_next / (product - momentum * norm_next / step_size)
            direction = residual + expand(momentum) * direction
            along = image_vec + expand(momentum) * along
            norm_now = norm_next
    source_part = solution[:members]
    unit_part = solution[members:]
    source_total, unit_total = lax.psum(
        (jnp.sum(source_part, axis=(1, 2, 3)), jnp.sum(unit_part, axis=(1, 2, 3))), ("cell", "sub")
    )
    multiplier = source_total / unit_total
    return source_part - expand(multiplier) * unit_part


def solution(mesh):
    placed = (
        P(("rep", "cell"), "sub", None, None),
        P(None, ("rep", "cell"), "sub", None),
        P(("rep", "cell"), "sub", None),
        P(("rep", "cell"), "sub"),
        P(),
        P(),
        P(),
        P(),
        P(),
    )
    rows, columns = mesh.shape["cell"], mesh.shape["sub"]
    return jax.shard_map(
        gathered if sum(pair_counts(rows, columns)) <= MOST_BLOCKS else body,
        mesh=mesh,
        in_specs=placed,
        out_specs=P(None, ("rep", "cell"), "sub", None),
        check_vma=False,
    )
```

```python
import jax
import jax.numpy as jnp
from jax import lax
from jax.experimental import pallas as pl
from jax.experimental.pallas import tpu as pltpu
from jax.sharding import PartitionSpec as P

ITERS = 2

ERF_CENTRE = 1.000001 / 0.36
ERF_SERIES = (
    0.5889464636197189,
    -0.09338177281045029,
    0.018898799573350084,
    -0.003564793815999453,
    0.0005967292996019212,
    -8.816834134949323e-05,
    1.1544704937919275e-05,
    -1.3330679803919568e-06,
    1.4072010724176845e-07,
    -1.592848428884591e-08,
    1.4031096882113396e-09,
)

HARD, PLACE, SPREAD, FULL, ROWS = 8, 16, 19, 20, 24
OFFSETS = ((0, 0), (0, 1), (1, -1), (1, 0), (1, 1))
MOST_BLOCKS = 128


def pair_counts(rows, cols):
    return [(rows - da) * (cols - abs(db)) for da, db in OFFSETS]


def choose(species, entries):
    value = jnp.full(species.shape, entries[3], jnp.float32)
    for kind in (2, 1, 0):
        value = jnp.where(species == kind, entries[kind], value)
    return value


def slab_kernel(*refs):
    sources, out_ref, landed, done = refs[:9], refs[9], refs[10:19], refs[19]
    members = sources[4].shape[0]
    copies = []

    def fetch(source, target):
        copy = pltpu.make_async_copy(source, target, done.at[len(copies)])
        copy.start()
        copies.append(copy)
        return copy

    desc_ref, pos_ref, species_ref, counts_ref, w_in, b_in, w_hid, b_hid, w_out = landed
    early = [fetch(sources[k], landed[k]) for k in (0, 5)]
    first_in = [fetch(sources[4].at[m], w_in.at[m]) for m in range(1)]
    early.append(fetch(sources[7], b_hid))
    hidden = [fetch(sources[6].at[m], w_hid.at[m]) for m in range(1)]
    early.append(fetch(sources[8], w_out))
    for m in range(1, members):
        first_in.append(fetch(sources[4].at[m], w_in.at[m]))
        hidden.append(fetch(sources[6].at[m], w_hid.at[m]))
    late = [fetch(sources[k], landed[k]) for k in (1, 2, 3)]
    for copy in early:
        copy.wait()
    rows = desc_ref[...]
    slots = rows.shape[0]
    electro, raw = [], []
    for m in range(members):
        first_in[m].wait()
        hidden[m].wait()
        first = jnp.tanh(
            jnp.dot(rows, w_in[m], preferred_element_type=jnp.float32) + b_in[m : m + 1, :]
        ).astype(jnp.bfloat16)
        second = jnp.tanh(
            jnp.dot(first, w_hid[m], preferred_element_type=jnp.float32) + b_hid[m : m + 1, :]
        ).astype(jnp.bfloat16)
        outputs = lax.dot_general(
            w_out[m], second, (((1,), (1,)), ((), ())), preferred_element_type=jnp.float32
        )
        electro.append(outputs[0:1])
        raw.append(outputs[1:2])
    for copy in late:
        copy.wait()
    species = species_ref[0]
    slot_iota = lax.broadcasted_iota(jnp.int32, (1, slots), 1)
    occupancy = (slot_iota < counts_ref[0, 0]).astype(jnp.float32)
    widths = choose(species, (0.3, 0.4, 0.5, 0.35))
    shifts = choose(species, (-0.8, 0.4, 1.2, -0.3))
    raw = jnp.concatenate(raw, axis=0)
    hardness = 2.5 + (jnp.maximum(raw, 0.0) + jnp.log1p(jnp.exp(-jnp.abs(raw))))
    right = -(jnp.concatenate(electro, axis=0) + shifts) * occupancy
    atoms = jnp.concatenate(
        [pos_ref[0, 0], pos_ref[1, 0], pos_ref[2, 0], widths * widths, occupancy]
        + [jnp.zeros((1, slots), jnp.float32)] * (ROWS - FULL - 1),
        axis=0,
    )
    for peer in range(out_ref.shape[0]):
        out_ref[peer, 0:HARD, :] = right
        out_ref[peer, HARD:PLACE, :] = hardness
        out_ref[peer, PLACE:ROWS, :] = atoms


def pair_block(cols, slab_ref, c, d, first_row, height, own):
    span = pl.ds(first_row, height)

    def gap(k):
        return cols[c, span, k : k + 1] - slab_ref[d, PLACE + k : PLACE + k + 1, :]

    da, db, dc = gap(0), gap(1), gap(2)
    capped = jnp.minimum(da * da + db * db + dc * dc, 1.0)
    left = 1.0 - capped
    inv = lax.rsqrt(cols[c, span, 3:4] + slab_ref[d, SPREAD : SPREAD + 1, :])
    y = (capped + 1e-06) * (inv * inv) - ERF_CENTRE
    value = jnp.full_like(y, 0.005 * ERF_SERIES[-1])
    for term in ERF_SERIES[-2::-1]:
        value = value * y + 0.005 * term
    value = value * ((left * inv) * (left * left))
    if own:
        i = lax.broadcasted_iota(jnp.int32, value.shape, 0) + first_row
        j = lax.broadcasted_iota(jnp.int32, value.shape, 1)
        value = jnp.where(i == j, 0.0, value)
    return value


def times(vectors, block):
    return jnp.dot(vectors, block, preferred_element_type=jnp.float32)


def times_t(vectors, block):
    return lax.dot_general(
        vectors, block, (((1,), (1,)), ((), ())), preferred_element_type=jnp.float32
    )


def halves(values):
    high = values.astype(jnp.bfloat16)
    return high, (values - high.astype(jnp.float32)).astype(jnp.bfloat16)


def solve_kernel(grid, slab_ref, out_ref, cols, vecs, sums, resid, resid_half, k_high, k_low):
    rows, columns = grid
    cells, _, slots = slab_ref.shape
    members = HARD
    starts = [0]
    for count in pair_counts(rows, columns):
        starts.append(starts[-1] + count)

    for c in range(cells):
        cols[c] = slab_ref[c, PLACE:ROWS, :].T
        high, low = halves(slab_ref[c, 0:HARD, :])
        vecs[c, 0:16, :] = jnp.concatenate([high.astype(jnp.float32), low.astype(jnp.float32)], axis=0).astype(jnp.bfloat16)
        full = slab_ref[c, FULL : FULL + 1, :]
        row = lax.broadcasted_iota(jnp.int32, (16, slots), 0)
        vecs[c, 16:32, :] = jnp.where(row == 0, full, 0.0).astype(jnp.bfloat16)
        sums[c] = jnp.zeros_like(sums[c])

    def each_pair(handle):
        for number, (da, db) in enumerate(OFFSETS):
            low_col = max(0, -db)
            width = columns - abs(db)

            def line(a, carry, number=number, da=da, db=db, low_col=low_col, width=width):
                pairs = []
                for step in range(width):
                    c = a * columns + (low_col + step)
                    d = (a + da) * columns + (low_col + step + db)
                    pairs.append((c, d, starts[number] + a * width + step))
                return handle(pairs, number == 0, carry)

            yield line, rows - da

    def first_pass(pairs, own, carry):
        terms = []
        for c, d, place in pairs:
            parts = []
            for first_row in range(0, slots, 32):
                parts.append(halves(pair_block(cols, slab_ref, c, d, first_row, 32, own)))
            high, low = (jnp.concatenate(part, axis=0) for part in zip(*parts))
            k_high[place] = high
            k_low[place] = low
            far = vecs[d]
            terms.append((c, times_t(far, high) + times_t(far, low)))
            if not own:
                near = vecs[c]
                terms.append((d, times(near, high) + times(near, low)))
        for cell, term in terms:
            sums[cell] += term
        return carry

    for line, length in each_pair(first_pass):
        lax.fori_loop(0, length, line, 0)

    def applied(c):
        hard = slab_ref[c, HARD:PLACE, :]
        full = slab_ref[c, FULL : FULL + 1, :]
        right = slab_ref[c, 0:HARD, :]
        coupled = sums[c]
        image_s = hard * right + full * (coupled[0:8] + coupled[8:16])
        image_u = full * (hard + coupled[16:17])
        return hard, full, right, image_s, image_u

    shape = (members, slots)
    norm_s, prod_s, prod_u, total_s = (jnp.zeros(shape, jnp.float32) for _ in range(4))
    norm_u = jnp.zeros((1, slots), jnp.float32)
    for c in range(cells):
        hard, full, right, image_s, image_u = applied(c)
        norm_s += right * right
        norm_u += full * full
        prod_s += right * image_s
        prod_u += full * image_u
        total_s += right

    def over(values):
        return jnp.sum(values, axis=1, keepdims=True)

    both = lambda s, u: jnp.concatenate([s, jnp.broadcast_to(u, s.shape)], axis=0)
    norm0 = both(over(norm_s), over(norm_u))
    total0 = both(over(total_s), over(norm_u))
    alpha0 = norm0 / both(over(prod_s), over(prod_u))

    norm1, prod1, total1 = (jnp.zeros((2 * members, slots), jnp.float32) for _ in range(3))
    for c in range(cells):
        hard, full, right, image_s, image_u = applied(c)
        left = both(right, full) - alpha0 * jnp.concatenate([image_s, image_u], axis=0)
        resid[c] = left
        high, low = halves(left)
        resid_half[c, 0:16, :] = high
        resid_half[c, 16:32, :] = low
        square = left * left
        norm1 += square
        prod1 += jnp.concatenate([hard, hard], axis=0) * square
        total1 += left

    def second_pass(pairs, own, carry):
        parts = []
        for c, d, place in pairs:
            near = resid_half[c]
            image = times(near, k_high[place]) + times(near, k_low[place])
            parts.append((image[0:16] + image[16:32]) * resid[d])
        total = sum(parts[1:], parts[0])
        return carry + (total if own else 2.0 * total)

    for line, length in each_pair(second_pass):
        prod1 = lax.fori_loop(0, length, line, prod1)

    norm1, prod1, total1 = over(norm1), over(prod1), over(total1)
    momentum = norm1 / norm0
    alpha1 = norm1 / (prod1 - momentum * norm1 / alpha0)
    weight0 = alpha0 + alpha1 * momentum
    totals = weight0 * total0 + alpha1 * total1
    multiplier = totals[0:members] / totals[members:]
    mine = lax.axis_index("cell") * columns + lax.axis_index("sub")
    right = both(slab_ref[mine, 0:HARD, :], slab_ref[mine, FULL : FULL + 1, :])
    answer = weight0 * right + alpha1 * resid[mine]
    out_ref[...] = answer[0:members] - multiplier * answer[members:]


def solve_only(slabs):
    rows, columns = lax.axis_size("cell"), lax.axis_size("sub")
    cells, _, slots = slabs.shape
    vmem = pl.BlockSpec(memory_space=pltpu.VMEM)
    blocks = sum(pair_counts(rows, columns))
    return pl.pallas_call(
        lambda *refs: solve_kernel((rows, columns), *refs),
        out_shape=jax.ShapeDtypeStruct((HARD, slots), jnp.float32),
        in_specs=[vmem],
        out_specs=vmem,
        scratch_shapes=[
            pltpu.VMEM((cells, slots, ROWS - PLACE), jnp.float32),
            pltpu.VMEM((cells, 32, slots), jnp.bfloat16),
            pltpu.VMEM((cells, 32, slots), jnp.float32),
            pltpu.VMEM((cells, 16, slots), jnp.float32),
            pltpu.VMEM((cells, 32, slots), jnp.bfloat16),
            pltpu.VMEM((blocks, slots, slots), jnp.bfloat16),
            pltpu.VMEM((blocks, slots, slots), jnp.bfloat16),
        ],
        compiler_params=pltpu.CompilerParams(vmem_limit_bytes=32 << 20),
        name="solve",
    )(slabs)


def gathered(descriptors, positions, species, counts, w_in, b_in, w_hid, b_hid, w_out):
    rows, columns = lax.axis_size("cell"), lax.axis_size("sub")
    cells, slots, members = rows * columns, descriptors.shape[2], w_in.shape[0]
    vmem = pl.BlockSpec(memory_space=pltpu.VMEM)
    args = (
        descriptors.reshape(slots, -1), positions, species, counts, w_in, b_in, w_hid, b_hid, w_out
    )
    landed = [
        (pltpu.SMEM if arg is counts else pltpu.VMEM)(arg.shape, arg.dtype) for arg in args
    ]
    slabs = pl.pallas_call(
        slab_kernel,
        out_shape=jax.ShapeDtypeStruct((cells, ROWS, slots), jnp.float32),
        in_specs=[pl.BlockSpec(memory_space=pltpu.HBM)] * len(args),
        out_specs=vmem,
        scratch_shapes=landed + [pltpu.SemaphoreType.DMA((7 + 2 * members,))],
        compiler_params=pltpu.CompilerParams(vmem_limit_bytes=60 << 20),
        name="slab",
    )(*args)
    slabs = lax.all_to_all(slabs, ("cell", "sub"), 0, 0, tiled=True)
    charges = solve_only(slabs)
    return charges.reshape(members, 1, 1, slots)


def extended_2(shard, sides, width):
    for axis, dim in sides:
        size, length = (lax.axis_size(axis), shard.shape[dim])
        up = [(i, (i + 1) % size) for i in range(size - 1)]
        down = [(j, i) for i, j in up]
        last = lax.slice_in_dim(shard, length - width, length, axis=dim)
        leading = lax.slice_in_dim(shard, 0, width, axis=dim)
        before = lax.ppermute(last, axis, up)
        after = lax.ppermute(leading, axis, down)
        shard = jnp.concatenate([before, shard, after], axis=dim)
    return shard


def lookup(species, entries):
    choices_table = jnp.array(entries, jnp.float32)
    kinds = jnp.arange(4, dtype=jnp.int32)
    return jnp.sum((species[..., None] == kinds).astype(jnp.float32) * choices_table, axis=-1)


def coupling(own_atoms, far_atoms, self_cell):
    delta_a = own_atoms[0][..., :, None] - far_atoms[0][..., None, :]
    delta_b = own_atoms[1][..., :, None] - far_atoms[1][..., None, :]
    delta_c = own_atoms[2][..., :, None] - far_atoms[2][..., None, :]
    distance_sq = delta_a * delta_a + delta_b * delta_b + delta_c * delta_c
    radius = jnp.sqrt(distance_sq + 1e-06)
    pair_width = jnp.sqrt(own_atoms[3][..., :, None] ** 2 + far_atoms[3][..., None, :] ** 2)
    smooth_cut = (1.0 - jnp.minimum(distance_sq, 1.0)) ** 3
    kernel = 0.005 * smooth_cut * jax.scipy.special.erf(radius / pair_width) / radius
    kernel = kernel * own_atoms[4][..., :, None] * far_atoms[4][..., None, :]
    if self_cell:
        kernel = kernel * (1.0 - jnp.eye(kernel.shape[-1], dtype=jnp.float32))
    return kernel


def committee(flat_rows, w_in, b_in, w_hid, b_hid, w_out):

    def member_fn(weights):
        first_w, first_b, second_w, second_b, last_w = weights
        first = jnp.tanh(
            jnp.dot(flat_rows, first_w, preferred_element_type=jnp.float32) + first_b
        ).astype(jnp.bfloat16)
        second = jnp.tanh(
            jnp.dot(first, second_w, preferred_element_type=jnp.float32) + second_b
        ).astype(jnp.bfloat16)
        return jnp.dot(second, last_w.T, preferred_element_type=jnp.float32).T

    return lax.map(member_fn, (w_in, b_in, w_hid, b_hid, w_out))


def expand(values):
    return values[:, None, None, None]


def extend(vectors):
    return extended_2(vectors, (("cell", 1), ("sub", 2)), 1)


def two_products(residual, image_vec):
    return lax.psum(
        (
            jnp.sum(residual * residual, axis=(1, 2, 3)),
            jnp.sum(residual * image_vec, axis=(1, 2, 3)),
        ),
        ("cell", "sub"),
    )


def body(descriptors, positions, species, counts, w_in, b_in, w_hid, b_hid, w_out):
    rows_a, rows_b, slot_count, features = descriptors.shape
    members = w_in.shape[0]
    slot_iota = lax.broadcasted_iota(jnp.int32, (rows_a, rows_b, slot_count), 2)
    occupancy = (slot_iota < counts[:, :, None]).astype(jnp.float32)
    widths = lookup(species, (0.3, 0.4, 0.5, 0.35))
    shifts = lookup(species, (-0.8, 0.4, 1.2, -0.3))
    atom_data = jnp.stack([positions[0], positions[1], positions[2], widths, occupancy])
    extended = extended_2(atom_data, (("cell", 1), ("sub", 2)), 1)
    outputs = committee(descriptors.reshape(-1, features), w_in, b_in, w_hid, b_hid, w_out)
    electro = outputs[:, 0].reshape(members, rows_a, rows_b, slot_count) + shifts
    hardness = 2.5 + jax.nn.softplus(outputs[:, 1]).reshape(members, rows_a, rows_b, slot_count)
    right_side = jnp.concatenate([-electro * occupancy, jnp.broadcast_to(occupancy, electro.shape)])
    diagonal = jnp.concatenate([hardness, hardness])
    offsets = [(row_step, col_step) for row_step in (-1, 0, 1) for col_step in (-1, 0, 1)]

    def neighbours(grown, row_step, col_step):
        return grown[:, 1 + row_step : 1 + row_step + rows_a, 1 + col_step : 1 + col_step + rows_b]

    def block_for(row_step, col_step):
        return coupling(
            atom_data, neighbours(extended, row_step, col_step), row_step == 0 and col_step == 0
        )

    def operate(vectors):
        grown = extend(vectors)
        summed = diagonal * vectors
        for offset_number in range(9):
            row_step, col_step = offsets[offset_number]
            tile_block = block_for(row_step, col_step)
            summed = summed + jnp.einsum(
                "abij,rabj->rabi",
                tile_block,
                neighbours(grown, row_step, col_step),
                precision=lax.Precision.HIGHEST,
            )
        return summed

    solution = jnp.zeros_like(right_side)
    residual = right_side
    image_vec = operate(residual)
    norm_now, product = two_products(residual, image_vec)
    step_size = norm_now / product
    direction = residual
    along = image_vec
    for iteration in range(ITERS):
        solution = solution + expand(step_size) * direction
        residual = residual - expand(step_size) * along
        if iteration + 1 < ITERS:
            image_vec = operate(residual)
            norm_next, product = two_products(residual, image_vec)
            momentum = norm_next / norm_now
            step_size = norm_next / (product - momentum * norm_next / step_size)
            direction = residual + expand(momentum) * direction
            along = image_vec + expand(momentum) * along
            norm_now = norm_next
    source_part = solution[:members]
    unit_part = solution[members:]
    source_total, unit_total = lax.psum(
        (jnp.sum(source_part, axis=(1, 2, 3)), jnp.sum(unit_part, axis=(1, 2, 3))), ("cell", "sub")
    )
    multiplier = source_total / unit_total
    return source_part - expand(multiplier) * unit_part


def solution(mesh):
    placed = (
        P(("rep", "cell"), "sub", None, None),
        P(None, ("rep", "cell"), "sub", None),
        P(("rep", "cell"), "sub", None),
        P(("rep", "cell"), "sub"),
        P(),
        P(),
        P(),
        P(),
        P(),
    )
    rows, columns = mesh.shape["cell"], mesh.shape["sub"]
    return jax.shard_map(
        gathered if sum(pair_counts(rows, columns)) <= MOST_BLOCKS else body,
        mesh=mesh,
        in_specs=placed,
        out_specs=P(None, ("rep", "cell"), "sub", None),
        check_vma=False,
    )
```

```python
import jax
import jax.numpy as jnp
from jax import lax
from jax.experimental import pallas as pl
from jax.experimental.pallas import tpu as pltpu
from jax.sharding import PartitionSpec as P

ITERS = 2

ERF_CENTRE = 1.000001 / 0.36
ERF_SERIES = (
    0.5889464636197189,
    -0.09338177281045029,
    0.018898799573350084,
    -0.003564793815999453,
    0.0005967292996019212,
    -8.816834134949323e-05,
    1.1544704937919275e-05,
    -1.3330679803919568e-06,
    1.4072010724176845e-07,
    -1.592848428884591e-08,
    1.4031096882113396e-09,
)

WIDTHS = (0.3, 0.4, 0.5, 0.35)

HARD, PLACE, KIND, FULL, ROWS = 8, 16, 19, 20, 24
SQUARE, FEATURES = 24, 48
OFFSETS = ((0, 0), (0, 1), (1, -1), (1, 0), (1, 1))
MOST_BLOCKS = 128
CHUNK = 128


def pair_counts(rows, cols):
    return [(rows - da) * (cols - abs(db)) for da, db in OFFSETS]


def choose(species, entries):
    value = jnp.full(species.shape, entries[3], jnp.float32)
    for kind in (2, 1, 0):
        value = jnp.where(species == kind, entries[kind], value)
    return value


def slab_kernel(*refs):
    sources, out_ref, landed, done = refs[:9], refs[9], refs[10:19], refs[19]
    members = sources[4].shape[0]
    copies = []

    def fetch(source, target):
        copy = pltpu.make_async_copy(source, target, done.at[len(copies)])
        copy.start()
        copies.append(copy)
        return copy

    desc_ref, pos_ref, species_ref, counts_ref, w_in, b_in, w_hid, b_hid, w_out = landed
    early = [fetch(sources[k], landed[k]) for k in (0, 5)]
    first_in = [fetch(sources[4].at[m], w_in.at[m]) for m in range(1)]
    early.append(fetch(sources[7], b_hid))
    hidden = [fetch(sources[6].at[m], w_hid.at[m]) for m in range(1)]
    early.append(fetch(sources[8], w_out))
    for m in range(1, members):
        first_in.append(fetch(sources[4].at[m], w_in.at[m]))
        hidden.append(fetch(sources[6].at[m], w_hid.at[m]))
    late = [fetch(sources[k], landed[k]) for k in (1, 2, 3)]
    for copy in early:
        copy.wait()
    rows = desc_ref[...]
    slots = rows.shape[0]
    electro, raw = [], []
    for m in range(members):
        first_in[m].wait()
        hidden[m].wait()
        first = jnp.tanh(
            jnp.dot(rows, w_in[m], preferred_element_type=jnp.float32) + b_in[m : m + 1, :]
        ).astype(jnp.bfloat16)
        second = jnp.tanh(
            jnp.dot(first, w_hid[m], preferred_element_type=jnp.float32) + b_hid[m : m + 1, :]
        ).astype(jnp.bfloat16)
        outputs = lax.dot_general(
            w_out[m], second, (((1,), (1,)), ((), ())), preferred_element_type=jnp.float32
        )
        electro.append(outputs[0:1])
        raw.append(outputs[1:2])
    for copy in late:
        copy.wait()
    species = species_ref[0]
    slot_iota = lax.broadcasted_iota(jnp.int32, (1, slots), 1)
    occupancy = (slot_iota < counts_ref[0, 0]).astype(jnp.float32)
    shifts = choose(species, (-0.8, 0.4, 1.2, -0.3))
    raw = jnp.concatenate(raw, axis=0)
    hardness = 2.5 + (jnp.maximum(raw, 0.0) + jnp.log1p(jnp.exp(-jnp.abs(raw))))
    right = -(jnp.concatenate(electro, axis=0) + shifts) * occupancy
    atoms = jnp.concatenate(
        [pos_ref[0, 0], pos_ref[1, 0], pos_ref[2, 0], species.astype(jnp.float32), occupancy]
        + [jnp.zeros((1, slots), jnp.float32)] * (ROWS - FULL - 1),
        axis=0,
    )
    for peer in range(out_ref.shape[0]):
        out_ref[peer, 0:HARD, :] = right
        out_ref[peer, HARD:PLACE, :] = hardness
        out_ref[peer, PLACE:ROWS, :] = atoms


def thirds(values):
    high = values.astype(jnp.bfloat16).astype(jnp.float32)
    rest = values - high
    middle = rest.astype(jnp.bfloat16).astype(jnp.float32)
    return high, middle, rest - middle


def pair_features(places, kind):
    one, zero = jnp.ones_like(kind), jnp.zeros_like(kind)
    near, far = [], []
    for place in places:
        h, m, l = thirds(place)
        near += [h, h, m, m, h, l]
        far += [-2.0 * v for v in (h, m, h, m, l, h)]
    norm = list(thirds(sum(place * place for place in places)))
    near += norm + [one] * 3
    far += [one] * 3 + norm
    count = len(WIDTHS)
    near += [(kind == k).astype(jnp.float32) for k in range(count)] * 3
    pairs = [
        choose(kind, [(WIDTHS[k] ** 2 + other**2) ** -0.5 for other in WIDTHS])
        for k in range(count)
    ]
    far += [part for third in zip(*map(thirds, pairs)) for part in third]
    rest = [zero] * (FEATURES - len(near))
    return near + rest, far + rest


def pair_block(products, first_row, own):
    slots = products.shape[1] // 2
    capped = jnp.minimum(products[:, 0:slots], 1.0)
    inv = products[:, slots:]
    left = 1.0 - capped
    y = (capped + 1e-06) * (inv * inv) - ERF_CENTRE
    value = jnp.full_like(y, 0.005 * ERF_SERIES[-1])
    for term in ERF_SERIES[-2::-1]:
        value = value * y + 0.005 * term
    value = value * ((left * inv) * (left * left))
    if own:
        i = lax.broadcasted_iota(jnp.int32, value.shape, 0) + first_row
        j = lax.broadcasted_iota(jnp.int32, value.shape, 1)
        value = jnp.where(i == j, 0.0, value)
    return value


def times(vectors, block):
    return jnp.dot(vectors, block, preferred_element_type=jnp.float32)


def times_t(vectors, block):
    return lax.dot_general(
        vectors, block, (((1,), (1,)), ((), ())), preferred_element_type=jnp.float32
    )


def halves(values):
    high = values.astype(jnp.bfloat16)
    return high, (values - high.astype(jnp.float32)).astype(jnp.bfloat16)


def solve_kernel(grid, slab_ref, out_ref, feats, near, far, vecs, sums, resid, resid_half, blocks):
    rows, columns = grid
    cells, _, slots = slab_ref.shape
    members = HARD

    centres = (rows / 2, columns / 2, 0.5)
    rows_of = pair_features(
        [slab_ref[:, PLACE + k, :] - centres[k] for k in range(3)], slab_ref[:, KIND, :]
    )
    for k, row in enumerate(rows_of[0] + rows_of[1]):
        feats[:, k, :] = row
    blank = jnp.zeros((SQUARE, slots), jnp.float32)
    for c in range(cells):
        near[c] = feats[c, 0:FEATURES, :].T.astype(jnp.bfloat16)
        apart = jnp.concatenate([feats[c, FEATURES : FEATURES + SQUARE, :], blank], axis=0)
        spread = jnp.concatenate([blank, feats[c, FEATURES + SQUARE :, :]], axis=0)
        far[c] = jnp.concatenate([apart, spread], axis=1).astype(jnp.bfloat16)
        high, low = halves(slab_ref[c, 0:HARD, :])
        full = slab_ref[c, FULL : FULL + 1, :]
        row = lax.broadcasted_iota(jnp.int32, (16, slots), 0)
        lines = [high.astype(jnp.float32), low.astype(jnp.float32), jnp.where(row == 0, full, 0.0)]
        lines = jnp.concatenate(lines, axis=0).astype(jnp.bfloat16)
        vecs[c] = jnp.concatenate([lines, lines], axis=1)
        sums[c] = jnp.zeros_like(sums[c])

    def row_pairs(a, last):
        pairs = []
        for da, db in OFFSETS[:2] if last else OFFSETS:
            for column in range(max(0, -db), columns - max(0, db)):
                c = a * columns + column
                place = a * (5 * columns - 3) + len(pairs)
                pairs.append((c, c + da * columns + db, place, da == db == 0))
        return pairs

    def over_rows(handle, carry):
        for a in range(rows):
            carry = handle(row_pairs(a, a == rows - 1), carry)
        return carry

    def build(pairs, carry):
        for c, d, place, own in pairs:
            for first_row in range(0, slots, CHUNK):
                products = times(near[c, first_row : first_row + CHUNK, :], far[d])
                high, low = halves(pair_block(products, first_row, own))
                blocks[place, first_row : first_row + CHUNK, :] = high
                blocks[place, slots + first_row : slots + first_row + CHUNK, :] = low
        return carry

    def first_pass(pairs, carry):
        terms = []
        for c, d, place, own in pairs:
            block = blocks[place]
            terms.append((d, times(vecs[c], block)))
            if not own:
                image = times_t(vecs[d, :, 0:slots], block)
                terms.append((c, image[:, 0:slots] + image[:, slots:]))
        for cell, term in terms:
            sums[cell] += term
        return carry

    over_rows(build, 0)
    over_rows(first_pass, 0)

    def applied(c):
        hard = slab_ref[c, HARD:PLACE, :]
        full = slab_ref[c, FULL : FULL + 1, :]
        right = slab_ref[c, 0:HARD, :]
        coupled = sums[c]
        image_s = hard * right + full * (coupled[0:8] + coupled[8:16])
        image_u = full * (hard + coupled[16:17])
        return hard, full, right, image_s, image_u

    shape = (members, slots)
    norm_s, prod_s, prod_u, total_s = (jnp.zeros(shape, jnp.float32) for _ in range(4))
    norm_u = jnp.zeros((1, slots), jnp.float32)
    for c in range(cells):
        hard, full, right, image_s, image_u = applied(c)
        norm_s += right * right
        norm_u += full * full
        prod_s += right * image_s
        prod_u += full * image_u
        total_s += right

    def over(values):
        return jnp.sum(values, axis=1, keepdims=True)

    both = lambda s, u: jnp.concatenate([s, jnp.broadcast_to(u, s.shape)], axis=0)
    norm0 = both(over(norm_s), over(norm_u))
    total0 = both(over(total_s), over(norm_u))
    alpha0 = norm0 / both(over(prod_s), over(prod_u))

    norm1, prod1, total1 = (jnp.zeros((2 * members, slots), jnp.float32) for _ in range(3))
    for c in range(cells):
        hard, full, right, image_s, image_u = applied(c)
        left = both(right, full) - alpha0 * jnp.concatenate([image_s, image_u], axis=0)
        resid[c] = left
        high, low = halves(left)
        lines = jnp.concatenate([high, low], axis=0)
        resid_half[c] = jnp.concatenate([lines, lines], axis=1)
        square = left * left
        norm1 += square
        prod1 += jnp.concatenate([hard, hard], axis=0) * square
        total1 += left

    def second_pass(pairs, carry):
        for c, d, place, own in pairs:
            image = times(resid_half[c], blocks[place])
            part = (image[0:16] + image[16:32]) * resid[d]
            carry = carry + (part if own else 2.0 * part)
        return carry

    prod1 = over_rows(second_pass, prod1)

    norm1, prod1, total1 = over(norm1), over(prod1), over(total1)
    momentum = norm1 / norm0
    alpha1 = norm1 / (prod1 - momentum * norm1 / alpha0)
    weight0 = alpha0 + alpha1 * momentum
    totals = weight0 * total0 + alpha1 * total1
    multiplier = totals[0:members] / totals[members:]
    mine = lax.axis_index("cell") * columns + lax.axis_index("sub")
    right = both(slab_ref[mine, 0:HARD, :], slab_ref[mine, FULL : FULL + 1, :])
    answer = weight0 * right + alpha1 * resid[mine]
    out_ref[...] = answer[0:members] - multiplier * answer[members:]


def solve_only(slabs):
    rows, columns = lax.axis_size("cell"), lax.axis_size("sub")
    cells, _, slots = slabs.shape
    vmem = pl.BlockSpec(memory_space=pltpu.VMEM)
    blocks = sum(pair_counts(rows, columns))
    return pl.pallas_call(
        lambda *refs: solve_kernel((rows, columns), *refs),
        out_shape=jax.ShapeDtypeStruct((HARD, slots), jnp.float32),
        in_specs=[vmem],
        out_specs=vmem,
        scratch_shapes=[
            pltpu.VMEM((cells, 2 * FEATURES, slots), jnp.float32),
            pltpu.VMEM((cells, slots, FEATURES), jnp.bfloat16),
            pltpu.VMEM((cells, FEATURES, 2 * slots), jnp.bfloat16),
            pltpu.VMEM((cells, 32, 2 * slots), jnp.bfloat16),
            pltpu.VMEM((cells, 32, slots), jnp.float32),
            pltpu.VMEM((cells, 16, slots), jnp.float32),
            pltpu.VMEM((cells, 32, 2 * slots), jnp.bfloat16),
            pltpu.VMEM((blocks, 2 * slots, slots), jnp.bfloat16),
        ],
        compiler_params=pltpu.CompilerParams(vmem_limit_bytes=32 << 20),
        name="solve",
    )(slabs)


def gathered(descriptors, positions, species, counts, w_in, b_in, w_hid, b_hid, w_out):
    rows, columns = lax.axis_size("cell"), lax.axis_size("sub")
    cells, slots, members = rows * columns, descriptors.shape[2], w_in.shape[0]
    vmem = pl.BlockSpec(memory_space=pltpu.VMEM)
    args = (
        descriptors.reshape(slots, -1), positions, species, counts, w_in, b_in, w_hid, b_hid, w_out
    )
    landed = [
        (pltpu.SMEM if arg is counts else pltpu.VMEM)(arg.shape, arg.dtype) for arg in args
    ]
    slabs = pl.pallas_call(
        slab_kernel,
        out_shape=jax.ShapeDtypeStruct((cells, ROWS, slots), jnp.float32),
        in_specs=[pl.BlockSpec(memory_space=pltpu.HBM)] * len(args),
        out_specs=vmem,
        scratch_shapes=landed + [pltpu.SemaphoreType.DMA((7 + 2 * members,))],
        compiler_params=pltpu.CompilerParams(vmem_limit_bytes=60 << 20),
        name="slab",
    )(*args)
    slabs = lax.all_to_all(slabs, ("cell", "sub"), 0, 0, tiled=True)
    charges = solve_only(slabs)
    return charges.reshape(members, 1, 1, slots)


def extended_2(shard, sides, width):
    for axis, dim in sides:
        size, length = (lax.axis_size(axis), shard.shape[dim])
        up = [(i, (i + 1) % size) for i in range(size - 1)]
        down = [(j, i) for i, j in up]
        last = lax.slice_in_dim(shard, length - width, length, axis=dim)
        leading = lax.slice_in_dim(shard, 0, width, axis=dim)
        before = lax.ppermute(last, axis, up)
        after = lax.ppermute(leading, axis, down)
        shard = jnp.concatenate([before, shard, after], axis=dim)
    return shard


def lookup(species, entries):
    choices_table = jnp.array(entries, jnp.float32)
    kinds = jnp.arange(4, dtype=jnp.int32)
    return jnp.sum((species[..., None] == kinds).astype(jnp.float32) * choices_table, axis=-1)


def coupling(own_atoms, far_atoms, self_cell):
    delta_a = own_atoms[0][..., :, None] - far_atoms[0][..., None, :]
    delta_b = own_atoms[1][..., :, None] - far_atoms[1][..., None, :]
    delta_c = own_atoms[2][..., :, None] - far_atoms[2][..., None, :]
    distance_sq = delta_a * delta_a + delta_b * delta_b + delta_c * delta_c
    radius = jnp.sqrt(distance_sq + 1e-06)
    pair_width = jnp.sqrt(own_atoms[3][..., :, None] ** 2 + far_atoms[3][..., None, :] ** 2)
    smooth_cut = (1.0 - jnp.minimum(distance_sq, 1.0)) ** 3
    kernel = 0.005 * smooth_cut * jax.scipy.special.erf(radius / pair_width) / radius
    kernel = kernel * own_atoms[4][..., :, None] * far_atoms[4][..., None, :]
    if self_cell:
        kernel = kernel * (1.0 - jnp.eye(kernel.shape[-1], dtype=jnp.float32))
    return kernel


def committee(flat_rows, w_in, b_in, w_hid, b_hid, w_out):

    def member_fn(weights):
        first_w, first_b, second_w, second_b, last_w = weights
        first = jnp.tanh(
            jnp.dot(flat_rows, first_w, preferred_element_type=jnp.float32) + first_b
        ).astype(jnp.bfloat16)
        second = jnp.tanh(
            jnp.dot(first, second_w, preferred_element_type=jnp.float32) + second_b
        ).astype(jnp.bfloat16)
        return jnp.dot(second, last_w.T, preferred_element_type=jnp.float32).T

    return lax.map(member_fn, (w_in, b_in, w_hid, b_hid, w_out))


def expand(values):
    return values[:, None, None, None]


def extend(vectors):
    return extended_2(vectors, (("cell", 1), ("sub", 2)), 1)


def two_products(residual, image_vec):
    return lax.psum(
        (
            jnp.sum(residual * residual, axis=(1, 2, 3)),
            jnp.sum(residual * image_vec, axis=(1, 2, 3)),
        ),
        ("cell", "sub"),
    )


def body(descriptors, positions, species, counts, w_in, b_in, w_hid, b_hid, w_out):
    rows_a, rows_b, slot_count, features = descriptors.shape
    members = w_in.shape[0]
    slot_iota = lax.broadcasted_iota(jnp.int32, (rows_a, rows_b, slot_count), 2)
    occupancy = (slot_iota < counts[:, :, None]).astype(jnp.float32)
    widths = lookup(species, (0.3, 0.4, 0.5, 0.35))
    shifts = lookup(species, (-0.8, 0.4, 1.2, -0.3))
    atom_data = jnp.stack([positions[0], positions[1], positions[2], widths, occupancy])
    extended = extended_2(atom_data, (("cell", 1), ("sub", 2)), 1)
    outputs = committee(descriptors.reshape(-1, features), w_in, b_in, w_hid, b_hid, w_out)
    electro = outputs[:, 0].reshape(members, rows_a, rows_b, slot_count) + shifts
    hardness = 2.5 + jax.nn.softplus(outputs[:, 1]).reshape(members, rows_a, rows_b, slot_count)
    right_side = jnp.concatenate([-electro * occupancy, jnp.broadcast_to(occupancy, electro.shape)])
    diagonal = jnp.concatenate([hardness, hardness])
    offsets = [(row_step, col_step) for row_step in (-1, 0, 1) for col_step in (-1, 0, 1)]

    def neighbours(grown, row_step, col_step):
        return grown[:, 1 + row_step : 1 + row_step + rows_a, 1 + col_step : 1 + col_step + rows_b]

    def block_for(row_step, col_step):
        return coupling(
            atom_data, neighbours(extended, row_step, col_step), row_step == 0 and col_step == 0
        )

    def operate(vectors):
        grown = extend(vectors)
        summed = diagonal * vectors
        for offset_number in range(9):
            row_step, col_step = offsets[offset_number]
            tile_block = block_for(row_step, col_step)
            summed = summed + jnp.einsum(
                "abij,rabj->rabi",
                tile_block,
                neighbours(grown, row_step, col_step),
                precision=lax.Precision.HIGHEST,
            )
        return summed

    solution = jnp.zeros_like(right_side)
    residual = right_side
    image_vec = operate(residual)
    norm_now, product = two_products(residual, image_vec)
    step_size = norm_now / product
    direction = residual
    along = image_vec
    for iteration in range(ITERS):
        solution = solution + expand(step_size) * direction
        residual = residual - expand(step_size) * along
        if iteration + 1 < ITERS:
            image_vec = operate(residual)
            norm_next, product = two_products(residual, image_vec)
            momentum = norm_next / norm_now
            step_size = norm_next / (product - momentum * norm_next / step_size)
            direction = residual + expand(momentum) * direction
            along = image_vec + expand(momentum) * along
            norm_now = norm_next
    source_part = solution[:members]
    unit_part = solution[members:]
    source_total, unit_total = lax.psum(
        (jnp.sum(source_part, axis=(1, 2, 3)), jnp.sum(unit_part, axis=(1, 2, 3))), ("cell", "sub")
    )
    multiplier = source_total / unit_total
    return source_part - expand(multiplier) * unit_part


def solution(mesh):
    placed = (
        P(("rep", "cell"), "sub", None, None),
        P(None, ("rep", "cell"), "sub", None),
        P(("rep", "cell"), "sub", None),
        P(("rep", "cell"), "sub"),
        P(),
        P(),
        P(),
        P(),
        P(),
    )
    rows, columns = mesh.shape["cell"], mesh.shape["sub"]
    return jax.shard_map(
        gathered if sum(pair_counts(rows, columns)) <= MOST_BLOCKS else body,
        mesh=mesh,
        in_specs=placed,
        out_specs=P(None, ("rep", "cell"), "sub", None),
        check_vma=False,
    )
```

```python
import jax
import jax.numpy as jnp
from jax import lax
from jax.experimental import pallas as pl
from jax.experimental.pallas import tpu as pltpu
from jax.sharding import PartitionSpec as P

ITERS = 2

ERF_SERIES = (
    1.1283791338788207,
    -0.37612471240078243,
    0.11282450088960652,
    -0.026825992168818515,
    0.005164800720113156,
    -0.0008061635856414364,
    9.67168369375208e-05,
    -7.756955478859171e-06,
    3.007955257374649e-07,
)

WIDTHS = (0.3, 0.4, 0.5, 0.35)

HARD, PLACE, KIND, FULL, ROWS = 8, 16, 19, 20, 24
SQUARE, FEATURES = 24, 48
OFFSETS = ((0, 0), (0, 1), (1, -1), (1, 0), (1, 1))
MOST_BLOCKS = 128
CHUNK = 128
LAG = 12
GROUP = 8


def pair_counts(rows, cols):
    return [(rows - da) * (cols - abs(db)) for da, db in OFFSETS]


def choose(species, entries):
    value = jnp.full(species.shape, entries[3], jnp.float32)
    for kind in (2, 1, 0):
        value = jnp.where(species == kind, entries[kind], value)
    return value


def slab_kernel(*refs):
    sources, out_ref, landed, done = refs[:9], refs[9], refs[10:19], refs[19]
    members = sources[4].shape[0]
    copies = []

    def fetch(source, target):
        copy = pltpu.make_async_copy(source, target, done.at[len(copies)])
        copy.start()
        copies.append(copy)
        return copy

    desc_ref, pos_ref, species_ref, counts_ref, w_in, b_in, w_hid, b_hid, w_out = landed
    early = [fetch(sources[k], landed[k]) for k in (0, 5, 4)]
    middle = [fetch(sources[k], landed[k]) for k in (6, 7, 8)]
    late = [fetch(sources[k], landed[k]) for k in (1, 2, 3)]
    for copy in early:
        copy.wait()
    rows = desc_ref[...]
    slots = rows.shape[0]
    firsts, electro, raw = [], [], []
    for m in range(members):
        summed = jnp.dot(rows, w_in[m], preferred_element_type=jnp.float32) + b_in[m : m + 1, :]
        firsts.append(jnp.tanh(summed).astype(jnp.bfloat16))
    for copy in middle:
        copy.wait()
    for start in range(0, members, GROUP):
        group = range(start, start + GROUP)
        seconds = []
        for m in group:
            summed = jnp.dot(firsts[m], w_hid[m], preferred_element_type=jnp.float32)
            seconds.append(jnp.tanh(summed + b_hid[m : m + 1, :]).astype(jnp.bfloat16))
        for m in group:
            outputs = lax.dot_general(
                w_out[m],
                seconds[m - start],
                (((1,), (1,)), ((), ())),
                preferred_element_type=jnp.float32,
            )
            electro.append(outputs[0:1])
            raw.append(outputs[1:2])
    for copy in late:
        copy.wait()
    species = species_ref[0]
    slot_iota = lax.broadcasted_iota(jnp.int32, (1, slots), 1)
    occupancy = (slot_iota < counts_ref[0, 0]).astype(jnp.float32)
    shifts = choose(species, (-0.8, 0.4, 1.2, -0.3))
    raw = jnp.concatenate(raw, axis=0)
    hardness = 2.5 + (jnp.maximum(raw, 0.0) + jnp.log1p(jnp.exp(-jnp.abs(raw))))
    right = -(jnp.concatenate(electro, axis=0) + shifts) * occupancy
    atoms = jnp.concatenate(
        [pos_ref[0, 0], pos_ref[1, 0], pos_ref[2, 0], species.astype(jnp.float32), occupancy]
        + [jnp.zeros((1, slots), jnp.float32)] * (ROWS - FULL - 1),
        axis=0,
    )
    for peer in range(out_ref.shape[0]):
        out_ref[peer, 0:HARD, :] = right
        out_ref[peer, HARD:PLACE, :] = hardness
        out_ref[peer, PLACE:ROWS, :] = atoms


def thirds(values):
    high = values.astype(jnp.bfloat16).astype(jnp.float32)
    rest = values - high
    middle = rest.astype(jnp.bfloat16).astype(jnp.float32)
    return high, middle, rest - middle


def pair_features(places, kind):
    one, zero = jnp.ones_like(kind), jnp.zeros_like(kind)
    near, far = [], []
    for place in places:
        h, m, l = thirds(place)
        near += [h, h, m, m, h, l]
        far += [2.0 * v for v in (h, m, h, m, l, h)]
    norm = sum(place * place for place in places)
    near += [*thirds(norm), one, one, one]
    far += [-one, -one, -one, *thirds(1.0 - norm)]
    count = len(WIDTHS)
    near += [(kind == k).astype(jnp.float32) for k in range(count)] * 3
    pairs = [
        choose(kind, [(WIDTHS[k] ** 2 + other**2) ** -0.5 for other in WIDTHS])
        for k in range(count)
    ]
    far += [part for third in zip(*map(thirds, pairs)) for part in third]
    rest = [zero] * (FEATURES - len(near))
    return near + rest, far + rest


def pair_block(products, first_row, own):
    slots = products.shape[1] // 2
    left = jnp.maximum(products[:, 0:slots], 0.0)
    inv = products[:, slots:]
    y = (1.000001 - left) * (inv * inv)
    value = jnp.full_like(y, 0.005 * ERF_SERIES[-1])
    for term in ERF_SERIES[-2::-1]:
        value = value * y + 0.005 * term
    value = value * ((left * inv) * (left * left))
    if own:
        i = lax.broadcasted_iota(jnp.int32, value.shape, 0) + first_row
        j = lax.broadcasted_iota(jnp.int32, value.shape, 1)
        value = jnp.where(i == j, 0.0, value)
    return value


def times(vectors, block):
    return jnp.dot(vectors, block, preferred_element_type=jnp.float32)


def times_t(vectors, block):
    return lax.dot_general(
        vectors, block, (((1,), (1,)), ((), ())), preferred_element_type=jnp.float32
    )


def halves(values):
    high = values.astype(jnp.bfloat16)
    return high, (values - high.astype(jnp.float32)).astype(jnp.bfloat16)


def solve_kernel(grid, slab_ref, out_ref, feats, near, far, vecs, sums, resid, resid_half, blocks):
    rows, columns = grid
    cells, _, slots = slab_ref.shape
    members = HARD

    centres = (rows / 2, columns / 2, 0.5)
    rows_of = pair_features(
        [slab_ref[:, PLACE + k, :] - centres[k] for k in range(3)], slab_ref[:, KIND, :]
    )
    for k, row in enumerate(rows_of[0] + rows_of[1]):
        feats[:, k, :] = row
    blank = jnp.zeros((SQUARE, slots), jnp.float32)
    for c in range(cells):
        near[c] = feats[c, 0:FEATURES, :].T.astype(jnp.bfloat16)
        apart = jnp.concatenate([feats[c, FEATURES : FEATURES + SQUARE, :], blank], axis=0)
        spread = jnp.concatenate([blank, feats[c, FEATURES + SQUARE :, :]], axis=0)
        far[c] = jnp.concatenate([apart, spread], axis=1).astype(jnp.bfloat16)
        high, low = halves(slab_ref[c, 0:HARD, :])
        full = slab_ref[c, FULL : FULL + 1, :]
        row = lax.broadcasted_iota(jnp.int32, (16, slots), 0)
        lines = [high.astype(jnp.float32), low.astype(jnp.float32), jnp.where(row == 0, full, 0.0)]
        lines = jnp.concatenate(lines, axis=0).astype(jnp.bfloat16)
        vecs[c] = jnp.concatenate([lines, lines], axis=1)
        sums[c] = jnp.zeros_like(sums[c])

    def row_pairs(a, last):
        pairs = []
        for da, db in OFFSETS[:2] if last else OFFSETS:
            for column in range(max(0, -db), columns - max(0, db)):
                c = a * columns + column
                place = a * (5 * columns - 3) + len(pairs)
                pairs.append((c, c + da * columns + db, place, da == db == 0))
        return pairs

    def over_rows(handle, carry):
        for a in range(rows):
            carry = handle(row_pairs(a, a == rows - 1), carry)
        return carry

    def build(pairs, carry):
        for c, d, place, own in pairs:
            for first_row in range(0, slots, CHUNK):
                products = times(near[c, first_row : first_row + CHUNK, :], far[d])
                high, low = halves(pair_block(products, first_row, own))
                blocks[place, first_row : first_row + CHUNK, :] = high
                blocks[place, slots + first_row : slots + first_row + CHUNK, :] = low
        return carry

    def first_pass(pairs, carry):
        terms = []
        for c, d, place, own in pairs:
            block = blocks[place]
            terms.append((d, times(vecs[c], block)))
            if not own:
                image = times_t(vecs[d, :, 0:slots], block)
                terms.append((c, image[:, 0:slots] + image[:, slots:]))
        for cell, term in terms:
            sums[cell] += term
        return carry

    every = over_rows(lambda pairs, kept: kept + pairs, [])
    for i in range(len(every) + LAG):
        if i >= LAG:
            first_pass(every[i - LAG : i - LAG + 1], 0)
        build(every[i : i + 1], 0)

    def applied(c):
        hard = slab_ref[c, HARD:PLACE, :]
        full = slab_ref[c, FULL : FULL + 1, :]
        right = slab_ref[c, 0:HARD, :]
        coupled = sums[c]
        image_s = hard * right + full * (coupled[0:8] + coupled[8:16])
        image_u = full * (hard + coupled[16:17])
        return hard, full, right, image_s, image_u

    shape = (members, slots)
    norm_s, prod_s, prod_u, total_s = (jnp.zeros(shape, jnp.float32) for _ in range(4))
    norm_u = jnp.zeros((1, slots), jnp.float32)
    for c in range(cells):
        hard, full, right, image_s, image_u = applied(c)
        norm_s += right * right
        norm_u += full * full
        prod_s += right * image_s
        prod_u += full * image_u
        total_s += right

    def over(values):
        return jnp.sum(values, axis=1, keepdims=True)

    both = lambda s, u: jnp.concatenate([s, jnp.broadcast_to(u, s.shape)], axis=0)
    norm0 = both(over(norm_s), over(norm_u))
    total0 = both(over(total_s), over(norm_u))
    alpha0 = norm0 / both(over(prod_s), over(prod_u))

    norm1, prod1, total1 = (jnp.zeros((2 * members, slots), jnp.float32) for _ in range(3))
    for c in range(cells):
        hard, full, right, image_s, image_u = applied(c)
        left = both(right, full) - alpha0 * jnp.concatenate([image_s, image_u], axis=0)
        resid[c] = left
        high, low = halves(left)
        lines = jnp.concatenate([high, low], axis=0)
        resid_half[c] = jnp.concatenate([lines, lines], axis=1)
        square = left * left
        norm1 += square
        prod1 += jnp.concatenate([hard, hard], axis=0) * square
        total1 += left

    def second_pass(pairs, carry):
        for c, d, place, own in pairs:
            image = times(resid_half[c], blocks[place])
            part = (image[0:16] + image[16:32]) * resid[d]
            carry = carry + (part if own else 2.0 * part)
        return carry

    prod1 = over_rows(second_pass, prod1)

    norm1, prod1, total1 = over(norm1), over(prod1), over(total1)
    momentum = norm1 / norm0
    alpha1 = norm1 / (prod1 - momentum * norm1 / alpha0)
    weight0 = alpha0 + alpha1 * momentum
    totals = weight0 * total0 + alpha1 * total1
    multiplier = totals[0:members] / totals[members:]
    mine = lax.axis_index("cell") * columns + lax.axis_index("sub")
    right = both(slab_ref[mine, 0:HARD, :], slab_ref[mine, FULL : FULL + 1, :])
    answer = weight0 * right + alpha1 * resid[mine]
    out_ref[...] = answer[0:members] - multiplier * answer[members:]


def solve_only(slabs):
    rows, columns = lax.axis_size("cell"), lax.axis_size("sub")
    cells, _, slots = slabs.shape
    vmem = pl.BlockSpec(memory_space=pltpu.VMEM)
    blocks = sum(pair_counts(rows, columns))
    return pl.pallas_call(
        lambda *refs: solve_kernel((rows, columns), *refs),
        out_shape=jax.ShapeDtypeStruct((HARD, slots), jnp.float32),
        in_specs=[vmem],
        out_specs=vmem,
        scratch_shapes=[
            pltpu.VMEM((cells, 2 * FEATURES, slots), jnp.float32),
            pltpu.VMEM((cells, slots, FEATURES), jnp.bfloat16),
            pltpu.VMEM((cells, FEATURES, 2 * slots), jnp.bfloat16),
            pltpu.VMEM((cells, 32, 2 * slots), jnp.bfloat16),
            pltpu.VMEM((cells, 32, slots), jnp.float32),
            pltpu.VMEM((cells, 16, slots), jnp.float32),
            pltpu.VMEM((cells, 32, 2 * slots), jnp.bfloat16),
            pltpu.VMEM((blocks, 2 * slots, slots), jnp.bfloat16),
        ],
        compiler_params=pltpu.CompilerParams(vmem_limit_bytes=32 << 20),
        name="solve",
    )(slabs)


def gathered(descriptors, positions, species, counts, w_in, b_in, w_hid, b_hid, w_out):
    rows, columns = lax.axis_size("cell"), lax.axis_size("sub")
    cells, slots, members = rows * columns, descriptors.shape[2], w_in.shape[0]
    vmem = pl.BlockSpec(memory_space=pltpu.VMEM)
    args = (
        descriptors.reshape(slots, -1), positions, species, counts, w_in, b_in, w_hid, b_hid, w_out
    )
    landed = [
        (pltpu.SMEM if arg is counts else pltpu.VMEM)(arg.shape, arg.dtype) for arg in args
    ]
    slabs = pl.pallas_call(
        slab_kernel,
        out_shape=jax.ShapeDtypeStruct((cells, ROWS, slots), jnp.float32),
        in_specs=[pl.BlockSpec(memory_space=pltpu.HBM)] * len(args),
        out_specs=vmem,
        scratch_shapes=landed + [pltpu.SemaphoreType.DMA((len(args),))],
        compiler_params=pltpu.CompilerParams(vmem_limit_bytes=60 << 20),
        name="slab",
    )(*args)
    slabs = lax.all_to_all(slabs, ("cell", "sub"), 0, 0, tiled=True)
    charges = solve_only(slabs)
    return charges.reshape(members, 1, 1, slots)


def extended_2(shard, sides, width):
    for axis, dim in sides:
        size, length = (lax.axis_size(axis), shard.shape[dim])
        up = [(i, (i + 1) % size) for i in range(size - 1)]
        down = [(j, i) for i, j in up]
        last = lax.slice_in_dim(shard, length - width, length, axis=dim)
        leading = lax.slice_in_dim(shard, 0, width, axis=dim)
        before = lax.ppermute(last, axis, up)
        after = lax.ppermute(leading, axis, down)
        shard = jnp.concatenate([before, shard, after], axis=dim)
    return shard


def lookup(species, entries):
    choices_table = jnp.array(entries, jnp.float32)
    kinds = jnp.arange(4, dtype=jnp.int32)
    return jnp.sum((species[..., None] == kinds).astype(jnp.float32) * choices_table, axis=-1)


def coupling(own_atoms, far_atoms, self_cell):
    delta_a = own_atoms[0][..., :, None] - far_atoms[0][..., None, :]
    delta_b = own_atoms[1][..., :, None] - far_atoms[1][..., None, :]
    delta_c = own_atoms[2][..., :, None] - far_atoms[2][..., None, :]
    distance_sq = delta_a * delta_a + delta_b * delta_b + delta_c * delta_c
    radius = jnp.sqrt(distance_sq + 1e-06)
    pair_width = jnp.sqrt(own_atoms[3][..., :, None] ** 2 + far_atoms[3][..., None, :] ** 2)
    smooth_cut = (1.0 - jnp.minimum(distance_sq, 1.0)) ** 3
    kernel = 0.005 * smooth_cut * jax.scipy.special.erf(radius / pair_width) / radius
    kernel = kernel * own_atoms[4][..., :, None] * far_atoms[4][..., None, :]
    if self_cell:
        kernel = kernel * (1.0 - jnp.eye(kernel.shape[-1], dtype=jnp.float32))
    return kernel


def committee(flat_rows, w_in, b_in, w_hid, b_hid, w_out):

    def member_fn(weights):
        first_w, first_b, second_w, second_b, last_w = weights
        first = jnp.tanh(
            jnp.dot(flat_rows, first_w, preferred_element_type=jnp.float32) + first_b
        ).astype(jnp.bfloat16)
        second = jnp.tanh(
            jnp.dot(first, second_w, preferred_element_type=jnp.float32) + second_b
        ).astype(jnp.bfloat16)
        return jnp.dot(second, last_w.T, preferred_element_type=jnp.float32).T

    return lax.map(member_fn, (w_in, b_in, w_hid, b_hid, w_out))


def expand(values):
    return values[:, None, None, None]


def extend(vectors):
    return extended_2(vectors, (("cell", 1), ("sub", 2)), 1)


def two_products(residual, image_vec):
    return lax.psum(
        (
            jnp.sum(residual * residual, axis=(1, 2, 3)),
            jnp.sum(residual * image_vec, axis=(1, 2, 3)),
        ),
        ("cell", "sub"),
    )


def body(descriptors, positions, species, counts, w_in, b_in, w_hid, b_hid, w_out):
    rows_a, rows_b, slot_count, features = descriptors.shape
    members = w_in.shape[0]
    slot_iota = lax.broadcasted_iota(jnp.int32, (rows_a, rows_b, slot_count), 2)
    occupancy = (slot_iota < counts[:, :, None]).astype(jnp.float32)
    widths = lookup(species, (0.3, 0.4, 0.5, 0.35))
    shifts = lookup(species, (-0.8, 0.4, 1.2, -0.3))
    atom_data = jnp.stack([positions[0], positions[1], positions[2], widths, occupancy])
    extended = extended_2(atom_data, (("cell", 1), ("sub", 2)), 1)
    outputs = committee(descriptors.reshape(-1, features), w_in, b_in, w_hid, b_hid, w_out)
    electro = outputs[:, 0].reshape(members, rows_a, rows_b, slot_count) + shifts
    hardness = 2.5 + jax.nn.softplus(outputs[:, 1]).reshape(members, rows_a, rows_b, slot_count)
    right_side = jnp.concatenate([-electro * occupancy, jnp.broadcast_to(occupancy, electro.shape)])
    diagonal = jnp.concatenate([hardness, hardness])
    offsets = [(row_step, col_step) for row_step in (-1, 0, 1) for col_step in (-1, 0, 1)]

    def neighbours(grown, row_step, col_step):
        return grown[:, 1 + row_step : 1 + row_step + rows_a, 1 + col_step : 1 + col_step + rows_b]

    def block_for(row_step, col_step):
        return coupling(
            atom_data, neighbours(extended, row_step, col_step), row_step == 0 and col_step == 0
        )

    def operate(vectors):
        grown = extend(vectors)
        summed = diagonal * vectors
        for offset_number in range(9):
            row_step, col_step = offsets[offset_number]
            tile_block = block_for(row_step, col_step)
            summed = summed + jnp.einsum(
                "abij,rabj->rabi",
                tile_block,
                neighbours(grown, row_step, col_step),
                precision=lax.Precision.HIGHEST,
            )
        return summed

    solution = jnp.zeros_like(right_side)
    residual = right_side
    image_vec = operate(residual)
    norm_now, product = two_products(residual, image_vec)
    step_size = norm_now / product
    direction = residual
    along = image_vec
    for iteration in range(ITERS):
        solution = solution + expand(step_size) * direction
        residual = residual - expand(step_size) * along
        if iteration + 1 < ITERS:
            image_vec = operate(residual)
            norm_next, product = two_products(residual, image_vec)
            momentum = norm_next / norm_now
            step_size = norm_next / (product - momentum * norm_next / step_size)
            direction = residual + expand(momentum) * direction
            along = image_vec + expand(momentum) * along
            norm_now = norm_next
    source_part = solution[:members]
    unit_part = solution[members:]
    source_total, unit_total = lax.psum(
        (jnp.sum(source_part, axis=(1, 2, 3)), jnp.sum(unit_part, axis=(1, 2, 3))), ("cell", "sub")
    )
    multiplier = source_total / unit_total
    return source_part - expand(multiplier) * unit_part


def solution(mesh):
    placed = (
        P(("rep", "cell"), "sub", None, None),
        P(None, ("rep", "cell"), "sub", None),
        P(("rep", "cell"), "sub", None),
        P(("rep", "cell"), "sub"),
        P(),
        P(),
        P(),
        P(),
        P(),
    )
    rows, columns = mesh.shape["cell"], mesh.shape["sub"]
    return jax.shard_map(
        gathered if sum(pair_counts(rows, columns)) <= MOST_BLOCKS else body,
        mesh=mesh,
        in_specs=placed,
        out_specs=P(None, ("rep", "cell"), "sub", None),
        check_vma=False,
    )
```

```python
import jax
import jax.numpy as jnp
from jax import lax
from jax.experimental import pallas as pl
from jax.experimental.pallas import tpu as pltpu
from jax.sharding import PartitionSpec as P

ITERS = 2

ERF_SERIES = (
    1.1283791338788207,
    -0.37612471240078243,
    0.11282450088960652,
    -0.026825992168818515,
    0.005164800720113156,
    -0.0008061635856414364,
    9.67168369375208e-05,
    -7.756955478859171e-06,
    3.007955257374649e-07,
)

WIDTHS = (0.3, 0.4, 0.5, 0.35)

HARD, PLACE, KIND, FULL, ROWS = 8, 16, 19, 20, 24
SQUARE, FEATURES = 24, 48
OFFSETS = ((0, 0), (0, 1), (1, -1), (1, 0), (1, 1))
MOST_BLOCKS = 128
CHUNK = 128
LAG = 12
GROUP = 8
SIDES = 2


def pair_counts(rows, cols):
    return [(rows - da) * (cols - abs(db)) for da, db in OFFSETS]


def choose(species, entries):
    value = jnp.full(species.shape, entries[3], jnp.float32)
    for kind in (2, 1, 0):
        value = jnp.where(species == kind, entries[kind], value)
    return value


def slab_kernel(*refs):
    sources, out_ref, landed, done = refs[:9], refs[9], refs[10:19], refs[19]
    members = sources[4].shape[0]
    copies = []

    def fetch(source, target):
        copy = pltpu.make_async_copy(source, target, done.at[len(copies)])
        copy.start()
        copies.append(copy)
        return copy

    desc_ref, pos_ref, species_ref, counts_ref, w_in, b_in, w_hid, b_hid, w_out = landed
    early = [fetch(sources[k], landed[k]) for k in (0, 5, 4)]
    middle = [fetch(sources[k], landed[k]) for k in (6, 7, 8)]
    late = [fetch(sources[k], landed[k]) for k in (1, 2, 3)]
    for copy in early:
        copy.wait()
    rows = desc_ref[...]
    slots = rows.shape[0]
    firsts, electro, raw = [], [], []
    for m in range(members):
        summed = jnp.dot(rows, w_in[m], preferred_element_type=jnp.float32) + b_in[m : m + 1, :]
        firsts.append(jnp.tanh(summed).astype(jnp.bfloat16))
    for copy in middle:
        copy.wait()
    for start in range(0, members, GROUP):
        group = range(start, start + GROUP)
        seconds = []
        for m in group:
            summed = jnp.dot(firsts[m], w_hid[m], preferred_element_type=jnp.float32)
            seconds.append(jnp.tanh(summed + b_hid[m : m + 1, :]).astype(jnp.bfloat16))
        for m in group:
            outputs = lax.dot_general(
                w_out[m],
                seconds[m - start],
                (((1,), (1,)), ((), ())),
                preferred_element_type=jnp.float32,
            )
            electro.append(outputs[0:1])
            raw.append(outputs[1:2])
    for copy in late:
        copy.wait()
    species = species_ref[0]
    slot_iota = lax.broadcasted_iota(jnp.int32, (1, slots), 1)
    occupancy = (slot_iota < counts_ref[0, 0]).astype(jnp.float32)
    shifts = choose(species, (-0.8, 0.4, 1.2, -0.3))
    raw = jnp.concatenate(raw, axis=0)
    hardness = 2.5 + (jnp.maximum(raw, 0.0) + jnp.log1p(jnp.exp(-jnp.abs(raw))))
    right = -(jnp.concatenate(electro, axis=0) + shifts) * occupancy
    atoms = jnp.concatenate(
        [pos_ref[0, 0], pos_ref[1, 0], pos_ref[2, 0], species.astype(jnp.float32), occupancy]
        + [jnp.zeros((1, slots), jnp.float32)] * (ROWS - FULL - 1),
        axis=0,
    )
    for peer in range(out_ref.shape[0]):
        out_ref[peer, 0:HARD, :] = right
        out_ref[peer, HARD:PLACE, :] = hardness
        out_ref[peer, PLACE:ROWS, :] = atoms


def thirds(values):
    high = values.astype(jnp.bfloat16).astype(jnp.float32)
    rest = values - high
    middle = rest.astype(jnp.bfloat16).astype(jnp.float32)
    return high, middle, rest - middle


def pair_features(places, kind):
    one, zero = jnp.ones_like(kind), jnp.zeros_like(kind)
    near, far = [], []
    for place in places:
        h, m, l = thirds(place)
        near += [h, h, m, m, h, l]
        far += [2.0 * v for v in (h, m, h, m, l, h)]
    norm = sum(place * place for place in places)
    near += [*thirds(norm), one, one, one]
    far += [-one, -one, -one, *thirds(1.0 - norm)]
    count = len(WIDTHS)
    near += [(kind == k).astype(jnp.float32) for k in range(count)] * 3
    pairs = [
        choose(kind, [(WIDTHS[k] ** 2 + other**2) ** -0.5 for other in WIDTHS])
        for k in range(count)
    ]
    far += [part for third in zip(*map(thirds, pairs)) for part in third]
    rest = [zero] * (FEATURES - len(near))
    return near + rest, far + rest


def pair_block(products, first_row, own):
    slots = products.shape[1] // 2
    left = jnp.maximum(products[:, 0:slots], 0.0)
    inv = products[:, slots:]
    y = (1.000001 - left) * (inv * inv)
    value = jnp.full_like(y, 0.005 * ERF_SERIES[-1])
    for term in ERF_SERIES[-2::-1]:
        value = value * y + 0.005 * term
    value = value * ((left * inv) * (left * left))
    if own:
        i = lax.broadcasted_iota(jnp.int32, value.shape, 0) + first_row
        j = lax.broadcasted_iota(jnp.int32, value.shape, 1)
        value = jnp.where(i == j, 0.0, value)
    return value


def times(vectors, block):
    return jnp.dot(vectors, block, preferred_element_type=jnp.float32)


def times_t(vectors, block):
    return lax.dot_general(
        vectors, block, (((1,), (1,)), ((), ())), preferred_element_type=jnp.float32
    )


def halves(values):
    high = values.astype(jnp.bfloat16)
    return high, (values - high.astype(jnp.float32)).astype(jnp.bfloat16)


def solve_kernel(
    grid, mine_ref, theirs_ref, out_ref, slab_ref, feats, near, far, vecs, sums, resid, resid_half, blocks
):
    rows, columns = grid
    cells, _, slots = slab_ref.shape
    members = HARD
    side = lax.rem(lax.axis_index("sub"), SIDES)
    for k in range(cells // SIDES):
        slab_ref[SIDES * k + side] = mine_ref[k]
        slab_ref[SIDES * k + (1 - side)] = theirs_ref[k]
    centres = (rows / 2, columns / 2, 0.5)
    rows_of = pair_features(
        [slab_ref[:, PLACE + k, :] - centres[k] for k in range(3)], slab_ref[:, KIND, :]
    )
    for k, row in enumerate(rows_of[0] + rows_of[1]):
        feats[:, k, :] = row
    blank = jnp.zeros((SQUARE, slots), jnp.float32)
    for c in range(cells):
        near[c] = feats[c, 0:FEATURES, :].T.astype(jnp.bfloat16)
        apart = jnp.concatenate([feats[c, FEATURES : FEATURES + SQUARE, :], blank], axis=0)
        spread = jnp.concatenate([blank, feats[c, FEATURES + SQUARE :, :]], axis=0)
        far[c] = jnp.concatenate([apart, spread], axis=1).astype(jnp.bfloat16)
        high, low = halves(slab_ref[c, 0:HARD, :])
        full = slab_ref[c, FULL : FULL + 1, :]
        row = lax.broadcasted_iota(jnp.int32, (16, slots), 0)
        lines = [high.astype(jnp.float32), low.astype(jnp.float32), jnp.where(row == 0, full, 0.0)]
        lines = jnp.concatenate(lines, axis=0).astype(jnp.bfloat16)
        vecs[c] = jnp.concatenate([lines, lines], axis=1)
        sums[c] = jnp.zeros_like(sums[c])

    def row_pairs(a, last):
        pairs = []
        for da, db in OFFSETS[:2] if last else OFFSETS:
            for column in range(max(0, -db), columns - max(0, db)):
                c = a * columns + column
                place = a * (5 * columns - 3) + len(pairs)
                pairs.append((c, c + da * columns + db, place, da == db == 0))
        return pairs

    def over_rows(handle, carry):
        for a in range(rows):
            carry = handle(row_pairs(a, a == rows - 1), carry)
        return carry

    def build(pairs, carry):
        for c, d, place, own in pairs:
            for first_row in range(0, slots, CHUNK):
                products = times(near[c, first_row : first_row + CHUNK, :], far[d])
                high, low = halves(pair_block(products, first_row, own))
                blocks[place, first_row : first_row + CHUNK, :] = high
                blocks[place, slots + first_row : slots + first_row + CHUNK, :] = low
        return carry

    def first_pass(pairs, carry):
        terms = []
        for c, d, place, own in pairs:
            block = blocks[place]
            terms.append((d, times(vecs[c], block)))
            if not own:
                image = times_t(vecs[d, :, 0:slots], block)
                terms.append((c, image[:, 0:slots] + image[:, slots:]))
        for cell, term in terms:
            sums[cell] += term
        return carry

    every = over_rows(lambda pairs, kept: kept + pairs, [])
    for i in range(len(every) + LAG):
        if i >= LAG:
            first_pass(every[i - LAG : i - LAG + 1], 0)
        build(every[i : i + 1], 0)

    def applied(c):
        hard = slab_ref[c, HARD:PLACE, :]
        full = slab_ref[c, FULL : FULL + 1, :]
        right = slab_ref[c, 0:HARD, :]
        coupled = sums[c]
        image_s = hard * right + full * (coupled[0:8] + coupled[8:16])
        image_u = full * (hard + coupled[16:17])
        return hard, full, right, image_s, image_u

    shape = (members, slots)
    norm_s, prod_s, prod_u, total_s = (jnp.zeros(shape, jnp.float32) for _ in range(4))
    norm_u = jnp.zeros((1, slots), jnp.float32)
    for c in range(cells):
        hard, full, right, image_s, image_u = applied(c)
        norm_s += right * right
        norm_u += full * full
        prod_s += right * image_s
        prod_u += full * image_u
        total_s += right

    def over(values):
        return jnp.sum(values, axis=1, keepdims=True)

    both = lambda s, u: jnp.concatenate([s, jnp.broadcast_to(u, s.shape)], axis=0)
    norm0 = both(over(norm_s), over(norm_u))
    total0 = both(over(total_s), over(norm_u))
    alpha0 = norm0 / both(over(prod_s), over(prod_u))

    norm1, prod1, total1 = (jnp.zeros((2 * members, slots), jnp.float32) for _ in range(3))
    for c in range(cells):
        hard, full, right, image_s, image_u = applied(c)
        left = both(right, full) - alpha0 * jnp.concatenate([image_s, image_u], axis=0)
        resid[c] = left
        high, low = halves(left)
        lines = jnp.concatenate([high, low], axis=0)
        resid_half[c] = jnp.concatenate([lines, lines], axis=1)
        square = left * left
        norm1 += square
        prod1 += jnp.concatenate([hard, hard], axis=0) * square
        total1 += left

    def second_pass(pairs, carry):
        for c, d, place, own in pairs:
            image = times(resid_half[c], blocks[place])
            part = (image[0:16] + image[16:32]) * resid[d]
            carry = carry + (part if own else 2.0 * part)
        return carry

    prod1 = over_rows(second_pass, prod1)

    norm1, prod1, total1 = over(norm1), over(prod1), over(total1)
    momentum = norm1 / norm0
    alpha1 = norm1 / (prod1 - momentum * norm1 / alpha0)
    weight0 = alpha0 + alpha1 * momentum
    totals = weight0 * total0 + alpha1 * total1
    multiplier = totals[0:members] / totals[members:]
    mine = lax.axis_index("cell") * columns + lax.axis_index("sub")
    right = both(slab_ref[mine, 0:HARD, :], slab_ref[mine, FULL : FULL + 1, :])
    answer = weight0 * right + alpha1 * resid[mine]
    out_ref[...] = answer[0:members] - multiplier * answer[members:]


def solve_only(mine, theirs):
    rows, columns = lax.axis_size("cell"), lax.axis_size("sub")
    cells, slots = rows * columns, mine.shape[2]
    vmem = pl.BlockSpec(memory_space=pltpu.VMEM)
    blocks = sum(pair_counts(rows, columns))
    return pl.pallas_call(
        lambda *refs: solve_kernel((rows, columns), *refs),
        out_shape=jax.ShapeDtypeStruct((HARD, slots), jnp.float32),
        in_specs=[vmem] * SIDES,
        out_specs=vmem,
        scratch_shapes=[
            pltpu.VMEM((cells, ROWS, slots), jnp.float32),
            pltpu.VMEM((cells, 2 * FEATURES, slots), jnp.float32),
            pltpu.VMEM((cells, slots, FEATURES), jnp.bfloat16),
            pltpu.VMEM((cells, FEATURES, 2 * slots), jnp.bfloat16),
            pltpu.VMEM((cells, 32, 2 * slots), jnp.bfloat16),
            pltpu.VMEM((cells, 32, slots), jnp.float32),
            pltpu.VMEM((cells, 16, slots), jnp.float32),
            pltpu.VMEM((cells, 32, 2 * slots), jnp.bfloat16),
            pltpu.VMEM((blocks, 2 * slots, slots), jnp.bfloat16),
        ],
        compiler_params=pltpu.CompilerParams(vmem_limit_bytes=32 << 20),
        name="solve",
    )(mine, theirs)


def gathered(descriptors, positions, species, counts, w_in, b_in, w_hid, b_hid, w_out):
    rows, columns = lax.axis_size("cell"), lax.axis_size("sub")
    cells, slots, members = rows * columns, descriptors.shape[2], w_in.shape[0]
    vmem = pl.BlockSpec(memory_space=pltpu.VMEM)
    args = (
        descriptors.reshape(slots, -1), positions, species, counts, w_in, b_in, w_hid, b_hid, w_out
    )
    landed = [
        (pltpu.SMEM if arg is counts else pltpu.VMEM)(arg.shape, arg.dtype) for arg in args
    ]
    slabs = pl.pallas_call(
        slab_kernel,
        out_shape=jax.ShapeDtypeStruct((cells // SIDES, ROWS, slots), jnp.float32),
        in_specs=[pl.BlockSpec(memory_space=pltpu.HBM)] * len(args),
        out_specs=vmem,
        scratch_shapes=landed + [pltpu.SemaphoreType.DMA((len(args),))],
        compiler_params=pltpu.CompilerParams(vmem_limit_bytes=60 << 20),
        name="slab",
    )(*args)
    groups = [
        [row * columns + column for row in range(rows) for column in range(side, columns, SIDES)]
        for side in range(SIDES)
    ]
    mine = lax.all_to_all(
        slabs, ("cell", "sub"), 0, 0, tiled=True, axis_index_groups=groups
    )
    theirs = lax.ppermute(mine, "sub", [(column, column ^ 1) for column in range(columns)])
    charges = solve_only(mine, theirs)
    return charges.reshape(members, 1, 1, slots)


def extended_2(shard, sides, width):
    for axis, dim in sides:
        size, length = (lax.axis_size(axis), shard.shape[dim])
        up = [(i, (i + 1) % size) for i in range(size - 1)]
        down = [(j, i) for i, j in up]
        last = lax.slice_in_dim(shard, length - width, length, axis=dim)
        leading = lax.slice_in_dim(shard, 0, width, axis=dim)
        before = lax.ppermute(last, axis, up)
        after = lax.ppermute(leading, axis, down)
        shard = jnp.concatenate([before, shard, after], axis=dim)
    return shard


def lookup(species, entries):
    choices_table = jnp.array(entries, jnp.float32)
    kinds = jnp.arange(4, dtype=jnp.int32)
    return jnp.sum((species[..., None] == kinds).astype(jnp.float32) * choices_table, axis=-1)


def coupling(own_atoms, far_atoms, self_cell):
    delta_a = own_atoms[0][..., :, None] - far_atoms[0][..., None, :]
    delta_b = own_atoms[1][..., :, None] - far_atoms[1][..., None, :]
    delta_c = own_atoms[2][..., :, None] - far_atoms[2][..., None, :]
    distance_sq = delta_a * delta_a + delta_b * delta_b + delta_c * delta_c
    radius = jnp.sqrt(distance_sq + 1e-06)
    pair_width = jnp.sqrt(own_atoms[3][..., :, None] ** 2 + far_atoms[3][..., None, :] ** 2)
    smooth_cut = (1.0 - jnp.minimum(distance_sq, 1.0)) ** 3
    kernel = 0.005 * smooth_cut * jax.scipy.special.erf(radius / pair_width) / radius
    kernel = kernel * own_atoms[4][..., :, None] * far_atoms[4][..., None, :]
    if self_cell:
        kernel = kernel * (1.0 - jnp.eye(kernel.shape[-1], dtype=jnp.float32))
    return kernel


def committee(flat_rows, w_in, b_in, w_hid, b_hid, w_out):

    def member_fn(weights):
        first_w, first_b, second_w, second_b, last_w = weights
        first = jnp.tanh(
            jnp.dot(flat_rows, first_w, preferred_element_type=jnp.float32) + first_b
        ).astype(jnp.bfloat16)
        second = jnp.tanh(
            jnp.dot(first, second_w, preferred_element_type=jnp.float32) + second_b
        ).astype(jnp.bfloat16)
        return jnp.dot(second, last_w.T, preferred_element_type=jnp.float32).T

    return lax.map(member_fn, (w_in, b_in, w_hid, b_hid, w_out))


def expand(values):
    return values[:, None, None, None]


def extend(vectors):
    return extended_2(vectors, (("cell", 1), ("sub", 2)), 1)


def two_products(residual, image_vec):
    return lax.psum(
        (
            jnp.sum(residual * residual, axis=(1, 2, 3)),
            jnp.sum(residual * image_vec, axis=(1, 2, 3)),
        ),
        ("cell", "sub"),
    )


def body(descriptors, positions, species, counts, w_in, b_in, w_hid, b_hid, w_out):
    rows_a, rows_b, slot_count, features = descriptors.shape
    members = w_in.shape[0]
    slot_iota = lax.broadcasted_iota(jnp.int32, (rows_a, rows_b, slot_count), 2)
    occupancy = (slot_iota < counts[:, :, None]).astype(jnp.float32)
    widths = lookup(species, (0.3, 0.4, 0.5, 0.35))
    shifts = lookup(species, (-0.8, 0.4, 1.2, -0.3))
    atom_data = jnp.stack([positions[0], positions[1], positions[2], widths, occupancy])
    extended = extended_2(atom_data, (("cell", 1), ("sub", 2)), 1)
    outputs = committee(descriptors.reshape(-1, features), w_in, b_in, w_hid, b_hid, w_out)
    electro = outputs[:, 0].reshape(members, rows_a, rows_b, slot_count) + shifts
    hardness = 2.5 + jax.nn.softplus(outputs[:, 1]).reshape(members, rows_a, rows_b, slot_count)
    right_side = jnp.concatenate([-electro * occupancy, jnp.broadcast_to(occupancy, electro.shape)])
    diagonal = jnp.concatenate([hardness, hardness])
    offsets = [(row_step, col_step) for row_step in (-1, 0, 1) for col_step in (-1, 0, 1)]

    def neighbours(grown, row_step, col_step):
        return grown[:, 1 + row_step : 1 + row_step + rows_a, 1 + col_step : 1 + col_step + rows_b]

    def block_for(row_step, col_step):
        return coupling(
            atom_data, neighbours(extended, row_step, col_step), row_step == 0 and col_step == 0
        )

    def operate(vectors):
        grown = extend(vectors)
        summed = diagonal * vectors
        for offset_number in range(9):
            row_step, col_step = offsets[offset_number]
            tile_block = block_for(row_step, col_step)
            summed = summed + jnp.einsum(
                "abij,rabj->rabi",
                tile_block,
                neighbours(grown, row_step, col_step),
                precision=lax.Precision.HIGHEST,
            )
        return summed

    solution = jnp.zeros_like(right_side)
    residual = right_side
    image_vec = operate(residual)
    norm_now, product = two_products(residual, image_vec)
    step_size = norm_now / product
    direction = residual
    along = image_vec
    for iteration in range(ITERS):
        solution = solution + expand(step_size) * direction
        residual = residual - expand(step_size) * along
        if iteration + 1 < ITERS:
            image_vec = operate(residual)
            norm_next, product = two_products(residual, image_vec)
            momentum = norm_next / norm_now
            step_size = norm_next / (product - momentum * norm_next / step_size)
            direction = residual + expand(momentum) * direction
            along = image_vec + expand(momentum) * along
            norm_now = norm_next
    source_part = solution[:members]
    unit_part = solution[members:]
    source_total, unit_total = lax.psum(
        (jnp.sum(source_part, axis=(1, 2, 3)), jnp.sum(unit_part, axis=(1, 2, 3))), ("cell", "sub")
    )
    multiplier = source_total / unit_total
    return source_part - expand(multiplier) * unit_part


def solution(mesh):
    placed = (
        P(("rep", "cell"), "sub", None, None),
        P(None, ("rep", "cell"), "sub", None),
        P(("rep", "cell"), "sub", None),
        P(("rep", "cell"), "sub"),
        P(),
        P(),
        P(),
        P(),
        P(),
    )
    rows, columns = mesh.shape["cell"], mesh.shape["sub"]
    return jax.shard_map(
        gathered if columns % SIDES == 0 and sum(pair_counts(rows, columns)) <= MOST_BLOCKS else body,
        mesh=mesh,
        in_specs=placed,
        out_specs=P(None, ("rep", "cell"), "sub", None),
        check_vma=False,
    )
```

```python
import jax
import jax.numpy as jnp
from jax import lax
from jax.experimental import pallas as pl
from jax.experimental.pallas import tpu as pltpu
from jax.sharding import PartitionSpec as P

ITERS = 2

ERF_SERIES = (
    1.1283791338788207,
    -0.37612471240078243,
    0.11282450088960652,
    -0.026825992168818515,
    0.005164800720113156,
    -0.0008061635856414364,
    9.67168369375208e-05,
    -7.756955478859171e-06,
    3.007955257374649e-07,
)

WIDTHS = (0.3, 0.4, 0.5, 0.35)

HARD, PLACE, KIND, FULL, ROWS = 8, 16, 19, 20, 24
SQUARE, FEATURES = 24, 48
OFFSETS = ((0, 0), (0, 1), (1, -1), (1, 0), (1, 1))
MOST_BLOCKS = 128
CHUNK = 128
LAG = 12
GROUP = 8
SIDES = 2


def pair_counts(rows, cols):
    return [(rows - da) * (cols - abs(db)) for da, db in OFFSETS]


def choose(species, entries):
    value = jnp.full(species.shape, entries[3], jnp.float32)
    for kind in (2, 1, 0):
        value = jnp.where(species == kind, entries[kind], value)
    return value


def slab_kernel(*refs):
    sources, out_ref, landed, done = refs[:9], refs[9], refs[10:19], refs[19]
    members = sources[4].shape[0]
    copies = []

    def fetch(source, target):
        copy = pltpu.make_async_copy(source, target, done.at[len(copies)])
        copy.start()
        copies.append(copy)
        return copy

    desc_ref, pos_ref, species_ref, counts_ref, w_in, b_in, w_hid, b_hid, w_out = landed
    early = [fetch(sources[k], landed[k]) for k in (0, 5, 4)]
    middle = [fetch(sources[k], landed[k]) for k in (6, 7, 8)]
    late = [fetch(sources[k], landed[k]) for k in (1, 2, 3)]
    for copy in early:
        copy.wait()
    rows = desc_ref[...]
    slots = rows.shape[0]
    firsts, electro, raw = [], [], []
    for m in range(members):
        summed = jnp.dot(rows, w_in[m], preferred_element_type=jnp.float32) + b_in[m : m + 1, :]
        firsts.append(jnp.tanh(summed).astype(jnp.bfloat16))
    for copy in middle:
        copy.wait()
    for start in range(0, members, GROUP):
        group = range(start, start + GROUP)
        seconds = []
        for m in group:
            summed = jnp.dot(firsts[m], w_hid[m], preferred_element_type=jnp.float32)
            seconds.append(jnp.tanh(summed + b_hid[m : m + 1, :]).astype(jnp.bfloat16))
        for m in group:
            outputs = lax.dot_general(
                w_out[m],
                seconds[m - start],
                (((1,), (1,)), ((), ())),
                preferred_element_type=jnp.float32,
            )
            electro.append(outputs[0:1])
            raw.append(outputs[1:2])
    for copy in late:
        copy.wait()
    species = species_ref[0]
    slot_iota = lax.broadcasted_iota(jnp.int32, (1, slots), 1)
    occupancy = (slot_iota < counts_ref[0, 0]).astype(jnp.float32)
    shifts = choose(species, (-0.8, 0.4, 1.2, -0.3))
    raw = jnp.concatenate(raw, axis=0)
    hardness = 2.5 + (jnp.maximum(raw, 0.0) + jnp.log1p(jnp.exp(-jnp.abs(raw))))
    right = -(jnp.concatenate(electro, axis=0) + shifts) * occupancy
    atoms = jnp.concatenate(
        [pos_ref[0, 0], pos_ref[1, 0], pos_ref[2, 0], species.astype(jnp.float32), occupancy]
        + [jnp.zeros((1, slots), jnp.float32)] * (ROWS - FULL - 1),
        axis=0,
    )
    for peer in range(out_ref.shape[0]):
        out_ref[peer, 0:HARD, :] = right
        out_ref[peer, HARD:PLACE, :] = hardness
        out_ref[peer, PLACE:ROWS, :] = atoms


def thirds(values):
    high = values.astype(jnp.bfloat16).astype(jnp.float32)
    rest = values - high
    middle = rest.astype(jnp.bfloat16).astype(jnp.float32)
    return high, middle, rest - middle


def pair_features(places, kind):
    one, zero = jnp.ones_like(kind), jnp.zeros_like(kind)
    near, far = [], []
    for place in places:
        h, m, l = thirds(place)
        near += [h, h, m, m, h, l]
        far += [2.0 * v for v in (h, m, h, m, l, h)]
    norm = sum(place * place for place in places)
    near += [*thirds(norm), one, one, one]
    far += [-one, -one, -one, *thirds(1.0 - norm)]
    count = len(WIDTHS)
    near += [(kind == k).astype(jnp.float32) for k in range(count)] * 3
    pairs = [
        choose(kind, [(WIDTHS[k] ** 2 + other**2) ** -0.5 for other in WIDTHS])
        for k in range(count)
    ]
    far += [part for third in zip(*map(thirds, pairs)) for part in third]
    rest = [zero] * (FEATURES - len(near))
    return near + rest, far + rest


def pair_block(products, first_row, own):
    slots = products.shape[1] // 2
    left = jnp.maximum(products[:, 0:slots], 0.0)
    inv = products[:, slots:]
    y = (1.000001 - left) * (inv * inv)
    value = jnp.full_like(y, 0.005 * ERF_SERIES[-1])
    for term in ERF_SERIES[-2::-1]:
        value = value * y + 0.005 * term
    value = value * ((left * inv) * (left * left))
    if own:
        i = lax.broadcasted_iota(jnp.int32, value.shape, 0) + first_row
        j = lax.broadcasted_iota(jnp.int32, value.shape, 1)
        value = jnp.where(i == j, 0.0, value)
    return value


def times(vectors, block):
    return jnp.dot(vectors, block, preferred_element_type=jnp.float32)


def times_t(vectors, block):
    return lax.dot_general(
        vectors, block, (((1,), (1,)), ((), ())), preferred_element_type=jnp.float32
    )


def halves(values):
    high = values.astype(jnp.bfloat16)
    return high, (values - high.astype(jnp.float32)).astype(jnp.bfloat16)


def solve_kernel(
    grid, mine_ref, theirs_ref, out_ref, slab_ref, feats, near, far, vecs, sums, resid, resid_half, blocks
):
    rows, columns = grid
    cells, _, slots = slab_ref.shape
    members = HARD
    side = lax.rem(lax.axis_index("sub"), SIDES)
    for k in range(cells // SIDES):
        slab_ref[SIDES * k + side] = mine_ref[k]
        slab_ref[SIDES * k + (1 - side)] = theirs_ref[k]
    centres = (rows / 2, columns / 2, 0.5)
    rows_of = pair_features(
        [slab_ref[:, PLACE + k, :] - centres[k] for k in range(3)], slab_ref[:, KIND, :]
    )
    for k, row in enumerate(rows_of[0] + rows_of[1]):
        feats[:, k, :] = row
    blank = jnp.zeros((SQUARE, slots), jnp.float32)
    for c in range(cells):
        near[c] = feats[c, 0:FEATURES, :].T.astype(jnp.bfloat16)
        apart = jnp.concatenate([feats[c, FEATURES : FEATURES + SQUARE, :], blank], axis=0)
        spread = jnp.concatenate([blank, feats[c, FEATURES + SQUARE :, :]], axis=0)
        far[c] = jnp.concatenate([apart, spread], axis=1).astype(jnp.bfloat16)
        high, low = halves(slab_ref[c, 0:HARD, :])
        full = slab_ref[c, FULL : FULL + 1, :]
        row = lax.broadcasted_iota(jnp.int32, (16, slots), 0)
        lines = [high.astype(jnp.float32), low.astype(jnp.float32), jnp.where(row == 0, full, 0.0)]
        lines = jnp.concatenate(lines, axis=0).astype(jnp.bfloat16)
        vecs[c] = jnp.concatenate([lines, lines], axis=1)
        sums[c] = jnp.zeros_like(sums[c])

    def row_pairs(a, last):
        pairs = []
        for da, db in OFFSETS[:2] if last else OFFSETS:
            for column in range(max(0, -db), columns - max(0, db)):
                c = a * columns + column
                place = a * (5 * columns - 3) + len(pairs)
                pairs.append((c, c + da * columns + db, place, da == db == 0))
        return pairs

    def over_rows(handle, carry):
        for a in range(rows):
            carry = handle(row_pairs(a, a == rows - 1), carry)
        return carry

    def build(pairs, carry):
        for c, d, place, own in pairs:
            for first_row in range(0, slots, CHUNK):
                products = times(near[c, first_row : first_row + CHUNK, :], far[d])
                high, low = halves(pair_block(products, first_row, own))
                blocks[place, first_row : first_row + CHUNK, :] = high
                blocks[place, slots + first_row : slots + first_row + CHUNK, :] = low
        return carry

    def first_pass(pairs, carry):
        terms = []
        for c, d, place, own in pairs:
            block = blocks[place]
            terms.append((d, times(vecs[c], block)))
            if not own:
                image = times_t(vecs[d, :, 0:slots], block)
                terms.append((c, image[:, 0:slots] + image[:, slots:]))
        for cell, term in terms:
            sums[cell] += term
        return carry

    every = over_rows(lambda pairs, kept: kept + pairs, [])
    for i in range(len(every) + LAG):
        if i >= LAG:
            first_pass(every[i - LAG : i - LAG + 1], 0)
        build(every[i : i + 1], 0)

    def applied(c):
        hard = slab_ref[c, HARD:PLACE, :]
        full = slab_ref[c, FULL : FULL + 1, :]
        right = slab_ref[c, 0:HARD, :]
        coupled = sums[c]
        image_s = hard * right + full * (coupled[0:8] + coupled[8:16])
        image_u = full * (hard + coupled[16:17])
        return hard, full, right, image_s, image_u

    shape = (members, slots)
    norm_s, prod_s, prod_u, total_s = (jnp.zeros(shape, jnp.float32) for _ in range(4))
    norm_u = jnp.zeros((1, slots), jnp.float32)
    for c in range(cells):
        hard, full, right, image_s, image_u = applied(c)
        norm_s += right * right
        norm_u += full * full
        prod_s += right * image_s
        prod_u += full * image_u
        total_s += right

    def over(values):
        return jnp.sum(values, axis=1, keepdims=True)

    both = lambda s, u: jnp.concatenate([s, jnp.broadcast_to(u, s.shape)], axis=0)
    norm0 = both(over(norm_s), over(norm_u))
    total0 = both(over(total_s), over(norm_u))
    alpha0 = norm0 / both(over(prod_s), over(prod_u))

    norm1, prod1, total1 = (jnp.zeros((2 * members, slots), jnp.float32) for _ in range(3))
    for c in range(cells):
        hard, full, right, image_s, image_u = applied(c)
        left = both(right, full) - alpha0 * jnp.concatenate([image_s, image_u], axis=0)
        resid[c] = left
        high, low = halves(left)
        lines = jnp.concatenate([high, low], axis=0)
        resid_half[c] = jnp.concatenate([lines, lines], axis=1)
        square = left * left
        norm1 += square
        prod1 += jnp.concatenate([hard, hard], axis=0) * square
        total1 += left

    def second_pass(pairs, carry):
        for c, d, place, own in pairs:
            image = times(resid_half[c], blocks[place])
            part = (image[0:16] + image[16:32]) * resid[d]
            carry = carry + (part if own else 2.0 * part)
        return carry

    prod1 = over_rows(second_pass, prod1)

    norm1, prod1, total1 = over(norm1), over(prod1), over(total1)
    momentum = norm1 / norm0
    alpha1 = norm1 / (prod1 - momentum * norm1 / alpha0)
    weight0 = alpha0 + alpha1 * momentum
    totals = weight0 * total0 + alpha1 * total1
    multiplier = totals[0:members] / totals[members:]
    mine = lax.axis_index("cell") * columns + lax.axis_index("sub")
    right = both(slab_ref[mine, 0:HARD, :], slab_ref[mine, FULL : FULL + 1, :])
    answer = weight0 * right + alpha1 * resid[mine]
    out_ref[...] = answer[0:members] - multiplier * answer[members:]


def solve_only(mine, theirs):
    rows, columns = lax.axis_size("cell"), lax.axis_size("sub")
    cells, slots = rows * columns, mine.shape[2]
    vmem = pl.BlockSpec(memory_space=pltpu.VMEM)
    blocks = sum(pair_counts(rows, columns))
    return pl.pallas_call(
        lambda *refs: solve_kernel((rows, columns), *refs),
        out_shape=jax.ShapeDtypeStruct((HARD, slots), jnp.float32),
        in_specs=[vmem] * SIDES,
        out_specs=vmem,
        scratch_shapes=[
            pltpu.VMEM((cells, ROWS, slots), jnp.float32),
            pltpu.VMEM((cells, 2 * FEATURES, slots), jnp.float32),
            pltpu.VMEM((cells, slots, FEATURES), jnp.bfloat16),
            pltpu.VMEM((cells, FEATURES, 2 * slots), jnp.bfloat16),
            pltpu.VMEM((cells, 32, 2 * slots), jnp.bfloat16),
            pltpu.VMEM((cells, 32, slots), jnp.float32),
            pltpu.VMEM((cells, 16, slots), jnp.float32),
            pltpu.VMEM((cells, 32, 2 * slots), jnp.bfloat16),
            pltpu.VMEM((blocks, 2 * slots, slots), jnp.bfloat16),
        ],
        compiler_params=pltpu.CompilerParams(vmem_limit_bytes=32 << 20),
        name="solve",
    )(mine, theirs)


def gathered(descriptors, positions, species, counts, w_in, b_in, w_hid, b_hid, w_out):
    rows, columns = lax.axis_size("cell"), lax.axis_size("sub")
    cells, slots, members = rows * columns, descriptors.shape[2], w_in.shape[0]
    vmem = pl.BlockSpec(memory_space=pltpu.VMEM)
    args = (
        descriptors.reshape(slots, -1), positions, species, counts, w_in, b_in, w_hid, b_hid, w_out
    )
    landed = [
        (pltpu.SMEM if arg is counts else pltpu.VMEM)(arg.shape, arg.dtype) for arg in args
    ]
    slabs = pl.pallas_call(
        slab_kernel,
        out_shape=pltpu.VMEM((cells // SIDES, ROWS, slots), jnp.float32),
        in_specs=[pl.BlockSpec(memory_space=pltpu.HBM)] * len(args),
        out_specs=vmem,
        scratch_shapes=landed + [pltpu.SemaphoreType.DMA((len(args),))],
        compiler_params=pltpu.CompilerParams(vmem_limit_bytes=60 << 20),
        name="slab",
    )(*args)
    groups = [
        [row * columns + column for row in range(rows) for column in range(side, columns, SIDES)]
        for side in range(SIDES)
    ]
    mine = lax.all_to_all(
        slabs, ("cell", "sub"), 0, 0, tiled=True, axis_index_groups=groups
    )
    theirs = lax.ppermute(mine, "sub", [(column, column ^ 1) for column in range(columns)])
    charges = solve_only(mine, theirs)
    return charges.reshape(members, 1, 1, slots)


def extended_2(shard, sides, width):
    for axis, dim in sides:
        size, length = (lax.axis_size(axis), shard.shape[dim])
        up = [(i, (i + 1) % size) for i in range(size - 1)]
        down = [(j, i) for i, j in up]
        last = lax.slice_in_dim(shard, length - width, length, axis=dim)
        leading = lax.slice_in_dim(shard, 0, width, axis=dim)
        before = lax.ppermute(last, axis, up)
        after = lax.ppermute(leading, axis, down)
        shard = jnp.concatenate([before, shard, after], axis=dim)
    return shard


def lookup(species, entries):
    choices_table = jnp.array(entries, jnp.float32)
    kinds = jnp.arange(4, dtype=jnp.int32)
    return jnp.sum((species[..., None] == kinds).astype(jnp.float32) * choices_table, axis=-1)


def coupling(own_atoms, far_atoms, self_cell):
    delta_a = own_atoms[0][..., :, None] - far_atoms[0][..., None, :]
    delta_b = own_atoms[1][..., :, None] - far_atoms[1][..., None, :]
    delta_c = own_atoms[2][..., :, None] - far_atoms[2][..., None, :]
    distance_sq = delta_a * delta_a + delta_b * delta_b + delta_c * delta_c
    radius = jnp.sqrt(distance_sq + 1e-06)
    pair_width = jnp.sqrt(own_atoms[3][..., :, None] ** 2 + far_atoms[3][..., None, :] ** 2)
    smooth_cut = (1.0 - jnp.minimum(distance_sq, 1.0)) ** 3
    kernel = 0.005 * smooth_cut * jax.scipy.special.erf(radius / pair_width) / radius
    kernel = kernel * own_atoms[4][..., :, None] * far_atoms[4][..., None, :]
    if self_cell:
        kernel = kernel * (1.0 - jnp.eye(kernel.shape[-1], dtype=jnp.float32))
    return kernel


def committee(flat_rows, w_in, b_in, w_hid, b_hid, w_out):

    def member_fn(weights):
        first_w, first_b, second_w, second_b, last_w = weights
        first = jnp.tanh(
            jnp.dot(flat_rows, first_w, preferred_element_type=jnp.float32) + first_b
        ).astype(jnp.bfloat16)
        second = jnp.tanh(
            jnp.dot(first, second_w, preferred_element_type=jnp.float32) + second_b
        ).astype(jnp.bfloat16)
        return jnp.dot(second, last_w.T, preferred_element_type=jnp.float32).T

    return lax.map(member_fn, (w_in, b_in, w_hid, b_hid, w_out))


def expand(values):
    return values[:, None, None, None]


def extend(vectors):
    return extended_2(vectors, (("cell", 1), ("sub", 2)), 1)


def two_products(residual, image_vec):
    return lax.psum(
        (
            jnp.sum(residual * residual, axis=(1, 2, 3)),
            jnp.sum(residual * image_vec, axis=(1, 2, 3)),
        ),
        ("cell", "sub"),
    )


def body(descriptors, positions, species, counts, w_in, b_in, w_hid, b_hid, w_out):
    rows_a, rows_b, slot_count, features = descriptors.shape
    members = w_in.shape[0]
    slot_iota = lax.broadcasted_iota(jnp.int32, (rows_a, rows_b, slot_count), 2)
    occupancy = (slot_iota < counts[:, :, None]).astype(jnp.float32)
    widths = lookup(species, (0.3, 0.4, 0.5, 0.35))
    shifts = lookup(species, (-0.8, 0.4, 1.2, -0.3))
    atom_data = jnp.stack([positions[0], positions[1], positions[2], widths, occupancy])
    extended = extended_2(atom_data, (("cell", 1), ("sub", 2)), 1)
    outputs = committee(descriptors.reshape(-1, features), w_in, b_in, w_hid, b_hid, w_out)
    electro = outputs[:, 0].reshape(members, rows_a, rows_b, slot_count) + shifts
    hardness = 2.5 + jax.nn.softplus(outputs[:, 1]).reshape(members, rows_a, rows_b, slot_count)
    right_side = jnp.concatenate([-electro * occupancy, jnp.broadcast_to(occupancy, electro.shape)])
    diagonal = jnp.concatenate([hardness, hardness])
    offsets = [(row_step, col_step) for row_step in (-1, 0, 1) for col_step in (-1, 0, 1)]

    def neighbours(grown, row_step, col_step):
        return grown[:, 1 + row_step : 1 + row_step + rows_a, 1 + col_step : 1 + col_step + rows_b]

    def block_for(row_step, col_step):
        return coupling(
            atom_data, neighbours(extended, row_step, col_step), row_step == 0 and col_step == 0
        )

    def operate(vectors):
        grown = extend(vectors)
        summed = diagonal * vectors
        for offset_number in range(9):
            row_step, col_step = offsets[offset_number]
            tile_block = block_for(row_step, col_step)
            summed = summed + jnp.einsum(
                "abij,rabj->rabi",
                tile_block,
                neighbours(grown, row_step, col_step),
                precision=lax.Precision.HIGHEST,
            )
        return summed

    solution = jnp.zeros_like(right_side)
    residual = right_side
    image_vec = operate(residual)
    norm_now, product = two_products(residual, image_vec)
    step_size = norm_now / product
    direction = residual
    along = image_vec
    for iteration in range(ITERS):
        solution = solution + expand(step_size) * direction
        residual = residual - expand(step_size) * along
        if iteration + 1 < ITERS:
            image_vec = operate(residual)
            norm_next, product = two_products(residual, image_vec)
            momentum = norm_next / norm_now
            step_size = norm_next / (product - momentum * norm_next / step_size)
            direction = residual + expand(momentum) * direction
            along = image_vec + expand(momentum) * along
            norm_now = norm_next
    source_part = solution[:members]
    unit_part = solution[members:]
    source_total, unit_total = lax.psum(
        (jnp.sum(source_part, axis=(1, 2, 3)), jnp.sum(unit_part, axis=(1, 2, 3))), ("cell", "sub")
    )
    multiplier = source_total / unit_total
    return source_part - expand(multiplier) * unit_part


def solution(mesh):
    placed = (
        P(("rep", "cell"), "sub", None, None),
        P(None, ("rep", "cell"), "sub", None),
        P(("rep", "cell"), "sub", None),
        P(("rep", "cell"), "sub"),
        P(),
        P(),
        P(),
        P(),
        P(),
    )
    rows, columns = mesh.shape["cell"], mesh.shape["sub"]
    return jax.shard_map(
        gathered if columns % SIDES == 0 and sum(pair_counts(rows, columns)) <= MOST_BLOCKS else body,
        mesh=mesh,
        in_specs=placed,
        out_specs=P(None, ("rep", "cell"), "sub", None),
        check_vma=False,
    )
```

```python
import functools

import jax
import jax.numpy as jnp
from jax import lax
from jax.experimental import pallas as pl
from jax.experimental.pallas import tpu as pltpu
from jax.sharding import PartitionSpec as P

ITERS = 2

ERF_SERIES = (
    1.1283791338788207,
    -0.37612471240078243,
    0.11282450088960652,
    -0.026825992168818515,
    0.005164800720113156,
    -0.0008061635856414364,
    9.67168369375208e-05,
    -7.756955478859171e-06,
    3.007955257374649e-07,
)

WIDTHS = (0.3, 0.4, 0.5, 0.35)

HARD, PLACE, KIND, FULL, ROWS = 8, 16, 19, 20, 24
SQUARE, FEATURES = 24, 48
OFFSETS = ((0, 0), (0, 1), (1, -1), (1, 0), (1, 1))
MOST_BLOCKS = 128
LAG = 12
GROUP = 8
SIDES = 2


def pair_counts(rows, cols):
    return [(rows - da) * (cols - abs(db)) for da, db in OFFSETS]


def choose(species, entries):
    value = jnp.full(species.shape, entries[3], jnp.float32)
    for kind in (2, 1, 0):
        value = jnp.where(species == kind, entries[kind], value)
    return value


def slab_kernel(*refs):
    sources, out_ref, landed, done = refs[:9], refs[9], refs[10:19], refs[19]
    members = sources[4].shape[0]
    copies = []

    def fetch(source, target):
        copy = pltpu.make_async_copy(source, target, done.at[len(copies)])
        copy.start()
        copies.append(copy)
        return copy

    desc_ref, pos_ref, species_ref, counts_ref, w_in, b_in, w_hid, b_hid, w_out = landed
    early = [fetch(sources[k], landed[k]) for k in (0, 5, 4)]
    middle = [fetch(sources[k], landed[k]) for k in (6, 7, 8)]
    late = [fetch(sources[k], landed[k]) for k in (1, 2, 3)]
    for copy in early:
        copy.wait()
    rows = desc_ref[...]
    slots = rows.shape[0]
    firsts, electro, raw = [], [], []
    for m in range(members):
        summed = jnp.dot(rows, w_in[m], preferred_element_type=jnp.float32) + b_in[m : m + 1, :]
        firsts.append(jnp.tanh(summed).astype(jnp.bfloat16))
    for copy in middle:
        copy.wait()
    for start in range(0, members, GROUP):
        group = range(start, start + GROUP)
        seconds = []
        for m in group:
            summed = jnp.dot(firsts[m], w_hid[m], preferred_element_type=jnp.float32)
            seconds.append(jnp.tanh(summed + b_hid[m : m + 1, :]).astype(jnp.bfloat16))
        for m in group:
            outputs = lax.dot_general(
                w_out[m],
                seconds[m - start],
                (((1,), (1,)), ((), ())),
                preferred_element_type=jnp.float32,
            )
            electro.append(outputs[0:1])
            raw.append(outputs[1:2])
    for copy in late:
        copy.wait()
    species = species_ref[0]
    slot_iota = lax.broadcasted_iota(jnp.int32, (1, slots), 1)
    occupancy = (slot_iota < counts_ref[0, 0]).astype(jnp.float32)
    shifts = choose(species, (-0.8, 0.4, 1.2, -0.3))
    raw = jnp.concatenate(raw, axis=0)
    hardness = 2.5 + (jnp.maximum(raw, 0.0) + jnp.log1p(jnp.exp(-jnp.abs(raw))))
    right = -(jnp.concatenate(electro, axis=0) + shifts) * occupancy
    atoms = jnp.concatenate(
        [pos_ref[0, 0], pos_ref[1, 0], pos_ref[2, 0], species.astype(jnp.float32), occupancy]
        + [jnp.zeros((1, slots), jnp.float32)] * (ROWS - FULL - 1),
        axis=0,
    )
    for peer in range(out_ref.shape[0]):
        out_ref[peer, 0:HARD, :] = right
        out_ref[peer, HARD:PLACE, :] = hardness
        out_ref[peer, PLACE:ROWS, :] = atoms


def thirds(values):
    high = values.astype(jnp.bfloat16).astype(jnp.float32)
    rest = values - high
    middle = rest.astype(jnp.bfloat16).astype(jnp.float32)
    return high, middle, rest - middle


def pair_features(places, kind):
    one, zero = jnp.ones_like(kind), jnp.zeros_like(kind)
    near, far = [], []
    for place in places:
        h, m, l = thirds(place)
        near += [h, h, m, m, h, l]
        far += [2.0 * v for v in (h, m, h, m, l, h)]
    norm = sum(place * place for place in places)
    near += [*thirds(norm), one, one, one]
    far += [-one, -one, -one, *thirds(1.0 - norm)]
    count = len(WIDTHS)
    near += [(kind == k).astype(jnp.float32) for k in range(count)] * 3
    pairs = [
        choose(kind, [(WIDTHS[k] ** 2 + other**2) ** -0.5 for other in WIDTHS])
        for k in range(count)
    ]
    far += [part for third in zip(*map(thirds, pairs)) for part in third]
    rest = [zero] * (FEATURES - len(near))
    return near + rest, far + rest


def pair_block(products, first_row, own):
    slots = products.shape[1] // 2
    left = jnp.maximum(products[:, 0:slots], 0.0)
    inv = products[:, slots:]
    y = (1.000001 - left) * (inv * inv)
    value = jnp.full_like(y, 0.005 * ERF_SERIES[-1])
    for term in ERF_SERIES[-2::-1]:
        value = value * y + 0.005 * term
    value = value * ((left * inv) * (left * left))
    if own:
        i = lax.broadcasted_iota(jnp.int32, value.shape, 0) + first_row
        j = lax.broadcasted_iota(jnp.int32, value.shape, 1)
        value = jnp.where(i == j, 0.0, value)
    return value


def times(vectors, block):
    return jnp.dot(vectors, block, preferred_element_type=jnp.float32)


def times_t(vectors, block):
    return lax.dot_general(
        vectors, block, (((1,), (1,)), ((), ())), preferred_element_type=jnp.float32
    )


def halves(values):
    high = values.astype(jnp.bfloat16)
    return high, (values - high.astype(jnp.float32)).astype(jnp.bfloat16)


def grid_pairs(rows, columns):
    pairs = []
    for a in range(rows):
        for da, db in OFFSETS:
            for column in range(max(0, -db), columns - max(0, db)):
                c = a * columns + column
                if a + da < rows:
                    pairs.append((c, c + da * columns + db))
    return pairs


def same_side(pair):
    return pair[0] % SIDES == pair[1] % SIDES


def views(*sides):
    return [sides[c % len(sides)].at[c // len(sides)] for c in range(len(sides) * sides[0].shape[0])]


def prepare(grid, source, slab, feats, near, far, vecs, sums):
    rows, columns = grid
    half, slots = columns // SIDES, slab.shape[2]
    side = lax.rem(lax.axis_index("sub"), SIDES)
    for k in range(slab.shape[0]):
        h = k % half
        slab[k] = source[k + side * (half - 1 - 2 * h)]
    centres = (rows / 2, columns / 2, 0.5)
    rows_of = pair_features(
        [slab[:, PLACE + k, :] - centres[k] for k in range(3)], slab[:, KIND, :]
    )
    for k, row in enumerate(rows_of[0] + rows_of[1]):
        feats[:, k, :] = row
    blank = jnp.zeros((SQUARE, slots), jnp.float32)
    for c in range(slab.shape[0]):
        near[c] = feats[c, 0:FEATURES, :].T.astype(jnp.bfloat16)
        apart = jnp.concatenate([feats[c, FEATURES : FEATURES + SQUARE, :], blank], axis=0)
        spread = jnp.concatenate([blank, feats[c, FEATURES + SQUARE :, :]], axis=0)
        far[c] = jnp.concatenate([apart, spread], axis=1).astype(jnp.bfloat16)
        high, low = halves(slab[c, 0:HARD, :])
        full = slab[c, FULL : FULL + 1, :]
        row = lax.broadcasted_iota(jnp.int32, (16, slots), 0)
        lines = [high.astype(jnp.float32), low.astype(jnp.float32), jnp.where(row == 0, full, 0.0)]
        lines = jnp.concatenate(lines, axis=0).astype(jnp.bfloat16)
        vecs[c] = jnp.concatenate([lines, lines], axis=1)
        sums[c] = jnp.zeros_like(sums[c])


def build_and_apply(pairs, blocks, near, far, vecs, sums):
    slots = near[0].shape[0]
    lag = min(LAG, len(pairs) // 2)
    for i in range(len(pairs) + lag):
        if i >= lag:
            c, d = pairs[i - lag]
            block = blocks[i - lag]
            image = times(vecs[c][...], block)
            if c != d:
                back = times_t(vecs[d][:, 0:slots], block)
                sums[c][...] += back[:, 0:slots] + back[:, slots:]
            sums[d][...] += image
        if i < len(pairs):
            c, d = pairs[i]
            high, low = halves(pair_block(times(near[c][...], far[d][...]), 0, c == d))
            blocks[i, 0:slots, :] = high
            blocks[i, slots:, :] = low


def early_kernel(grid, mine, slab, near, far, vecs, sums, blocks, feats):
    prepare(grid, mine, slab, feats, near, far, vecs, sums)
    pairs = [(c // SIDES, d // SIDES) for c, d in grid_pairs(*grid) if same_side((c, d)) and c % SIDES == 0]
    build_and_apply(pairs, blocks, *(views(ref) for ref in (near, far, vecs, sums)))


def late_kernel(
    grid, mine_slab, mine_near, mine_far, mine_vecs, mine_sums, mine_blocks, theirs, out_ref,
    slab, near, far, vecs, sums, sums_kept, resid, resid_half, blocks, feats
):
    rows, columns = grid
    cells, members, slots = rows * columns, HARD, slab.shape[2]
    prepare(grid, theirs, slab, feats, near, far, vecs, sums)
    sums_kept[...] = mine_sums[...]
    slab_of, sums_of = views(mine_slab, slab), views(sums_kept, sums)
    every = grid_pairs(rows, columns)
    early = [pair for pair in every if same_side(pair) and pair[0] % SIDES == 0]
    late = [pair for pair in every if pair not in early]
    build_and_apply(
        late, blocks, views(mine_near, near), views(mine_far, far), views(mine_vecs, vecs), sums_of
    )

    def applied(c):
        hard = slab_of[c][HARD:PLACE, :]
        full = slab_of[c][FULL : FULL + 1, :]
        right = slab_of[c][0:HARD, :]
        coupled = sums_of[c][...]
        image_s = hard * right + full * (coupled[0:8] + coupled[8:16])
        image_u = full * (hard + coupled[16:17])
        return hard, full, right, image_s, image_u

    shape = (members, slots)
    norm_s, prod_s, prod_u, total_s = (jnp.zeros(shape, jnp.float32) for _ in range(4))
    norm_u = jnp.zeros((1, slots), jnp.float32)
    for c in range(cells):
        hard, full, right, image_s, image_u = applied(c)
        norm_s += right * right
        norm_u += full * full
        prod_s += right * image_s
        prod_u += full * image_u
        total_s += right

    def over(values):
        return jnp.sum(values, axis=1, keepdims=True)

    both = lambda s, u: jnp.concatenate([s, jnp.broadcast_to(u, s.shape)], axis=0)
    norm0 = both(over(norm_s), over(norm_u))
    total0 = both(over(total_s), over(norm_u))
    alpha0 = norm0 / both(over(prod_s), over(prod_u))

    norm1, prod1, total1 = (jnp.zeros((2 * members, slots), jnp.float32) for _ in range(3))
    for c in range(cells):
        hard, full, right, image_s, image_u = applied(c)
        left = both(right, full) - alpha0 * jnp.concatenate([image_s, image_u], axis=0)
        resid[c] = left
        high, low = halves(left)
        lines = jnp.concatenate([high, low], axis=0)
        resid_half[c] = jnp.concatenate([lines, lines], axis=1)
        square = left * left
        norm1 += square
        prod1 += jnp.concatenate([hard, hard], axis=0) * square
        total1 += left

    for pair, block in [*zip(early, views(mine_blocks)), *zip(late, views(blocks))]:
        c, d = pair
        image = times(resid_half[c], block[...])
        part = (image[0:16] + image[16:32]) * resid[d]
        prod1 = prod1 + (part if c == d else 2.0 * part)

    norm1, prod1, total1 = over(norm1), over(prod1), over(total1)
    momentum = norm1 / norm0
    alpha1 = norm1 / (prod1 - momentum * norm1 / alpha0)
    weight0 = alpha0 + alpha1 * momentum
    totals = weight0 * total0 + alpha1 * total1
    multiplier = totals[0:members] / totals[members:]
    half, column = columns // SIDES, lax.axis_index("sub")
    side, h = lax.rem(column, SIDES), lax.div(column, SIDES)
    own = lax.axis_index("cell") * half + h + side * (half - 1 - 2 * h)
    right = both(mine_slab[own, 0:HARD, :], mine_slab[own, FULL : FULL + 1, :])
    answer = weight0 * right + alpha1 * resid[SIDES * own]
    out_ref[...] = answer[0:members] - multiplier * answer[members:]


def solve_only(mine, theirs):
    grid = rows, columns = lax.axis_size("cell"), lax.axis_size("sub")
    cells, slots = rows * columns, mine.shape[2]
    side = cells // SIDES
    every = grid_pairs(rows, columns)
    early = len([pair for pair in every if same_side(pair) and pair[0] % SIDES == 0])
    vmem = pl.BlockSpec(memory_space=pltpu.VMEM)
    limit = pltpu.CompilerParams(vmem_limit_bytes=32 << 20)
    kept = [
        pltpu.VMEM((side, ROWS, slots), jnp.float32),
        pltpu.VMEM((side, slots, FEATURES), jnp.bfloat16),
        pltpu.VMEM((side, FEATURES, 2 * slots), jnp.bfloat16),
        pltpu.VMEM((side, 32, 2 * slots), jnp.bfloat16),
        pltpu.VMEM((side, 32, slots), jnp.float32),
    ]
    feats = pltpu.VMEM((side, 2 * FEATURES, slots), jnp.float32)
    begun = pl.pallas_call(
        functools.partial(early_kernel, grid),
        out_shape=[*kept, pltpu.VMEM((early, 2 * slots, slots), jnp.bfloat16)],
        in_specs=[vmem],
        out_specs=[vmem] * (len(kept) + 1),
        scratch_shapes=[feats],
        compiler_params=limit,
        cost_estimate=pl.CostEstimate(flops=10**9, bytes_accessed=4 * 10**6, transcendentals=0),
        name="early",
    )(mine)
    return pl.pallas_call(
        functools.partial(late_kernel, grid),
        out_shape=jax.ShapeDtypeStruct((HARD, slots), jnp.float32),
        in_specs=[vmem] * (len(begun) + 1),
        out_specs=vmem,
        scratch_shapes=[
            *kept,
            pltpu.VMEM((side, 32, slots), jnp.float32),
            pltpu.VMEM((cells, 16, slots), jnp.float32),
            pltpu.VMEM((cells, 32, 2 * slots), jnp.bfloat16),
            pltpu.VMEM((len(every) - early, 2 * slots, slots), jnp.bfloat16),
            feats,
        ],
        compiler_params=limit,
        name="late",
    )(*begun, theirs)


def gathered(descriptors, positions, species, counts, w_in, b_in, w_hid, b_hid, w_out):
    rows, columns = lax.axis_size("cell"), lax.axis_size("sub")
    cells, slots, members = rows * columns, descriptors.shape[2], w_in.shape[0]
    vmem = pl.BlockSpec(memory_space=pltpu.VMEM)
    args = (
        descriptors.reshape(slots, -1), positions, species, counts, w_in, b_in, w_hid, b_hid, w_out
    )
    landed = [
        (pltpu.SMEM if arg is counts else pltpu.VMEM)(arg.shape, arg.dtype) for arg in args
    ]
    slabs = pl.pallas_call(
        slab_kernel,
        out_shape=pltpu.VMEM((cells // SIDES, ROWS, slots), jnp.float32),
        in_specs=[pl.BlockSpec(memory_space=pltpu.HBM)] * len(args),
        out_specs=vmem,
        scratch_shapes=landed + [pltpu.SemaphoreType.DMA((len(args),))],
        compiler_params=pltpu.CompilerParams(vmem_limit_bytes=60 << 20),
        name="slab",
    )(*args)
    groups = [
        [row * columns + column for row in range(rows) for column in range(side, columns, SIDES)]
        for side in range(SIDES)
    ]
    mine = lax.all_to_all(
        slabs, ("cell", "sub"), 0, 0, tiled=True, axis_index_groups=groups
    )
    theirs = lax.ppermute(mine, "sub", [(column, column ^ 1) for column in range(columns)])
    charges = solve_only(mine, theirs)
    return charges.reshape(members, 1, 1, slots)


def extended_2(shard, sides, width):
    for axis, dim in sides:
        size, length = (lax.axis_size(axis), shard.shape[dim])
        up = [(i, (i + 1) % size) for i in range(size - 1)]
        down = [(j, i) for i, j in up]
        last = lax.slice_in_dim(shard, length - width, length, axis=dim)
        leading = lax.slice_in_dim(shard, 0, width, axis=dim)
        before = lax.ppermute(last, axis, up)
        after = lax.ppermute(leading, axis, down)
        shard = jnp.concatenate([before, shard, after], axis=dim)
    return shard


def lookup(species, entries):
    choices_table = jnp.array(entries, jnp.float32)
    kinds = jnp.arange(4, dtype=jnp.int32)
    return jnp.sum((species[..., None] == kinds).astype(jnp.float32) * choices_table, axis=-1)


def coupling(own_atoms, far_atoms, self_cell):
    delta_a = own_atoms[0][..., :, None] - far_atoms[0][..., None, :]
    delta_b = own_atoms[1][..., :, None] - far_atoms[1][..., None, :]
    delta_c = own_atoms[2][..., :, None] - far_atoms[2][..., None, :]
    distance_sq = delta_a * delta_a + delta_b * delta_b + delta_c * delta_c
    radius = jnp.sqrt(distance_sq + 1e-06)
    pair_width = jnp.sqrt(own_atoms[3][..., :, None] ** 2 + far_atoms[3][..., None, :] ** 2)
    smooth_cut = (1.0 - jnp.minimum(distance_sq, 1.0)) ** 3
    kernel = 0.005 * smooth_cut * jax.scipy.special.erf(radius / pair_width) / radius
    kernel = kernel * own_atoms[4][..., :, None] * far_atoms[4][..., None, :]
    if self_cell:
        kernel = kernel * (1.0 - jnp.eye(kernel.shape[-1], dtype=jnp.float32))
    return kernel


def committee(flat_rows, w_in, b_in, w_hid, b_hid, w_out):

    def member_fn(weights):
        first_w, first_b, second_w, second_b, last_w = weights
        first = jnp.tanh(
            jnp.dot(flat_rows, first_w, preferred_element_type=jnp.float32) + first_b
        ).astype(jnp.bfloat16)
        second = jnp.tanh(
            jnp.dot(first, second_w, preferred_element_type=jnp.float32) + second_b
        ).astype(jnp.bfloat16)
        return jnp.dot(second, last_w.T, preferred_element_type=jnp.float32).T

    return lax.map(member_fn, (w_in, b_in, w_hid, b_hid, w_out))


def expand(values):
    return values[:, None, None, None]


def extend(vectors):
    return extended_2(vectors, (("cell", 1), ("sub", 2)), 1)


def two_products(residual, image_vec):
    return lax.psum(
        (
            jnp.sum(residual * residual, axis=(1, 2, 3)),
            jnp.sum(residual * image_vec, axis=(1, 2, 3)),
        ),
        ("cell", "sub"),
    )


def body(descriptors, positions, species, counts, w_in, b_in, w_hid, b_hid, w_out):
    rows_a, rows_b, slot_count, features = descriptors.shape
    members = w_in.shape[0]
    slot_iota = lax.broadcasted_iota(jnp.int32, (rows_a, rows_b, slot_count), 2)
    occupancy = (slot_iota < counts[:, :, None]).astype(jnp.float32)
    widths = lookup(species, (0.3, 0.4, 0.5, 0.35))
    shifts = lookup(species, (-0.8, 0.4, 1.2, -0.3))
    atom_data = jnp.stack([positions[0], positions[1], positions[2], widths, occupancy])
    extended = extended_2(atom_data, (("cell", 1), ("sub", 2)), 1)
    outputs = committee(descriptors.reshape(-1, features), w_in, b_in, w_hid, b_hid, w_out)
    electro = outputs[:, 0].reshape(members, rows_a, rows_b, slot_count) + shifts
    hardness = 2.5 + jax.nn.softplus(outputs[:, 1]).reshape(members, rows_a, rows_b, slot_count)
    right_side = jnp.concatenate([-electro * occupancy, jnp.broadcast_to(occupancy, electro.shape)])
    diagonal = jnp.concatenate([hardness, hardness])
    offsets = [(row_step, col_step) for row_step in (-1, 0, 1) for col_step in (-1, 0, 1)]

    def neighbours(grown, row_step, col_step):
        return grown[:, 1 + row_step : 1 + row_step + rows_a, 1 + col_step : 1 + col_step + rows_b]

    def block_for(row_step, col_step):
        return coupling(
            atom_data, neighbours(extended, row_step, col_step), row_step == 0 and col_step == 0
        )

    def operate(vectors):
        grown = extend(vectors)
        summed = diagonal * vectors
        for offset_number in range(9):
            row_step, col_step = offsets[offset_number]
            tile_block = block_for(row_step, col_step)
            summed = summed + jnp.einsum(
                "abij,rabj->rabi",
                tile_block,
                neighbours(grown, row_step, col_step),
                precision=lax.Precision.HIGHEST,
            )
        return summed

    solution = jnp.zeros_like(right_side)
    residual = right_side
    image_vec = operate(residual)
    norm_now, product = two_products(residual, image_vec)
    step_size = norm_now / product
    direction = residual
    along = image_vec
    for iteration in range(ITERS):
        solution = solution + expand(step_size) * direction
        residual = residual - expand(step_size) * along
        if iteration + 1 < ITERS:
            image_vec = operate(residual)
            norm_next, product = two_products(residual, image_vec)
            momentum = norm_next / norm_now
            step_size = norm_next / (product - momentum * norm_next / step_size)
            direction = residual + expand(momentum) * direction
            along = image_vec + expand(momentum) * along
            norm_now = norm_next
    source_part = solution[:members]
    unit_part = solution[members:]
    source_total, unit_total = lax.psum(
        (jnp.sum(source_part, axis=(1, 2, 3)), jnp.sum(unit_part, axis=(1, 2, 3))), ("cell", "sub")
    )
    multiplier = source_total / unit_total
    return source_part - expand(multiplier) * unit_part


def solution(mesh):
    placed = (
        P(("rep", "cell"), "sub", None, None),
        P(None, ("rep", "cell"), "sub", None),
        P(("rep", "cell"), "sub", None),
        P(("rep", "cell"), "sub"),
        P(),
        P(),
        P(),
        P(),
        P(),
    )
    rows, columns = mesh.shape["cell"], mesh.shape["sub"]
    return jax.shard_map(
        gathered if columns % SIDES == 0 and sum(pair_counts(rows, columns)) <= MOST_BLOCKS else body,
        mesh=mesh,
        in_specs=placed,
        out_specs=P(None, ("rep", "cell"), "sub", None),
        check_vma=False,
    )
```

```python
import functools

import jax
import jax.numpy as jnp
from jax import lax
from jax.experimental import pallas as pl
from jax.experimental.pallas import tpu as pltpu
from jax.sharding import PartitionSpec as P

ITERS = 2

ERF_SERIES = (
    1.1283791338788207,
    -0.37612471240078243,
    0.11282450088960652,
    -0.026825992168818515,
    0.005164800720113156,
    -0.0008061635856414364,
    9.67168369375208e-05,
    -7.756955478859171e-06,
    3.007955257374649e-07,
)

WIDTHS = (0.3, 0.4, 0.5, 0.35)

HARD, PLACE, KIND, FULL, ROWS = 8, 16, 19, 20, 24
SQUARE, FEATURES = 24, 48
OFFSETS = ((0, 0), (0, 1), (1, -1), (1, 0), (1, 1))
MOST_BLOCKS = 128
LAG = 8
AHEAD = 2
CHUNK = 16
GROUP = 8
SIDES = 2


def pair_counts(rows, cols):
    return [(rows - da) * (cols - abs(db)) for da, db in OFFSETS]


def choose(species, entries):
    value = jnp.full(species.shape, entries[3], jnp.float32)
    for kind in (2, 1, 0):
        value = jnp.where(species == kind, entries[kind], value)
    return value


def slab_kernel(*refs):
    sources, out_ref, landed, done = refs[:9], refs[9], refs[10:19], refs[19]
    members = sources[4].shape[0]
    copies = []

    def fetch(source, target):
        copy = pltpu.make_async_copy(source, target, done.at[len(copies)])
        copy.start()
        copies.append(copy)
        return copy

    desc_ref, pos_ref, species_ref, counts_ref, w_in, b_in, w_hid, b_hid, w_out = landed
    early = [fetch(sources[k], landed[k]) for k in (0, 5, 4)]
    middle = [fetch(sources[k], landed[k]) for k in (6, 7, 8)]
    late = [fetch(sources[k], landed[k]) for k in (1, 2, 3)]
    for copy in early:
        copy.wait()
    rows = desc_ref[...]
    slots = rows.shape[0]
    firsts, electro, raw = [], [], []
    for m in range(members):
        summed = jnp.dot(rows, w_in[m], preferred_element_type=jnp.float32) + b_in[m : m + 1, :]
        firsts.append(jnp.tanh(summed).astype(jnp.bfloat16))
    for copy in middle:
        copy.wait()
    for start in range(0, members, GROUP):
        group = range(start, start + GROUP)
        seconds = []
        for m in group:
            summed = jnp.dot(firsts[m], w_hid[m], preferred_element_type=jnp.float32)
            seconds.append(jnp.tanh(summed + b_hid[m : m + 1, :]).astype(jnp.bfloat16))
        for m in group:
            outputs = lax.dot_general(
                w_out[m],
                seconds[m - start],
                (((1,), (1,)), ((), ())),
                preferred_element_type=jnp.float32,
            )
            electro.append(outputs[0:1])
            raw.append(outputs[1:2])
    for copy in late:
        copy.wait()
    species = species_ref[0]
    slot_iota = lax.broadcasted_iota(jnp.int32, (1, slots), 1)
    occupancy = (slot_iota < counts_ref[0, 0]).astype(jnp.float32)
    shifts = choose(species, (-0.8, 0.4, 1.2, -0.3))
    raw = jnp.concatenate(raw, axis=0)
    hardness = 2.5 + (jnp.maximum(raw, 0.0) + jnp.log1p(jnp.exp(-jnp.abs(raw))))
    right = -(jnp.concatenate(electro, axis=0) + shifts) * occupancy
    atoms = jnp.concatenate(
        [pos_ref[0, 0], pos_ref[1, 0], pos_ref[2, 0], species.astype(jnp.float32), occupancy]
        + [jnp.zeros((1, slots), jnp.float32)] * (ROWS - FULL - 1),
        axis=0,
    )
    for peer in range(out_ref.shape[0]):
        out_ref[peer, 0:HARD, :] = right
        out_ref[peer, HARD:PLACE, :] = hardness
        out_ref[peer, PLACE:ROWS, :] = atoms


def thirds(values):
    high = values.astype(jnp.bfloat16).astype(jnp.float32)
    rest = values - high
    middle = rest.astype(jnp.bfloat16).astype(jnp.float32)
    return high, middle, rest - middle


def pair_features(places, kind):
    one, zero = jnp.ones_like(kind), jnp.zeros_like(kind)
    near, far = [], []
    for place in places:
        h, m, l = thirds(place)
        near += [h, h, m, m, h, l]
        far += [2.0 * v for v in (h, m, h, m, l, h)]
    norm = sum(place * place for place in places)
    near += [*thirds(norm), one, one, one]
    far += [-one, -one, -one, *thirds(1.0 - norm)]
    count = len(WIDTHS)
    near += [(kind == k).astype(jnp.float32) for k in range(count)] * 3
    pairs = [
        choose(kind, [(WIDTHS[k] ** 2 + other**2) ** -0.5 for other in WIDTHS])
        for k in range(count)
    ]
    far += [part for third in zip(*map(thirds, pairs)) for part in third]
    rest = [zero] * (FEATURES - len(near))
    return near + rest, far + rest


def pair_block(products, first_row, own):
    slots = products.shape[1] // 2
    left = jnp.maximum(products[:, 0:slots], 0.0)
    inv = products[:, slots:]
    y = (1.000001 - left) * (inv * inv)
    value = jnp.full_like(y, 0.005 * ERF_SERIES[-1])
    for term in ERF_SERIES[-2::-1]:
        value = value * y + 0.005 * term
    value = value * ((left * inv) * (left * left))
    if own:
        i = lax.broadcasted_iota(jnp.int32, value.shape, 0) + first_row
        j = lax.broadcasted_iota(jnp.int32, value.shape, 1)
        value = jnp.where(i == j, 0.0, value)
    return value


def times(vectors, block):
    return jnp.dot(vectors, block, preferred_element_type=jnp.float32)


def times_t(vectors, block):
    return lax.dot_general(
        vectors, block, (((1,), (1,)), ((), ())), preferred_element_type=jnp.float32
    )


def halves(values):
    high = values.astype(jnp.bfloat16)
    return high, (values - high.astype(jnp.float32)).astype(jnp.bfloat16)


def grid_pairs(rows, columns):
    pairs = []
    for a in range(rows):
        for da, db in OFFSETS:
            for column in range(max(0, -db), columns - max(0, db)):
                c = a * columns + column
                if a + da < rows:
                    pairs.append((c, c + da * columns + db))
    return pairs


def colour(c, columns):
    return (c // columns + c % columns) % SIDES


def split_pairs(rows, columns):
    every = grid_pairs(rows, columns)
    early = [pair for pair in every if not any(colour(c, columns) for c in pair)]
    return early, [pair for pair in every if pair not in early]


def items(ref):
    return [ref.at[k] for k in range(ref.shape[0])]


def views(columns, *sides):
    cells = SIDES * sides[0].shape[0]
    return [sides[colour(c, columns)].at[c // SIDES] for c in range(cells)]


def my_side():
    return lax.rem(lax.axis_index("cell") + lax.axis_index("sub"), SIDES)


def prepare(grid, source, slab, feats, near, far, vecs, sums):
    rows, columns = grid
    half, slots = columns // SIDES, slab.shape[2]
    side = my_side()
    for k in range(slab.shape[0]):
        h = k % half
        slab[k] = source[k + side * (half - 1 - 2 * h)]
    centres = (rows / 2, columns / 2, 0.5)
    rows_of = pair_features(
        [slab[:, PLACE + k, :] - centres[k] for k in range(3)], slab[:, KIND, :]
    )
    for k, row in enumerate(rows_of[0] + rows_of[1]):
        feats[:, k, :] = row
    blank = jnp.zeros((SQUARE, slots), jnp.float32)
    for c in range(slab.shape[0]):
        near[c] = feats[c, 0:FEATURES, :].T.astype(jnp.bfloat16)
        apart = jnp.concatenate([feats[c, FEATURES : FEATURES + SQUARE, :], blank], axis=0)
        spread = jnp.concatenate([blank, feats[c, FEATURES + SQUARE :, :]], axis=0)
        far[c] = jnp.concatenate([apart, spread], axis=1).astype(jnp.bfloat16)
        high, low = halves(slab[c, 0:HARD, :])
        full = slab[c, FULL : FULL + 1, :]
        row = lax.broadcasted_iota(jnp.int32, (16, slots), 0)
        lines = [high.astype(jnp.float32), low.astype(jnp.float32), jnp.where(row == 0, full, 0.0)]
        lines = jnp.concatenate(lines, axis=0).astype(jnp.bfloat16)
        vecs[c] = jnp.concatenate([lines, lines], axis=1)
        sums[c] = jnp.zeros_like(sums[c])


def build_and_apply(pairs, blocks, near, far, vecs, sums, products):
    slots = near[0].shape[0]
    lag = min(LAG, len(pairs) // 2)
    for i in range(len(pairs) + AHEAD + lag):
        if i < len(pairs):
            c, d = pairs[i]
            products[i % (AHEAD + 1)] = times(near[c][...], far[d][...])
        k = i - AHEAD - lag
        if k >= 0:
            c, d = pairs[k]
            block = blocks[k]
            image = times(vecs[c][...], block)
            if c != d:
                wide = jnp.concatenate([block[0:slots], block[slots:]], axis=1)
                sums[c][...] += times_t(vecs[d][...], wide)
            sums[d][...] += image
        k = i - AHEAD
        if 0 <= k < len(pairs):
            c, d = pairs[k]
            for row in range(0, slots, CHUNK):
                part = products[k % (AHEAD + 1), row : row + CHUNK, :]
                high, low = halves(pair_block(part, row, c == d))
                blocks[k, row : row + CHUNK, :] = high
                blocks[k, slots + row : slots + row + CHUNK, :] = low


def early_kernel(grid, mine, slab, near, far, vecs, sums, blocks, feats, products):
    prepare(grid, mine, slab, feats, near, far, vecs, sums)
    pairs = [(c // SIDES, d // SIDES) for c, d in split_pairs(*grid)[0]]
    build_and_apply(pairs, blocks, *map(items, (near, far, vecs, sums)), products)


def late_kernel(
    grid, mine_slab, mine_near, mine_far, mine_vecs, mine_sums, mine_blocks, theirs, out_ref,
    slab, near, far, vecs, sums, sums_kept, resid, resid_half, blocks, feats, products
):
    rows, columns = grid
    cells, members, slots = rows * columns, HARD, slab.shape[2]
    prepare(grid, theirs, slab, feats, near, far, vecs, sums)
    sums_kept[...] = mine_sums[...]
    slab_of, sums_of = views(columns, mine_slab, slab), views(columns, sums_kept, sums)
    early, late = split_pairs(rows, columns)
    held = ((mine_near, near), (mine_far, far), (mine_vecs, vecs))
    sides = [views(columns, *pair) for pair in held]
    build_and_apply(late, blocks, *sides, sums_of, products)

    def applied(c):
        hard = slab_of[c][HARD:PLACE, :]
        full = slab_of[c][FULL : FULL + 1, :]
        right = slab_of[c][0:HARD, :]
        coupled = sums_of[c][...]
        image_s = hard * right + full * (coupled[0:8] + coupled[8:16])
        image_u = full * (hard + coupled[16:17])
        return hard, full, right, image_s, image_u

    shape = (members, slots)
    norm_s, prod_s, prod_u, total_s = (jnp.zeros(shape, jnp.float32) for _ in range(4))
    norm_u = jnp.zeros((1, slots), jnp.float32)
    for c in range(cells):
        hard, full, right, image_s, image_u = applied(c)
        norm_s += right * right
        norm_u += full * full
        prod_s += right * image_s
        prod_u += full * image_u
        total_s += right

    def over(values):
        return jnp.sum(values, axis=1, keepdims=True)

    both = lambda s, u: jnp.concatenate([s, jnp.broadcast_to(u, s.shape)], axis=0)
    norm0 = both(over(norm_s), over(norm_u))
    total0 = both(over(total_s), over(norm_u))
    alpha0 = norm0 / both(over(prod_s), over(prod_u))

    norm1, prod1, total1 = (jnp.zeros((2 * members, slots), jnp.float32) for _ in range(3))
    for c in range(cells):
        hard, full, right, image_s, image_u = applied(c)
        left = both(right, full) - alpha0 * jnp.concatenate([image_s, image_u], axis=0)
        resid[c] = left
        high, low = halves(left)
        lines = jnp.concatenate([high, low], axis=0)
        resid_half[c] = jnp.concatenate([lines, lines], axis=1)
        square = left * left
        norm1 += square
        prod1 += jnp.concatenate([hard, hard], axis=0) * square
        total1 += left

    for pair, block in [*zip(early, items(mine_blocks)), *zip(late, items(blocks))]:
        c, d = pair
        image = times(resid_half[c], block[...])
        part = (image[0:16] + image[16:32]) * resid[d]
        prod1 = prod1 + (part if c == d else 2.0 * part)

    norm1, prod1, total1 = over(norm1), over(prod1), over(total1)
    momentum = norm1 / norm0
    alpha1 = norm1 / (prod1 - momentum * norm1 / alpha0)
    weight0 = alpha0 + alpha1 * momentum
    totals = weight0 * total0 + alpha1 * total1
    multiplier = totals[0:members] / totals[members:]
    half, row, side = columns // SIDES, lax.axis_index("cell"), my_side()
    h = lax.div(lax.axis_index("sub"), SIDES)
    h = h + side * (half - 1 - 2 * h)
    own, cell = row * half + h, row * columns + SIDES * h + lax.rem(row, SIDES)
    right = both(mine_slab[own, 0:HARD, :], mine_slab[own, FULL : FULL + 1, :])
    answer = weight0 * right + alpha1 * resid[cell]
    out_ref[...] = answer[0:members] - multiplier * answer[members:]


def solve_only(mine, theirs):
    grid = rows, columns = lax.axis_size("cell"), lax.axis_size("sub")
    cells, slots = rows * columns, mine.shape[2]
    side = cells // SIDES
    early, late = map(len, split_pairs(rows, columns))
    vmem = pl.BlockSpec(memory_space=pltpu.VMEM)
    limit = pltpu.CompilerParams(vmem_limit_bytes=32 << 20)
    kept = [
        pltpu.VMEM((side, ROWS, slots), jnp.float32),
        pltpu.VMEM((side, slots, FEATURES), jnp.bfloat16),
        pltpu.VMEM((side, FEATURES, 2 * slots), jnp.bfloat16),
        pltpu.VMEM((side, 32, 2 * slots), jnp.bfloat16),
        pltpu.VMEM((side, 32, slots), jnp.float32),
    ]
    work = [
        pltpu.VMEM((side, 2 * FEATURES, slots), jnp.float32),
        pltpu.VMEM((AHEAD + 1, slots, 2 * slots), jnp.float32),
    ]
    begun = pl.pallas_call(
        functools.partial(early_kernel, grid),
        out_shape=[*kept, pltpu.VMEM((early, 2 * slots, slots), jnp.bfloat16)],
        in_specs=[vmem],
        out_specs=[vmem] * (len(kept) + 1),
        scratch_shapes=work,
        compiler_params=limit,
        cost_estimate=pl.CostEstimate(flops=10**9, bytes_accessed=4 * 10**6, transcendentals=0),
        name="early",
    )(mine)
    return pl.pallas_call(
        functools.partial(late_kernel, grid),
        out_shape=jax.ShapeDtypeStruct((HARD, slots), jnp.float32),
        in_specs=[vmem] * (len(begun) + 1),
        out_specs=vmem,
        scratch_shapes=[
            *kept,
            pltpu.VMEM((side, 32, slots), jnp.float32),
            pltpu.VMEM((cells, 16, slots), jnp.float32),
            pltpu.VMEM((cells, 32, 2 * slots), jnp.bfloat16),
            pltpu.VMEM((late, 2 * slots, slots), jnp.bfloat16),
            *work,
        ],
        compiler_params=limit,
        name="late",
    )(*begun, theirs)


def gathered(descriptors, positions, species, counts, w_in, b_in, w_hid, b_hid, w_out):
    rows, columns = lax.axis_size("cell"), lax.axis_size("sub")
    cells, slots, members = rows * columns, descriptors.shape[2], w_in.shape[0]
    vmem = pl.BlockSpec(memory_space=pltpu.VMEM)
    args = (
        descriptors.reshape(slots, -1), positions, species, counts, w_in, b_in, w_hid, b_hid, w_out
    )
    landed = [
        (pltpu.SMEM if arg is counts else pltpu.VMEM)(arg.shape, arg.dtype) for arg in args
    ]
    slabs = pl.pallas_call(
        slab_kernel,
        out_shape=pltpu.VMEM((cells // SIDES, ROWS, slots), jnp.float32),
        in_specs=[pl.BlockSpec(memory_space=pltpu.HBM)] * len(args),
        out_specs=vmem,
        scratch_shapes=landed + [pltpu.SemaphoreType.DMA((len(args),))],
        compiler_params=pltpu.CompilerParams(vmem_limit_bytes=60 << 20),
        name="slab",
    )(*args)
    groups = [
        [c for c in range(cells) if colour(c, columns) == side] for side in range(SIDES)
    ]
    mine = lax.all_to_all(
        slabs, ("cell", "sub"), 0, 0, tiled=True, axis_index_groups=groups
    )
    theirs = lax.ppermute(mine, "sub", [(column, column ^ 1) for column in range(columns)])
    charges = solve_only(mine, theirs)
    return charges.reshape(members, 1, 1, slots)


def extended_2(shard, sides, width):
    for axis, dim in sides:
        size, length = (lax.axis_size(axis), shard.shape[dim])
        up = [(i, (i + 1) % size) for i in range(size - 1)]
        down = [(j, i) for i, j in up]
        last = lax.slice_in_dim(shard, length - width, length, axis=dim)
        leading = lax.slice_in_dim(shard, 0, width, axis=dim)
        before = lax.ppermute(last, axis, up)
        after = lax.ppermute(leading, axis, down)
        shard = jnp.concatenate([before, shard, after], axis=dim)
    return shard


def lookup(species, entries):
    choices_table = jnp.array(entries, jnp.float32)
    kinds = jnp.arange(4, dtype=jnp.int32)
    return jnp.sum((species[..., None] == kinds).astype(jnp.float32) * choices_table, axis=-1)


def coupling(own_atoms, far_atoms, self_cell):
    delta_a = own_atoms[0][..., :, None] - far_atoms[0][..., None, :]
    delta_b = own_atoms[1][..., :, None] - far_atoms[1][..., None, :]
    delta_c = own_atoms[2][..., :, None] - far_atoms[2][..., None, :]
    distance_sq = delta_a * delta_a + delta_b * delta_b + delta_c * delta_c
    radius = jnp.sqrt(distance_sq + 1e-06)
    pair_width = jnp.sqrt(own_atoms[3][..., :, None] ** 2 + far_atoms[3][..., None, :] ** 2)
    smooth_cut = (1.0 - jnp.minimum(distance_sq, 1.0)) ** 3
    kernel = 0.005 * smooth_cut * jax.scipy.special.erf(radius / pair_width) / radius
    kernel = kernel * own_atoms[4][..., :, None] * far_atoms[4][..., None, :]
    if self_cell:
        kernel = kernel * (1.0 - jnp.eye(kernel.shape[-1], dtype=jnp.float32))
    return kernel


def committee(flat_rows, w_in, b_in, w_hid, b_hid, w_out):

    def member_fn(weights):
        first_w, first_b, second_w, second_b, last_w = weights
        first = jnp.tanh(
            jnp.dot(flat_rows, first_w, preferred_element_type=jnp.float32) + first_b
        ).astype(jnp.bfloat16)
        second = jnp.tanh(
            jnp.dot(first, second_w, preferred_element_type=jnp.float32) + second_b
        ).astype(jnp.bfloat16)
        return jnp.dot(second, last_w.T, preferred_element_type=jnp.float32).T

    return lax.map(member_fn, (w_in, b_in, w_hid, b_hid, w_out))


def expand(values):
    return values[:, None, None, None]


def extend(vectors):
    return extended_2(vectors, (("cell", 1), ("sub", 2)), 1)


def two_products(residual, image_vec):
    return lax.psum(
        (
            jnp.sum(residual * residual, axis=(1, 2, 3)),
            jnp.sum(residual * image_vec, axis=(1, 2, 3)),
        ),
        ("cell", "sub"),
    )


def body(descriptors, positions, species, counts, w_in, b_in, w_hid, b_hid, w_out):
    rows_a, rows_b, slot_count, features = descriptors.shape
    members = w_in.shape[0]
    slot_iota = lax.broadcasted_iota(jnp.int32, (rows_a, rows_b, slot_count), 2)
    occupancy = (slot_iota < counts[:, :, None]).astype(jnp.float32)
    widths = lookup(species, (0.3, 0.4, 0.5, 0.35))
    shifts = lookup(species, (-0.8, 0.4, 1.2, -0.3))
    atom_data = jnp.stack([positions[0], positions[1], positions[2], widths, occupancy])
    extended = extended_2(atom_data, (("cell", 1), ("sub", 2)), 1)
    outputs = committee(descriptors.reshape(-1, features), w_in, b_in, w_hid, b_hid, w_out)
    electro = outputs[:, 0].reshape(members, rows_a, rows_b, slot_count) + shifts
    hardness = 2.5 + jax.nn.softplus(outputs[:, 1]).reshape(members, rows_a, rows_b, slot_count)
    right_side = jnp.concatenate([-electro * occupancy, jnp.broadcast_to(occupancy, electro.shape)])
    diagonal = jnp.concatenate([hardness, hardness])
    offsets = [(row_step, col_step) for row_step in (-1, 0, 1) for col_step in (-1, 0, 1)]

    def neighbours(grown, row_step, col_step):
        return grown[:, 1 + row_step : 1 + row_step + rows_a, 1 + col_step : 1 + col_step + rows_b]

    def block_for(row_step, col_step):
        return coupling(
            atom_data, neighbours(extended, row_step, col_step), row_step == 0 and col_step == 0
        )

    def operate(vectors):
        grown = extend(vectors)
        summed = diagonal * vectors
        for offset_number in range(9):
            row_step, col_step = offsets[offset_number]
            tile_block = block_for(row_step, col_step)
            summed = summed + jnp.einsum(
                "abij,rabj->rabi",
                tile_block,
                neighbours(grown, row_step, col_step),
                precision=lax.Precision.HIGHEST,
            )
        return summed

    solution = jnp.zeros_like(right_side)
    residual = right_side
    image_vec = operate(residual)
    norm_now, product = two_products(residual, image_vec)
    step_size = norm_now / product
    direction = residual
    along = image_vec
    for iteration in range(ITERS):
        solution = solution + expand(step_size) * direction
        residual = residual - expand(step_size) * along
        if iteration + 1 < ITERS:
            image_vec = operate(residual)
            norm_next, product = two_products(residual, image_vec)
            momentum = norm_next / norm_now
            step_size = norm_next / (product - momentum * norm_next / step_size)
            direction = residual + expand(momentum) * direction
            along = image_vec + expand(momentum) * along
            norm_now = norm_next
    source_part = solution[:members]
    unit_part = solution[members:]
    source_total, unit_total = lax.psum(
        (jnp.sum(source_part, axis=(1, 2, 3)), jnp.sum(unit_part, axis=(1, 2, 3))), ("cell", "sub")
    )
    multiplier = source_total / unit_total
    return source_part - expand(multiplier) * unit_part


def solution(mesh):
    placed = (
        P(("rep", "cell"), "sub", None, None),
        P(None, ("rep", "cell"), "sub", None),
        P(("rep", "cell"), "sub", None),
        P(("rep", "cell"), "sub"),
        P(),
        P(),
        P(),
        P(),
        P(),
    )
    rows, columns = mesh.shape["cell"], mesh.shape["sub"]
    return jax.shard_map(
        gathered if columns % SIDES == 0 and sum(pair_counts(rows, columns)) <= MOST_BLOCKS else body,
        mesh=mesh,
        in_specs=placed,
        out_specs=P(None, ("rep", "cell"), "sub", None),
        check_vma=False,
    )
```

```python
import functools

import jax
import jax.numpy as jnp
from jax import lax
from jax.experimental import pallas as pl
from jax.experimental.pallas import tpu as pltpu
from jax.sharding import PartitionSpec as P

ITERS = 2

ERF_SERIES = (
    1.1283791338788207,
    -0.37612471240078243,
    0.11282450088960652,
    -0.026825992168818515,
    0.005164800720113156,
    -0.0008061635856414364,
    9.67168369375208e-05,
    -7.756955478859171e-06,
    3.007955257374649e-07,
)

WIDTHS = (0.3, 0.4, 0.5, 0.35)

HARD, PLACE, KIND, FULL, ROWS = 8, 16, 19, 20, 24
SQUARE, FEATURES = 24, 48
OFFSETS = ((0, 0), (0, 1), (1, -1), (1, 0), (1, 1))
MOST_BLOCKS = 128
LAG = 8
AHEAD = 2
CHUNK = 16
GROUP = 8
SIDES = 2


def pair_counts(rows, cols):
    return [(rows - da) * (cols - abs(db)) for da, db in OFFSETS]


def choose(species, entries):
    value = jnp.full(species.shape, entries[3], jnp.float32)
    for kind in (2, 1, 0):
        value = jnp.where(species == kind, entries[kind], value)
    return value


def slab_kernel(*refs):
    sources, out_ref, landed, done = refs[:9], refs[9], refs[10:19], refs[19]
    members = sources[4].shape[0]
    copies = []

    def fetch(source, target):
        copy = pltpu.make_async_copy(source, target, done.at[len(copies)])
        copy.start()
        copies.append(copy)
        return copy

    desc_ref, pos_ref, species_ref, counts_ref, w_in, b_in, w_hid, b_hid, w_out = landed
    early = [fetch(sources[k], landed[k]) for k in (0, 5, 4)]
    middle = [fetch(sources[k], landed[k]) for k in (6, 7, 8)]
    late = [fetch(sources[k], landed[k]) for k in (1, 2, 3)]
    for copy in early:
        copy.wait()
    rows = desc_ref[...]
    slots = rows.shape[0]
    firsts, electro, raw = [], [], []
    for m in range(members):
        summed = jnp.dot(rows, w_in[m], preferred_element_type=jnp.float32) + b_in[m : m + 1, :]
        firsts.append(jnp.tanh(summed).astype(jnp.bfloat16))
    for copy in middle:
        copy.wait()
    for start in range(0, members, GROUP):
        group = range(start, start + GROUP)
        seconds = []
        for m in group:
            summed = jnp.dot(firsts[m], w_hid[m], preferred_element_type=jnp.float32)
            seconds.append(jnp.tanh(summed + b_hid[m : m + 1, :]).astype(jnp.bfloat16))
        for m in group:
            outputs = lax.dot_general(
                w_out[m],
                seconds[m - start],
                (((1,), (1,)), ((), ())),
                preferred_element_type=jnp.float32,
            )
            electro.append(outputs[0:1])
            raw.append(outputs[1:2])
    for copy in late:
        copy.wait()
    species = species_ref[0]
    slot_iota = lax.broadcasted_iota(jnp.int32, (1, slots), 1)
    occupancy = (slot_iota < counts_ref[0, 0]).astype(jnp.float32)
    shifts = choose(species, (-0.8, 0.4, 1.2, -0.3))
    raw = jnp.concatenate(raw, axis=0)
    hardness = 2.5 + (jnp.maximum(raw, 0.0) + jnp.log1p(jnp.exp(-jnp.abs(raw))))
    right = -(jnp.concatenate(electro, axis=0) + shifts) * occupancy
    atoms = jnp.concatenate(
        [pos_ref[0, 0], pos_ref[1, 0], pos_ref[2, 0], species.astype(jnp.float32), occupancy]
        + [jnp.zeros((1, slots), jnp.float32)] * (ROWS - FULL - 1),
        axis=0,
    )
    for peer in range(out_ref.shape[0]):
        out_ref[peer, 0:HARD, :] = right
        out_ref[peer, HARD:PLACE, :] = hardness
        out_ref[peer, PLACE:ROWS, :] = atoms


def thirds(values):
    high = values.astype(jnp.bfloat16).astype(jnp.float32)
    rest = values - high
    middle = rest.astype(jnp.bfloat16).astype(jnp.float32)
    return high, middle, rest - middle


def pair_features(places, kind):
    one, zero = jnp.ones_like(kind), jnp.zeros_like(kind)
    near, far = [], []
    for place in places:
        h, m, l = thirds(place)
        near += [h, h, m, m, h, l]
        far += [2.0 * v for v in (h, m, h, m, l, h)]
    norm = sum(place * place for place in places)
    near += [*thirds(norm), one, one, one]
    far += [-one, -one, -one, *thirds(1.0 - norm)]
    count = len(WIDTHS)
    near += [(kind == k).astype(jnp.float32) for k in range(count)] * 3
    pairs = [
        choose(kind, [(WIDTHS[k] ** 2 + other**2) ** -0.5 for other in WIDTHS])
        for k in range(count)
    ]
    far += [part for third in zip(*map(thirds, pairs)) for part in third]
    rest = [zero] * (FEATURES - len(near))
    return near + rest, far + rest


def pair_block(products, first_row, own):
    slots = products.shape[1] // 2
    left = jnp.maximum(products[:, 0:slots], 0.0)
    inv = products[:, slots:]
    y = (1.000001 - left) * (inv * inv)
    value = jnp.full_like(y, 0.005 * ERF_SERIES[-1])
    for term in ERF_SERIES[-2::-1]:
        value = value * y + 0.005 * term
    value = value * ((left * inv) * (left * left))
    if own:
        i = lax.broadcasted_iota(jnp.int32, value.shape, 0) + first_row
        j = lax.broadcasted_iota(jnp.int32, value.shape, 1)
        value = jnp.where(i == j, 0.0, value)
    return value


def times(vectors, block):
    return jnp.dot(vectors, block, preferred_element_type=jnp.float32)


def times_t(vectors, block):
    return lax.dot_general(
        vectors, block, (((1,), (1,)), ((), ())), preferred_element_type=jnp.float32
    )


def halves(values):
    high = values.astype(jnp.bfloat16)
    return high, (values - high.astype(jnp.float32)).astype(jnp.bfloat16)


def grid_pairs(rows, columns):
    pairs = []
    for a in range(rows):
        for da, db in OFFSETS:
            for column in range(max(0, -db), columns - max(0, db)):
                c = a * columns + column
                if a + da < rows:
                    pairs.append((c, c + da * columns + db))
    return pairs


def colour(c, columns):
    return (c // columns + c % columns) % SIDES


def split_pairs(rows, columns):
    every = grid_pairs(rows, columns)
    early = [pair for pair in every if not any(colour(c, columns) for c in pair)]
    return early, [pair for pair in every if pair not in early]


def items(ref):
    return [ref.at[k] for k in range(ref.shape[0])]


def views(columns, *sides):
    cells = SIDES * sides[0].shape[0]
    return [sides[colour(c, columns)].at[c // SIDES] for c in range(cells)]


def my_side():
    return lax.rem(lax.axis_index("cell") + lax.axis_index("sub"), SIDES)


def prepare(grid, source, slab, feats, near, far, vecs, sums):
    rows, columns = grid
    half, slots = columns // SIDES, slab.shape[2]
    side = my_side()
    for k in range(slab.shape[0]):
        h = k % half
        slab[k] = source[k + side * (half - 1 - 2 * h)]
    centres = (rows / 2, columns / 2, 0.5)
    rows_of = pair_features(
        [slab[:, PLACE + k, :] - centres[k] for k in range(3)], slab[:, KIND, :]
    )
    for k, row in enumerate(rows_of[0] + rows_of[1]):
        feats[:, k, :] = row
    blank = jnp.zeros((SQUARE, slots), jnp.float32)
    for c in range(slab.shape[0]):
        near[c] = feats[c, 0:FEATURES, :].T.astype(jnp.bfloat16)
        apart = jnp.concatenate([feats[c, FEATURES : FEATURES + SQUARE, :], blank], axis=0)
        spread = jnp.concatenate([blank, feats[c, FEATURES + SQUARE :, :]], axis=0)
        far[c] = jnp.concatenate([apart, spread], axis=1).astype(jnp.bfloat16)
        high, low = halves(slab[c, 0:HARD, :])
        full = slab[c, FULL : FULL + 1, :]
        row = lax.broadcasted_iota(jnp.int32, (16, slots), 0)
        lines = [high.astype(jnp.float32), low.astype(jnp.float32), jnp.where(row == 0, full, 0.0)]
        lines = jnp.concatenate(lines, axis=0).astype(jnp.bfloat16)
        vecs[c] = jnp.concatenate([lines, lines], axis=1)
        sums[c] = jnp.zeros_like(sums[c])


def build_and_apply(pairs, blocks, near, far, vecs, sums, products):
    slots = near[0].shape[0]
    lag = min(LAG, len(pairs) // 2)
    for i in range(len(pairs) + AHEAD + lag):
        if i < len(pairs):
            c, d = pairs[i]
            products[i % (AHEAD + 1)] = times(near[c][...], far[d][...])
        k = i - AHEAD - lag
        if k >= 0:
            c, d = pairs[k]
            block = blocks[k]
            image = times(vecs[c][...], block)
            if c != d:
                wide = jnp.concatenate([block[0:slots], block[slots:]], axis=1)
                sums[c][...] += times_t(vecs[d][...], wide)
            sums[d][...] += image
        k = i - AHEAD
        if 0 <= k < len(pairs):
            c, d = pairs[k]
            for row in range(0, slots, CHUNK):
                part = products[k % (AHEAD + 1), row : row + CHUNK, :]
                high, low = halves(pair_block(part, row, c == d))
                blocks[k, row : row + CHUNK, :] = high
                blocks[k, slots + row : slots + row + CHUNK, :] = low


def early_kernel(grid, mine, slab, near, far, vecs, sums, blocks, feats, products):
    prepare(grid, mine, slab, feats, near, far, vecs, sums)
    pairs = [(c // SIDES, d // SIDES) for c, d in split_pairs(*grid)[0]]
    build_and_apply(pairs, blocks, *map(items, (near, far, vecs, sums)), products)


def late_kernel(
    grid, mine_slab, mine_near, mine_far, mine_vecs, mine_sums, mine_blocks, theirs, out_ref,
    slab, near, far, vecs, sums, sums_kept, resid, resid_half, blocks, feats, products
):
    rows, columns = grid
    cells, members, slots = rows * columns, HARD, slab.shape[2]
    prepare(grid, theirs, slab, feats, near, far, vecs, sums)
    sums_kept[...] = mine_sums[...]
    slab_of, sums_of = views(columns, mine_slab, slab), views(columns, sums_kept, sums)
    early, late = split_pairs(rows, columns)
    held = ((mine_near, near), (mine_far, far), (mine_vecs, vecs))
    sides = [views(columns, *pair) for pair in held]
    build_and_apply(late, blocks, *sides, sums_of, products)

    def applied(c):
        hard = slab_of[c][HARD:PLACE, :]
        full = slab_of[c][FULL : FULL + 1, :]
        right = slab_of[c][0:HARD, :]
        coupled = sums_of[c][...]
        image_s = hard * right + full * (coupled[0:8] + coupled[8:16])
        image_u = full * (hard + coupled[16:17])
        return hard, full, right, image_s, image_u

    shape = (members, slots)
    norm_s, prod_s, prod_u, total_s = (jnp.zeros(shape, jnp.float32) for _ in range(4))
    norm_u = jnp.zeros((1, slots), jnp.float32)
    for c in range(cells):
        hard, full, right, image_s, image_u = applied(c)
        resid[c] = jnp.concatenate([image_s, image_u], axis=0)
        norm_s += right * right
        norm_u += full * full
        prod_s += right * image_s
        prod_u += full * image_u
        total_s += right

    def over(values):
        return jnp.sum(values, axis=1, keepdims=True)

    both = lambda s, u: jnp.concatenate([s, jnp.broadcast_to(u, s.shape)], axis=0)
    norm0 = both(over(norm_s), over(norm_u))
    total0 = both(over(total_s), over(norm_u))
    alpha0 = norm0 / both(over(prod_s), over(prod_u))

    norm1, prod1, total1 = (jnp.zeros((2 * members, slots), jnp.float32) for _ in range(3))
    for c in range(cells):
        hard = slab_of[c][HARD:PLACE, :]
        right, full = slab_of[c][0:HARD, :], slab_of[c][FULL : FULL + 1, :]
        left = both(right, full) - alpha0 * resid[c]
        resid[c] = left
        high, low = halves(left)
        lines = jnp.concatenate([high, low], axis=0)
        resid_half[c] = jnp.concatenate([lines, lines], axis=1)
        square = left * left
        norm1 += square
        prod1 += jnp.concatenate([hard, hard], axis=0) * square
        total1 += left

    stored = dict(zip(early + late, items(mine_blocks) + items(blocks)))
    for c in range(cells):
        others = [d for b, d in stored if b == c]
        for first in range(0, len(others), 2):
            some = others[first : first + 2]
            image = times(resid_half[c], jnp.concatenate([stored[c, d][...] for d in some], axis=1))
            for k, d in enumerate(some):
                part = image[:, k * slots : (k + 1) * slots]
                part = (part[0:16] + part[16:32]) * resid[d]
                prod1 = prod1 + (part if c == d else 2.0 * part)

    norm1, prod1, total1 = over(norm1), over(prod1), over(total1)
    momentum = norm1 / norm0
    alpha1 = norm1 / (prod1 - momentum * norm1 / alpha0)
    weight0 = alpha0 + alpha1 * momentum
    totals = weight0 * total0 + alpha1 * total1
    multiplier = totals[0:members] / totals[members:]
    half, row, side = columns // SIDES, lax.axis_index("cell"), my_side()
    h = lax.div(lax.axis_index("sub"), SIDES)
    h = h + side * (half - 1 - 2 * h)
    own, cell = row * half + h, row * columns + SIDES * h + lax.rem(row, SIDES)
    right = both(mine_slab[own, 0:HARD, :], mine_slab[own, FULL : FULL + 1, :])
    answer = weight0 * right + alpha1 * resid[cell]
    out_ref[...] = answer[0:members] - multiplier * answer[members:]


def solve_only(mine, theirs):
    grid = rows, columns = lax.axis_size("cell"), lax.axis_size("sub")
    cells, slots = rows * columns, mine.shape[2]
    side = cells // SIDES
    early, late = map(len, split_pairs(rows, columns))
    vmem = pl.BlockSpec(memory_space=pltpu.VMEM)
    limit = pltpu.CompilerParams(vmem_limit_bytes=32 << 20)
    kept = [
        pltpu.VMEM((side, ROWS, slots), jnp.float32),
        pltpu.VMEM((side, slots, FEATURES), jnp.bfloat16),
        pltpu.VMEM((side, FEATURES, 2 * slots), jnp.bfloat16),
        pltpu.VMEM((side, 32, 2 * slots), jnp.bfloat16),
        pltpu.VMEM((side, 32, slots), jnp.float32),
    ]
    work = [
        pltpu.VMEM((side, 2 * FEATURES, slots), jnp.float32),
        pltpu.VMEM((AHEAD + 1, slots, 2 * slots), jnp.float32),
    ]
    begun = pl.pallas_call(
        functools.partial(early_kernel, grid),
        out_shape=[*kept, pltpu.VMEM((early, 2 * slots, slots), jnp.bfloat16)],
        in_specs=[vmem],
        out_specs=[vmem] * (len(kept) + 1),
        scratch_shapes=work,
        compiler_params=limit,
        cost_estimate=pl.CostEstimate(flops=10**9, bytes_accessed=4 * 10**6, transcendentals=0),
        name="early",
    )(mine)
    return pl.pallas_call(
        functools.partial(late_kernel, grid),
        out_shape=jax.ShapeDtypeStruct((HARD, slots), jnp.float32),
        in_specs=[vmem] * (len(begun) + 1),
        out_specs=vmem,
        scratch_shapes=[
            *kept,
            pltpu.VMEM((side, 32, slots), jnp.float32),
            pltpu.VMEM((cells, 16, slots), jnp.float32),
            pltpu.VMEM((cells, 32, 2 * slots), jnp.bfloat16),
            pltpu.VMEM((late, 2 * slots, slots), jnp.bfloat16),
            *work,
        ],
        compiler_params=limit,
        name="late",
    )(*begun, theirs)


def gathered(descriptors, positions, species, counts, w_in, b_in, w_hid, b_hid, w_out):
    rows, columns = lax.axis_size("cell"), lax.axis_size("sub")
    cells, slots, members = rows * columns, descriptors.shape[2], w_in.shape[0]
    vmem = pl.BlockSpec(memory_space=pltpu.VMEM)
    args = (
        descriptors.reshape(slots, -1), positions, species, counts, w_in, b_in, w_hid, b_hid, w_out
    )
    landed = [
        (pltpu.SMEM if arg is counts else pltpu.VMEM)(arg.shape, arg.dtype) for arg in args
    ]
    slabs = pl.pallas_call(
        slab_kernel,
        out_shape=pltpu.VMEM((cells // SIDES, ROWS, slots), jnp.float32),
        in_specs=[pl.BlockSpec(memory_space=pltpu.HBM)] * len(args),
        out_specs=vmem,
        scratch_shapes=landed + [pltpu.SemaphoreType.DMA((len(args),))],
        compiler_params=pltpu.CompilerParams(vmem_limit_bytes=60 << 20),
        name="slab",
    )(*args)
    groups = [
        [c for c in range(cells) if colour(c, columns) == side] for side in range(SIDES)
    ]
    mine = lax.all_to_all(
        slabs, ("cell", "sub"), 0, 0, tiled=True, axis_index_groups=groups
    )
    theirs = lax.ppermute(mine, "sub", [(column, column ^ 1) for column in range(columns)])
    charges = solve_only(mine, theirs)
    return charges.reshape(members, 1, 1, slots)


def extended_2(shard, sides, width):
    for axis, dim in sides:
        size, length = (lax.axis_size(axis), shard.shape[dim])
        up = [(i, (i + 1) % size) for i in range(size - 1)]
        down = [(j, i) for i, j in up]
        last = lax.slice_in_dim(shard, length - width, length, axis=dim)
        leading = lax.slice_in_dim(shard, 0, width, axis=dim)
        before = lax.ppermute(last, axis, up)
        after = lax.ppermute(leading, axis, down)
        shard = jnp.concatenate([before, shard, after], axis=dim)
    return shard


def lookup(species, entries):
    choices_table = jnp.array(entries, jnp.float32)
    kinds = jnp.arange(4, dtype=jnp.int32)
    return jnp.sum((species[..., None] == kinds).astype(jnp.float32) * choices_table, axis=-1)


def coupling(own_atoms, far_atoms, self_cell):
    delta_a = own_atoms[0][..., :, None] - far_atoms[0][..., None, :]
    delta_b = own_atoms[1][..., :, None] - far_atoms[1][..., None, :]
    delta_c = own_atoms[2][..., :, None] - far_atoms[2][..., None, :]
    distance_sq = delta_a * delta_a + delta_b * delta_b + delta_c * delta_c
    radius = jnp.sqrt(distance_sq + 1e-06)
    pair_width = jnp.sqrt(own_atoms[3][..., :, None] ** 2 + far_atoms[3][..., None, :] ** 2)
    smooth_cut = (1.0 - jnp.minimum(distance_sq, 1.0)) ** 3
    kernel = 0.005 * smooth_cut * jax.scipy.special.erf(radius / pair_width) / radius
    kernel = kernel * own_atoms[4][..., :, None] * far_atoms[4][..., None, :]
    if self_cell:
        kernel = kernel * (1.0 - jnp.eye(kernel.shape[-1], dtype=jnp.float32))
    return kernel


def committee(flat_rows, w_in, b_in, w_hid, b_hid, w_out):

    def member_fn(weights):
        first_w, first_b, second_w, second_b, last_w = weights
        first = jnp.tanh(
            jnp.dot(flat_rows, first_w, preferred_element_type=jnp.float32) + first_b
        ).astype(jnp.bfloat16)
        second = jnp.tanh(
            jnp.dot(first, second_w, preferred_element_type=jnp.float32) + second_b
        ).astype(jnp.bfloat16)
        return jnp.dot(second, last_w.T, preferred_element_type=jnp.float32).T

    return lax.map(member_fn, (w_in, b_in, w_hid, b_hid, w_out))


def expand(values):
    return values[:, None, None, None]


def extend(vectors):
    return extended_2(vectors, (("cell", 1), ("sub", 2)), 1)


def two_products(residual, image_vec):
    return lax.psum(
        (
            jnp.sum(residual * residual, axis=(1, 2, 3)),
            jnp.sum(residual * image_vec, axis=(1, 2, 3)),
        ),
        ("cell", "sub"),
    )


def body(descriptors, positions, species, counts, w_in, b_in, w_hid, b_hid, w_out):
    rows_a, rows_b, slot_count, features = descriptors.shape
    members = w_in.shape[0]
    slot_iota = lax.broadcasted_iota(jnp.int32, (rows_a, rows_b, slot_count), 2)
    occupancy = (slot_iota < counts[:, :, None]).astype(jnp.float32)
    widths = lookup(species, (0.3, 0.4, 0.5, 0.35))
    shifts = lookup(species, (-0.8, 0.4, 1.2, -0.3))
    atom_data = jnp.stack([positions[0], positions[1], positions[2], widths, occupancy])
    extended = extended_2(atom_data, (("cell", 1), ("sub", 2)), 1)
    outputs = committee(descriptors.reshape(-1, features), w_in, b_in, w_hid, b_hid, w_out)
    electro = outputs[:, 0].reshape(members, rows_a, rows_b, slot_count) + shifts
    hardness = 2.5 + jax.nn.softplus(outputs[:, 1]).reshape(members, rows_a, rows_b, slot_count)
    right_side = jnp.concatenate([-electro * occupancy, jnp.broadcast_to(occupancy, electro.shape)])
    diagonal = jnp.concatenate([hardness, hardness])
    offsets = [(row_step, col_step) for row_step in (-1, 0, 1) for col_step in (-1, 0, 1)]

    def neighbours(grown, row_step, col_step):
        return grown[:, 1 + row_step : 1 + row_step + rows_a, 1 + col_step : 1 + col_step + rows_b]

    def block_for(row_step, col_step):
        return coupling(
            atom_data, neighbours(extended, row_step, col_step), row_step == 0 and col_step == 0
        )

    def operate(vectors):
        grown = extend(vectors)
        summed = diagonal * vectors
        for offset_number in range(9):
            row_step, col_step = offsets[offset_number]
            tile_block = block_for(row_step, col_step)
            summed = summed + jnp.einsum(
                "abij,rabj->rabi",
                tile_block,
                neighbours(grown, row_step, col_step),
                precision=lax.Precision.HIGHEST,
            )
        return summed

    solution = jnp.zeros_like(right_side)
    residual = right_side
    image_vec = operate(residual)
    norm_now, product = two_products(residual, image_vec)
    step_size = norm_now / product
    direction = residual
    along = image_vec
    for iteration in range(ITERS):
        solution = solution + expand(step_size) * direction
        residual = residual - expand(step_size) * along
        if iteration + 1 < ITERS:
            image_vec = operate(residual)
            norm_next, product = two_products(residual, image_vec)
            momentum = norm_next / norm_now
            step_size = norm_next / (product - momentum * norm_next / step_size)
            direction = residual + expand(momentum) * direction
            along = image_vec + expand(momentum) * along
            norm_now = norm_next
    source_part = solution[:members]
    unit_part = solution[members:]
    source_total, unit_total = lax.psum(
        (jnp.sum(source_part, axis=(1, 2, 3)), jnp.sum(unit_part, axis=(1, 2, 3))), ("cell", "sub")
    )
    multiplier = source_total / unit_total
    return source_part - expand(multiplier) * unit_part


def solution(mesh):
    placed = (
        P(("rep", "cell"), "sub", None, None),
        P(None, ("rep", "cell"), "sub", None),
        P(("rep", "cell"), "sub", None),
        P(("rep", "cell"), "sub"),
        P(),
        P(),
        P(),
        P(),
        P(),
    )
    rows, columns = mesh.shape["cell"], mesh.shape["sub"]
    return jax.shard_map(
        gathered if columns % SIDES == 0 and sum(pair_counts(rows, columns)) <= MOST_BLOCKS else body,
        mesh=mesh,
        in_specs=placed,
        out_specs=P(None, ("rep", "cell"), "sub", None),
        check_vma=False,
    )
```

```python
import functools

import jax
import jax.numpy as jnp
from jax import lax
from jax.experimental import pallas as pl
from jax.experimental.pallas import tpu as pltpu
from jax.sharding import PartitionSpec as P

ITERS = 2

ERF_SERIES = (
    1.1283791338788207,
    -0.37612471240078243,
    0.11282450088960652,
    -0.026825992168818515,
    0.005164800720113156,
    -0.0008061635856414364,
    9.67168369375208e-05,
    -7.756955478859171e-06,
    3.007955257374649e-07,
)

WIDTHS = (0.3, 0.4, 0.5, 0.35)

HARD, PLACE, KIND, FULL, ROWS = 8, 16, 19, 20, 24
SQUARE, FEATURES = 24, 48
OFFSETS = ((0, 0), (0, 1), (1, -1), (1, 0), (1, 1))
MOST_BLOCKS = 128
LAG = 8
AHEAD = 2
CHUNK = 16
GROUP = 8
SIDES = 2
HELD = 24


def pair_counts(rows, cols):
    return [(rows - da) * (cols - abs(db)) for da, db in OFFSETS]


def choose(species, entries):
    value = jnp.full(species.shape, entries[3], jnp.float32)
    for kind in (2, 1, 0):
        value = jnp.where(species == kind, entries[kind], value)
    return value


def slab_kernel(*refs):
    sources, out_ref, landed, done = refs[:9], refs[9], refs[10:19], refs[19]
    members = sources[4].shape[0]
    copies = []

    def fetch(source, target):
        copy = pltpu.make_async_copy(source, target, done.at[len(copies)])
        copy.start()
        copies.append(copy)
        return copy

    desc_ref, pos_ref, species_ref, counts_ref, w_in, b_in, w_hid, b_hid, w_out = landed
    early = [fetch(sources[k], landed[k]) for k in (0, 5, 4)]
    middle = [fetch(sources[k], landed[k]) for k in (6, 7, 8)]
    late = [fetch(sources[k], landed[k]) for k in (1, 2, 3)]
    for copy in early:
        copy.wait()
    rows = desc_ref[...]
    slots = rows.shape[0]
    firsts, electro, raw = [], [], []
    for m in range(members):
        summed = jnp.dot(rows, w_in[m], preferred_element_type=jnp.float32) + b_in[m : m + 1, :]
        firsts.append(jnp.tanh(summed).astype(jnp.bfloat16))
    for copy in middle:
        copy.wait()
    for start in range(0, members, GROUP):
        group = range(start, start + GROUP)
        seconds = []
        for m in group:
            summed = jnp.dot(firsts[m], w_hid[m], preferred_element_type=jnp.float32)
            seconds.append(jnp.tanh(summed + b_hid[m : m + 1, :]).astype(jnp.bfloat16))
        for m in group:
            outputs = lax.dot_general(
                w_out[m],
                seconds[m - start],
                (((1,), (1,)), ((), ())),
                preferred_element_type=jnp.float32,
            )
            electro.append(outputs[0:1])
            raw.append(outputs[1:2])
    for copy in late:
        copy.wait()
    species = species_ref[0]
    slot_iota = lax.broadcasted_iota(jnp.int32, (1, slots), 1)
    occupancy = (slot_iota < counts_ref[0, 0]).astype(jnp.float32)
    shifts = choose(species, (-0.8, 0.4, 1.2, -0.3))
    raw = jnp.concatenate(raw, axis=0)
    hardness = 2.5 + (jnp.maximum(raw, 0.0) + jnp.log1p(jnp.exp(-jnp.abs(raw))))
    right = -(jnp.concatenate(electro, axis=0) + shifts) * occupancy
    atoms = jnp.concatenate(
        [pos_ref[0, 0], pos_ref[1, 0], pos_ref[2, 0], species.astype(jnp.float32), occupancy]
        + [jnp.zeros((1, slots), jnp.float32)] * (ROWS - FULL - 1),
        axis=0,
    )
    for peer in range(out_ref.shape[0]):
        out_ref[peer, 0:HARD, :] = right
        out_ref[peer, HARD:PLACE, :] = hardness
        out_ref[peer, PLACE:ROWS, :] = atoms


def thirds(values):
    high = values.astype(jnp.bfloat16).astype(jnp.float32)
    rest = values - high
    middle = rest.astype(jnp.bfloat16).astype(jnp.float32)
    return high, middle, rest - middle


def pair_features(places, kind):
    one, zero = jnp.ones_like(kind), jnp.zeros_like(kind)
    near, far = [], []
    for place in places:
        h, m, l = thirds(place)
        near += [h, h, m, m, h, l]
        far += [2.0 * v for v in (h, m, h, m, l, h)]
    norm = sum(place * place for place in places)
    near += [*thirds(norm), one, one, one]
    far += [-one, -one, -one, *thirds(1.0 - norm)]
    count = len(WIDTHS)
    near += [(kind == k).astype(jnp.float32) for k in range(count)] * 3
    pairs = [
        choose(kind, [(WIDTHS[k] ** 2 + other**2) ** -0.5 for other in WIDTHS])
        for k in range(count)
    ]
    far += [part for third in zip(*map(thirds, pairs)) for part in third]
    rest = [zero] * (FEATURES - len(near))
    return near + rest, far + rest


def pair_block(products, first_row, own):
    slots = products.shape[1] // 2
    left = jnp.maximum(products[:, 0:slots], 0.0)
    inv = products[:, slots:]
    y = (1.000001 - left) * (inv * inv)
    value = jnp.full_like(y, 0.005 * ERF_SERIES[-1])
    for term in ERF_SERIES[-2::-1]:
        value = value * y + 0.005 * term
    value = value * ((left * inv) * (left * left))
    if own:
        i = lax.broadcasted_iota(jnp.int32, value.shape, 0)
        j = lax.broadcasted_iota(jnp.int32, value.shape, 1)
        value = jnp.where(j - i == first_row, 0.0, value)
    return value


def times(vectors, block):
    return jnp.dot(vectors, block, preferred_element_type=jnp.float32)


def times_t(vectors, block):
    return lax.dot_general(
        vectors, block, (((1,), (1,)), ((), ())), preferred_element_type=jnp.float32
    )


def halves(values):
    high = values.astype(jnp.bfloat16)
    return high, (values - high.astype(jnp.float32)).astype(jnp.bfloat16)


def grid_pairs(rows, columns):
    pairs = []
    for a in range(rows):
        for da, db in OFFSETS:
            for column in range(max(0, -db), columns - max(0, db)):
                c = a * columns + column
                if a + da < rows:
                    pairs.append((c, c + da * columns + db))
    return pairs


def colour(c, columns):
    return (c // columns + c % columns) % SIDES


def split_pairs(rows, columns):
    every = grid_pairs(rows, columns)
    early = [pair for pair in every if not any(colour(c, columns) for c in pair)]
    return early, [pair for pair in every if pair not in early]


def items(ref):
    return [ref.at[k] for k in range(ref.shape[0])]


def views(columns, *sides):
    cells = SIDES * sides[0].shape[0]
    return [sides[colour(c, columns)].at[c // SIDES] for c in range(cells)]


def my_side():
    return lax.rem(lax.axis_index("cell") + lax.axis_index("sub"), SIDES)


def prepare(grid, source, slab, feats, near, far, vecs, sums):
    rows, columns = grid
    half, slots = columns // SIDES, slab.shape[2]
    side = my_side()
    for k in range(slab.shape[0]):
        h = k % half
        slab[k] = source[k + side * (half - 1 - 2 * h)]
    centres = (rows / 2, columns / 2, 0.5)
    rows_of = pair_features(
        [slab[:, PLACE + k, :] - centres[k] for k in range(3)], slab[:, KIND, :]
    )
    for k, row in enumerate(rows_of[0] + rows_of[1]):
        feats[:, k, :] = row
    blank = jnp.zeros((SQUARE, slots), jnp.float32)
    for c in range(slab.shape[0]):
        near[c] = feats[c, 0:FEATURES, :].T.astype(jnp.bfloat16)
        apart = jnp.concatenate([feats[c, FEATURES : FEATURES + SQUARE, :], blank], axis=0)
        spread = jnp.concatenate([blank, feats[c, FEATURES + SQUARE :, :]], axis=0)
        far[c] = jnp.concatenate([apart, spread], axis=1).astype(jnp.bfloat16)
        high, low = halves(slab[c, 0:HARD, :])
        full = slab[c, FULL : FULL + 1, :]
        row = lax.broadcasted_iota(jnp.int32, (16, slots), 0)
        lines = [high.astype(jnp.float32), low.astype(jnp.float32), jnp.where(row == 0, full, 0.0)]
        lines = jnp.concatenate(lines, axis=0).astype(jnp.bfloat16)
        vecs[c] = jnp.concatenate([lines, lines], axis=1)
        sums[c] = jnp.zeros_like(sums[c])


def build_and_apply(pairs, blocks, near, far, vecs, sums, products):
    slots = near[0].shape[0]
    lag = min(LAG, len(pairs) // 2)
    for i in range(len(pairs) + AHEAD + lag):
        if i < len(pairs):
            c, d = pairs[i]
            products[i % (AHEAD + 1)] = times(near[c][...], far[d][...])
        k = i - AHEAD - lag
        if k >= 0:
            c, d = pairs[k]
            block = blocks[k]
            image = times(vecs[c][...], block)
            if c != d:
                wide = jnp.concatenate([block[0:slots], block[slots:]], axis=1)
                sums[c][...] += times_t(vecs[d][...], wide)[0:HELD]
            sums[d][...] += image[0:HELD]
        k = i - AHEAD
        if 0 <= k < len(pairs):
            c, d = pairs[k]
            for row in range(0, slots, CHUNK):
                part = products[k % (AHEAD + 1), row : row + CHUNK, :]
                high, low = halves(pair_block(part, row, c == d))
                blocks[k, row : row + CHUNK, :] = high
                blocks[k, slots + row : slots + row + CHUNK, :] = low


def early_kernel(grid, mine, slab, near, far, vecs, sums, blocks, feats, products):
    prepare(grid, mine, slab, feats, near, far, vecs, sums)
    pairs = [(c // SIDES, d // SIDES) for c, d in split_pairs(*grid)[0]]
    build_and_apply(pairs, blocks, *map(items, (near, far, vecs, sums)), products)


def late_kernel(
    grid, mine_slab, mine_near, mine_far, mine_vecs, mine_sums, mine_blocks, theirs, out_ref,
    slab, near, far, vecs, sums, sums_kept, resid, resid_half, blocks, feats, products
):
    rows, columns = grid
    cells, members, slots = rows * columns, HARD, slab.shape[2]
    prepare(grid, theirs, slab, feats, near, far, vecs, sums)
    sums_kept[...] = mine_sums[...]
    slab_of, sums_of = views(columns, mine_slab, slab), views(columns, sums_kept, sums)
    early, late = split_pairs(rows, columns)
    held = ((mine_near, near), (mine_far, far), (mine_vecs, vecs))
    sides = [views(columns, *pair) for pair in held]
    build_and_apply(late, blocks, *sides, sums_of, products)

    def applied(c):
        hard = slab_of[c][HARD:PLACE, :]
        full = slab_of[c][FULL : FULL + 1, :]
        right = slab_of[c][0:HARD, :]
        coupled = sums_of[c][...]
        image_s = hard * right + full * (coupled[0:8] + coupled[8:16])
        image_u = full * (hard + coupled[16:17])
        return hard, full, right, image_s, image_u

    shape = (members, slots)
    norm_s, prod_s, prod_u, total_s = (jnp.zeros(shape, jnp.float32) for _ in range(4))
    norm_u = jnp.zeros((1, slots), jnp.float32)
    for c in range(cells):
        hard, full, right, image_s, image_u = applied(c)
        resid[c] = jnp.concatenate([image_s, image_u], axis=0)
        norm_s += right * right
        norm_u += full * full
        prod_s += right * image_s
        prod_u += full * image_u
        total_s += right

    def over(values):
        return jnp.sum(values, axis=1, keepdims=True)

    both = lambda s, u: jnp.concatenate([s, jnp.broadcast_to(u, s.shape)], axis=0)
    norm0 = both(over(norm_s), over(norm_u))
    total0 = both(over(total_s), over(norm_u))
    alpha0 = norm0 / both(over(prod_s), over(prod_u))

    norm1, prod1, total1 = (jnp.zeros((2 * members, slots), jnp.float32) for _ in range(3))
    for c in range(cells):
        hard = slab_of[c][HARD:PLACE, :]
        right, full = slab_of[c][0:HARD, :], slab_of[c][FULL : FULL + 1, :]
        left = both(right, full) - alpha0 * resid[c]
        resid[c] = left
        high, low = halves(left)
        lines = jnp.concatenate([high, low], axis=0)
        resid_half[c] = jnp.concatenate([lines, lines], axis=1)
        square = left * left
        norm1 += square
        prod1 += jnp.concatenate([hard, hard], axis=0) * square
        total1 += left

    stored = dict(zip(early + late, items(mine_blocks) + items(blocks)))
    for c in range(cells):
        others = [d for b, d in stored if b == c]
        for first in range(0, len(others), 2):
            some = others[first : first + 2]
            image = times(resid_half[c], jnp.concatenate([stored[c, d][...] for d in some], axis=1))
            for k, d in enumerate(some):
                part = image[:, k * slots : (k + 1) * slots]
                part = (part[0:16] + part[16:32]) * resid[d]
                prod1 = prod1 + (part if c == d else 2.0 * part)

    norm1, prod1, total1 = over(norm1), over(prod1), over(total1)
    momentum = norm1 / norm0
    alpha1 = norm1 / (prod1 - momentum * norm1 / alpha0)
    weight0 = alpha0 + alpha1 * momentum
    totals = weight0 * total0 + alpha1 * total1
    multiplier = totals[0:members] / totals[members:]
    half, row, side = columns // SIDES, lax.axis_index("cell"), my_side()
    h = lax.div(lax.axis_index("sub"), SIDES)
    h = h + side * (half - 1 - 2 * h)
    own, cell = row * half + h, row * columns + SIDES * h + lax.rem(row, SIDES)
    right = both(mine_slab[own, 0:HARD, :], mine_slab[own, FULL : FULL + 1, :])
    answer = weight0 * right + alpha1 * resid[cell]
    out_ref[...] = answer[0:members] - multiplier * answer[members:]


def solve_only(mine, theirs):
    grid = rows, columns = lax.axis_size("cell"), lax.axis_size("sub")
    cells, slots = rows * columns, mine.shape[2]
    side = cells // SIDES
    early, late = map(len, split_pairs(rows, columns))
    vmem = pl.BlockSpec(memory_space=pltpu.VMEM)
    limit = pltpu.CompilerParams(vmem_limit_bytes=32 << 20)
    kept = [
        pltpu.VMEM((side, ROWS, slots), jnp.float32),
        pltpu.VMEM((side, slots, FEATURES), jnp.bfloat16),
        pltpu.VMEM((side, FEATURES, 2 * slots), jnp.bfloat16),
        pltpu.VMEM((side, 32, 2 * slots), jnp.bfloat16),
        pltpu.VMEM((side, HELD, slots), jnp.float32),
    ]
    work = [
        pltpu.VMEM((side, 2 * FEATURES, slots), jnp.float32),
        pltpu.VMEM((AHEAD + 1, slots, 2 * slots), jnp.float32),
    ]
    begun = pl.pallas_call(
        functools.partial(early_kernel, grid),
        out_shape=[*kept, pltpu.VMEM((early, 2 * slots, slots), jnp.bfloat16)],
        in_specs=[vmem],
        out_specs=[vmem] * (len(kept) + 1),
        scratch_shapes=work,
        compiler_params=limit,
        cost_estimate=pl.CostEstimate(flops=10**9, bytes_accessed=4 * 10**6, transcendentals=0),
        name="early",
    )(mine)
    return pl.pallas_call(
        functools.partial(late_kernel, grid),
        out_shape=jax.ShapeDtypeStruct((HARD, slots), jnp.float32),
        in_specs=[vmem] * (len(begun) + 1),
        out_specs=vmem,
        scratch_shapes=[
            *kept,
            pltpu.VMEM((side, HELD, slots), jnp.float32),
            pltpu.VMEM((cells, 16, slots), jnp.float32),
            pltpu.VMEM((cells, 32, 2 * slots), jnp.bfloat16),
            pltpu.VMEM((late, 2 * slots, slots), jnp.bfloat16),
            *work,
        ],
        compiler_params=limit,
        name="late",
    )(*begun, theirs)


def gathered(descriptors, positions, species, counts, w_in, b_in, w_hid, b_hid, w_out):
    rows, columns = lax.axis_size("cell"), lax.axis_size("sub")
    cells, slots, members = rows * columns, descriptors.shape[2], w_in.shape[0]
    vmem = pl.BlockSpec(memory_space=pltpu.VMEM)
    args = (
        descriptors.reshape(slots, -1), positions, species, counts, w_in, b_in, w_hid, b_hid, w_out
    )
    landed = [
        (pltpu.SMEM if arg is counts else pltpu.VMEM)(arg.shape, arg.dtype) for arg in args
    ]
    slabs = pl.pallas_call(
        slab_kernel,
        out_shape=pltpu.VMEM((cells // SIDES, ROWS, slots), jnp.float32),
        in_specs=[pl.BlockSpec(memory_space=pltpu.HBM)] * len(args),
        out_specs=vmem,
        scratch_shapes=landed + [pltpu.SemaphoreType.DMA((len(args),))],
        compiler_params=pltpu.CompilerParams(vmem_limit_bytes=60 << 20),
        name="slab",
    )(*args)
    groups = [
        [c for c in range(cells) if colour(c, columns) == side] for side in range(SIDES)
    ]
    mine = lax.all_to_all(
        slabs, ("cell", "sub"), 0, 0, tiled=True, axis_index_groups=groups
    )
    theirs = lax.ppermute(mine, "sub", [(column, column ^ 1) for column in range(columns)])
    charges = solve_only(mine, theirs)
    return charges.reshape(members, 1, 1, slots)


def extended_2(shard, sides, width):
    for axis, dim in sides:
        size, length = (lax.axis_size(axis), shard.shape[dim])
        up = [(i, (i + 1) % size) for i in range(size - 1)]
        down = [(j, i) for i, j in up]
        last = lax.slice_in_dim(shard, length - width, length, axis=dim)
        leading = lax.slice_in_dim(shard, 0, width, axis=dim)
        before = lax.ppermute(last, axis, up)
        after = lax.ppermute(leading, axis, down)
        shard = jnp.concatenate([before, shard, after], axis=dim)
    return shard


def lookup(species, entries):
    choices_table = jnp.array(entries, jnp.float32)
    kinds = jnp.arange(4, dtype=jnp.int32)
    return jnp.sum((species[..., None] == kinds).astype(jnp.float32) * choices_table, axis=-1)


def coupling(own_atoms, far_atoms, self_cell):
    delta_a = own_atoms[0][..., :, None] - far_atoms[0][..., None, :]
    delta_b = own_atoms[1][..., :, None] - far_atoms[1][..., None, :]
    delta_c = own_atoms[2][..., :, None] - far_atoms[2][..., None, :]
    distance_sq = delta_a * delta_a + delta_b * delta_b + delta_c * delta_c
    radius = jnp.sqrt(distance_sq + 1e-06)
    pair_width = jnp.sqrt(own_atoms[3][..., :, None] ** 2 + far_atoms[3][..., None, :] ** 2)
    smooth_cut = (1.0 - jnp.minimum(distance_sq, 1.0)) ** 3
    kernel = 0.005 * smooth_cut * jax.scipy.special.erf(radius / pair_width) / radius
    kernel = kernel * own_atoms[4][..., :, None] * far_atoms[4][..., None, :]
    if self_cell:
        kernel = kernel * (1.0 - jnp.eye(kernel.shape[-1], dtype=jnp.float32))
    return kernel


def committee(flat_rows, w_in, b_in, w_hid, b_hid, w_out):

    def member_fn(weights):
        first_w, first_b, second_w, second_b, last_w = weights
        first = jnp.tanh(
            jnp.dot(flat_rows, first_w, preferred_element_type=jnp.float32) + first_b
        ).astype(jnp.bfloat16)
        second = jnp.tanh(
            jnp.dot(first, second_w, preferred_element_type=jnp.float32) + second_b
        ).astype(jnp.bfloat16)
        return jnp.dot(second, last_w.T, preferred_element_type=jnp.float32).T

    return lax.map(member_fn, (w_in, b_in, w_hid, b_hid, w_out))


def expand(values):
    return values[:, None, None, None]


def extend(vectors):
    return extended_2(vectors, (("cell", 1), ("sub", 2)), 1)


def two_products(residual, image_vec):
    return lax.psum(
        (
            jnp.sum(residual * residual, axis=(1, 2, 3)),
            jnp.sum(residual * image_vec, axis=(1, 2, 3)),
        ),
        ("cell", "sub"),
    )


def body(descriptors, positions, species, counts, w_in, b_in, w_hid, b_hid, w_out):
    rows_a, rows_b, slot_count, features = descriptors.shape
    members = w_in.shape[0]
    slot_iota = lax.broadcasted_iota(jnp.int32, (rows_a, rows_b, slot_count), 2)
    occupancy = (slot_iota < counts[:, :, None]).astype(jnp.float32)
    widths = lookup(species, (0.3, 0.4, 0.5, 0.35))
    shifts = lookup(species, (-0.8, 0.4, 1.2, -0.3))
    atom_data = jnp.stack([positions[0], positions[1], positions[2], widths, occupancy])
    extended = extended_2(atom_data, (("cell", 1), ("sub", 2)), 1)
    outputs = committee(descriptors.reshape(-1, features), w_in, b_in, w_hid, b_hid, w_out)
    electro = outputs[:, 0].reshape(members, rows_a, rows_b, slot_count) + shifts
    hardness = 2.5 + jax.nn.softplus(outputs[:, 1]).reshape(members, rows_a, rows_b, slot_count)
    right_side = jnp.concatenate([-electro * occupancy, jnp.broadcast_to(occupancy, electro.shape)])
    diagonal = jnp.concatenate([hardness, hardness])
    offsets = [(row_step, col_step) for row_step in (-1, 0, 1) for col_step in (-1, 0, 1)]

    def neighbours(grown, row_step, col_step):
        return grown[:, 1 + row_step : 1 + row_step + rows_a, 1 + col_step : 1 + col_step + rows_b]

    def block_for(row_step, col_step):
        return coupling(
            atom_data, neighbours(extended, row_step, col_step), row_step == 0 and col_step == 0
        )

    def operate(vectors):
        grown = extend(vectors)
        summed = diagonal * vectors
        for offset_number in range(9):
            row_step, col_step = offsets[offset_number]
            tile_block = block_for(row_step, col_step)
            summed = summed + jnp.einsum(
                "abij,rabj->rabi",
                tile_block,
                neighbours(grown, row_step, col_step),
                precision=lax.Precision.HIGHEST,
            )
        return summed

    solution = jnp.zeros_like(right_side)
    residual = right_side
    image_vec = operate(residual)
    norm_now, product = two_products(residual, image_vec)
    step_size = norm_now / product
    direction = residual
    along = image_vec
    for iteration in range(ITERS):
        solution = solution + expand(step_size) * direction
        residual = residual - expand(step_size) * along
        if iteration + 1 < ITERS:
            image_vec = operate(residual)
            norm_next, product = two_products(residual, image_vec)
            momentum = norm_next / norm_now
            step_size = norm_next / (product - momentum * norm_next / step_size)
            direction = residual + expand(momentum) * direction
            along = image_vec + expand(momentum) * along
            norm_now = norm_next
    source_part = solution[:members]
    unit_part = solution[members:]
    source_total, unit_total = lax.psum(
        (jnp.sum(source_part, axis=(1, 2, 3)), jnp.sum(unit_part, axis=(1, 2, 3))), ("cell", "sub")
    )
    multiplier = source_total / unit_total
    return source_part - expand(multiplier) * unit_part


def solution(mesh):
    placed = (
        P(("rep", "cell"), "sub", None, None),
        P(None, ("rep", "cell"), "sub", None),
        P(("rep", "cell"), "sub", None),
        P(("rep", "cell"), "sub"),
        P(),
        P(),
        P(),
        P(),
        P(),
    )
    rows, columns = mesh.shape["cell"], mesh.shape["sub"]
    return jax.shard_map(
        gathered if columns % SIDES == 0 and sum(pair_counts(rows, columns)) <= MOST_BLOCKS else body,
        mesh=mesh,
        in_specs=placed,
        out_specs=P(None, ("rep", "cell"), "sub", None),
        check_vma=False,
    )
```
